128 devices in a mesh: blk: 32 (over y_hi, x, z), head: 4 (over y_lo, core).
Axes of the slice: x: 4, y: 4 (y_hi: 2, y_lo: 2; y = y_hi * 2 + y_lo), z: 4, core: 2. Of those that a mesh axis runs over, the one named last changes fastest.
Arguments:
- states_in: bfloat16 [8192, 2048], P('blk'), may hold values from -12 to 12
- w_qkv: bfloat16 [3, 2048, 2048], P(None, None, 'head'), may hold values from -0.35355339 to 0.35355339
- qk_gain: float32 [2, 2048], P(None, 'head'), may hold values from 0.8 to 7.8
- w_out: bfloat16 [2048, 2048], P('head'), may hold values from -0.125 to 0.125
- post_gain: float32 [2, 2048], replicated, may hold values from 0.5 to 1.5
- w_gate_up: bfloat16 [2, 2048, 8192], P(None, None, 'blk'), may hold values from -0.125 to 0.125
- w_down: bfloat16 [8192, 2048], P('blk'), may hold values from -0.0625 to 0.0625
- cache_keys: bfloat16 [32, 256, 2048], P('blk', None, 'head'), may hold values from -6 to 6
- cache_values: bfloat16 [32, 256, 2048], P('blk', None, 'head'), may hold values from -6 to 6
- slot_node: int32 [32], replicated, may hold values from 0 to 31, each once
- node_length: int32 [32], replicated, may hold values from 1 to 256, 5120 in all
- node_parent: int32 [28], replicated, may hold values from 0 to 3
- leaf_segment: int32 [32, 256], replicated, may hold values from 0 to 7, never falling along the last dimension, each value on 1 to 128 neighbouring positions
- leaf_node: int32 [32, 8], replicated, may hold values from 4 to 31
Outputs:
- layer_out: bfloat16 [8192, 2048], P(('blk', 'head'))
The draws below stay inside these ranges and needn't reach their ends.
Inputs may be any that keep to these rules, and one draw needn't show every extreme that they name: Slot s holds node slot_node[s]; every node is held once. Rows 0 to node_length[n] - 1 of node n's slot are valid; the longest node has 256 rows. Nodes 0 to 3 are roots; middle node 4 + i hangs under root node_parent[i]. `leaf_segment`: never falls along a group; every leaf of a group has 1 to 128 tokens. `leaf_node`: every leaf hangs under a middle node.
All inputs are finite; a program needn't handle non-finite values.
Results may differ from the reference program's by a relative error of at most 0.025.
Values may be sent and summed in bfloat16 or wider, within the bound.
No kernel may reach another device: no remote copies, remote signals or barrier semaphores. Data moves between devices by JAX's collectives and lax.ppermute only.
A program may use at most 192 MiB of HBM per device.

```python
import math
import jax
import jax.numpy as jnp
import numpy as np
from jax import lax

D = 2048
HEADS = 16
HD = 128
FF = 8192
TENANTS = 4
TOK_DEV = 256
NODE_LEN = 256
LEAVES_DEV = 8
GROUPS = 32
NODES = 32
MIDDLES = 28
TOKENS = 8192


def draw_states_in(key, part):
    key_base = jax.random.fold_in(key, 0)
    base = jax.random.truncated_normal(key_base, -6.0, 6.0, (TOKENS, D), jnp.float32)
    return base.astype(jnp.bfloat16)


def draw_w_qkv(key, part):
    key_base, key_jitter = jax.random.split(key)
    columns = HEADS * HD
    base = jax.random.truncated_normal(key_base, -6.0, 6.0, (3, D, columns), jnp.float32) / math.sqrt(D)
    column_at = jnp.arange(columns, dtype=jnp.float32) / (columns - 1)
    jitter = jnp.exp(jax.random.uniform(key_jitter, (2, 1, columns), jnp.float32, -0.35, 0.35))
    shaped = base[0:2] * (0.6 * 3.0 ** column_at) * jitter
    return jnp.concatenate([shaped, base[2:3]], axis=0).astype(jnp.bfloat16)


def draw_qk_gain(key, part):
    key_main = jax.random.fold_in(key, 0)
    columns = HEADS * HD
    return jax.random.uniform(key_main, (2, columns), jnp.float32, 0.8, 1.25)


def set_ends(drawn, own_key, low, top_value):
    spot = [jax.random.randint(jax.random.fold_in(own_key, axis), (), 0, length) for axis, length in enumerate(drawn.shape)]
    widest = drawn.shape.index(max(drawn.shape))
    beside = spot[:widest] + [(spot[widest] + 1) % drawn.shape[widest]] + spot[widest + 1:]
    return drawn.at[tuple(spot)].set(low).at[tuple(beside)].set(top_value)


def levels(own_key, shape, cuts, least, top_value):
    def one(dim, blocks):
        steps = jax.random.uniform(jax.random.fold_in(jax.random.fold_in(own_key, 6), dim), (blocks,), jnp.float32, least / len(cuts), top_value / len(cuts))
        return jnp.repeat(jnp.exp(steps), shape[dim] // blocks).reshape((-1,) + (1,) * (len(shape) - dim - 1))

    factor_of = one(*cuts[0])
    for cut in cuts[1:]:
        factor_of = factor_of * one(*cut)
    return factor_of


def length_profile(number_of, total, limit, skew):
    portions = [(1 << 20) // math.isqrt(standing ** skew) + 1 for standing in range(2, number_of + 1)]
    surplus, given = total - limit - (number_of - 1), [1] * (number_of - 1)
    while surplus > 0:
        free = [i for i in range(number_of - 1) if given[i] < limit]
        mass, remaining = sum([portions[i] for i in free]), surplus
        for i in free:
            extra = min(limit - given[i], max(1, remaining * portions[i] // mass), surplus)
            given[i] = given[i] + extra
            surplus = surplus - extra
    return np.array([limit] + given)


def uneven_parts(stream_key, amount, total, limit, skew):
    if amount == 2:
        one = jax.random.randint(stream_key, (), max(1, total - limit), min(limit, total - 1) + 1)
        return jnp.stack([one, total - one])
    sizes = jnp.asarray(length_profile(amount, total, limit, skew), jnp.int32)
    pairs = (amount - 1) // 2
    giver, sink = sizes[1:1 + 2 * pairs:2], sizes[2:2 + 2 * pairs:2]
    room = jnp.minimum(giver - 1, limit - sink)
    shifted = jax.random.randint(jax.random.fold_in(stream_key, 1), (pairs,), 0, 1 << 20) % (room + 1)
    sizes = sizes.at[1:1 + 2 * pairs:2].set(giver - shifted).at[2:2 + 2 * pairs:2].set(sink + shifted)
    return sizes[jax.random.permutation(jax.random.fold_in(stream_key, 2), amount)]


def centred(own_key, extent, width, bound, cuts=(), kind=jnp.bfloat16):
    result = jax.random.normal(own_key, extent, jnp.float32) * width
    if len(cuts) > 0:
        result = levels(own_key, extent, cuts, -0.22, 0.18) * result
    return jnp.clip(result, min=-bound, max=bound).astype(kind)


def setup_inputs(seed: int = 0) -> dict:
    key_list = jax.random.split(jax.random.key(seed), 15)
    return {
        "states_in": draw_states_in(jax.random.fold_in(key_list[14], 71), 0),
        "w_qkv": draw_w_qkv(jax.random.fold_in(key_list[14], 71), 0),
        "qk_gain": draw_qk_gain(jax.random.fold_in(key_list[14], 71), 0),
        "w_out": centred(key_list[3], (HEADS * HD, D), (HEADS * HD) ** -0.5, 0.125, ((0, 4),)),
        "post_gain": jnp.clip(1.0 + 0.1 * jax.random.normal(key_list[4], (2, D), jnp.float32), 0.5, 1.5),
        "w_gate_up": centred(key_list[5], (2, D, FF), D ** -0.5, 0.125, ((2, 32),)),
        "w_down": centred(key_list[6], (FF, D), FF ** -0.5, 0.0625, ((0, 32),)),
        "cache_keys": centred(key_list[7], (NODES, NODE_LEN, HEADS * HD), 1.0, 6.0, ((0, 32), (2, 4))),
        "cache_values": centred(key_list[8], (NODES, NODE_LEN, HEADS * HD), 1.0, 6.0, ((0, 32), (2, 4))),
        "slot_node": jax.random.permutation(key_list[9], NODES).astype(jnp.int32),
        "node_length": uneven_parts(key_list[10], NODES, NODES * NODE_LEN * 5 // 8, NODE_LEN, 1).astype(jnp.int32),
        "node_parent": set_ends(jax.random.randint(key_list[11], (MIDDLES,), 0, TENANTS), jax.random.fold_in(key_list[11], 1), 0, TENANTS - 1).astype(jnp.int32),
        "leaf_segment": jax.vmap(lambda own: jnp.searchsorted(jnp.cumsum(uneven_parts(own, LEAVES_DEV, TOK_DEV, TOK_DEV // 2, 1)), jnp.arange(TOK_DEV), side="right"))(jax.random.split(key_list[12], GROUPS)).reshape((GROUPS, TOK_DEV)).astype(jnp.int32),
        "leaf_node": set_ends(jax.random.randint(key_list[13], (GROUPS, LEAVES_DEV), TENANTS, NODES), jax.random.fold_in(key_list[13], 1), TENANTS, NODES - 1).astype(jnp.int32),
    }


EPS = 1e-06
THETA = 500000.0
NEG = -1e+30

def tree_info(leaf_segment, leaf_node, node_parent, node_length):
    groups, tok_rows = leaf_segment.shape
    leaf_count = leaf_node.shape[1]
    middles = node_parent.shape[0]
    all_nodes = node_length.shape[0]
    tenant_count = all_nodes - middles
    leaf_ids = jnp.arange(leaf_count, dtype=jnp.int32)
    onehot = (leaf_segment[:, :, None] == leaf_ids[None, None, :]).astype(jnp.int32)
    middle = lax.optimization_barrier(jnp.sum(onehot * leaf_node[:, None, :], axis=-1))
    counts = lax.optimization_barrier(jnp.sum(onehot, axis=1))
    starts = jnp.cumsum(counts, axis=1) - counts
    first_at = lax.optimization_barrier(jnp.sum(onehot * starts[:, None, :], axis=-1))
    middle_ids = jnp.arange(middles, dtype=jnp.int32) + tenant_count
    root_node = lax.optimization_barrier(jnp.sum(jnp.where(middle[..., None] == middle_ids, node_parent, 0), axis=-1))
    node_ids = jnp.arange(all_nodes, dtype=jnp.int32)
    len_middle = lax.optimization_barrier(jnp.sum(jnp.where(middle[..., None] == node_ids, node_length, 0), axis=-1))
    len_root = lax.optimization_barrier(jnp.sum(jnp.where(root_node[..., None] == node_ids, node_length, 0), axis=-1))
    offsets = jnp.arange(tok_rows, dtype=jnp.int32)[None, :] - first_at
    position = len_root + len_middle + offsets
    return (middle, root_node, position)

def rotate(values_in, position):
    half_size = values_in.shape[-1] // 2
    frequency = THETA ** (-2.0 * jnp.arange(half_size, dtype=jnp.float32) / values_in.shape[-1])
    angles = position.astype(jnp.float32)[:, None] * frequency[None, :]
    cosine = jnp.cos(angles)[:, None, :]
    sine_part = jnp.sin(angles)[:, None, :]
    lower = values_in[..., :half_size]
    upper = values_in[..., half_size:]
    return jnp.concatenate([lower * cosine - upper * sine_part, upper * cosine + lower * sine_part], axis=-1)

def rms_norm(values_in, gain):
    return values_in * lax.rsqrt(lax.optimization_barrier(jnp.mean(values_in * values_in, axis=-1, keepdims=True)) + EPS) * gain

def reference(states_in, w_qkv, qk_gain, w_out, post_gain, w_gate_up, w_down, cache_keys, cache_values, slot_node, node_length, node_parent, leaf_segment, leaf_node):
    groups, tok_rows = leaf_segment.shape
    middle, root_node, position = tree_info(leaf_segment, leaf_node, node_parent, node_length)
    qkv_raw = jnp.einsum('td,cdw->ctw', states_in.astype(jnp.float32), w_qkv.astype(jnp.float32))
    flat_position = position.reshape(-1)

    def normed(raw_part, gain):
        scaled = rms_norm(raw_part, gain)
        return rotate(scaled.reshape(-1, HEADS, HD), flat_position).astype(jnp.bfloat16)
    queries = normed(qkv_raw[0], qk_gain[0])
    keys_new = normed(qkv_raw[1], qk_gain[1])
    values_cast = qkv_raw[2].astype(jnp.bfloat16).reshape(-1, HEADS, HD)
    slots, node_rows = (cache_keys.shape[0], cache_keys.shape[1])
    flat_keys = cache_keys.reshape(slots * node_rows, HEADS, HD).astype(jnp.float32)
    flat_values = cache_values.reshape(slots * node_rows, HEADS, HD).astype(jnp.float32)
    node_ids = jnp.arange(node_length.shape[0], dtype=jnp.int32)
    slot_length = lax.optimization_barrier(jnp.sum(jnp.where(slot_node[:, None] == node_ids[None, :], node_length[None, :], 0), axis=-1))
    node_flat = jnp.broadcast_to(slot_node[:, None], (slots, node_rows)).reshape(-1)
    length_flat = jnp.broadcast_to(slot_length[:, None], (slots, node_rows)).reshape(-1)
    row_flat = jnp.broadcast_to(jnp.arange(node_rows, dtype=jnp.int32)[None, :], (slots, node_rows)).reshape(-1)
    inside = row_flat < length_flat

    def one_group(items):
        group_q, group_k, group_v, group_mid, group_root, group_seg = items
        see_cache = ((node_flat[None, :] == group_mid[:, None]) | (node_flat[None, :] == group_root[:, None])) & inside[None, :]
        order = jnp.arange(tok_rows, dtype=jnp.int32)
        see_leaf = (group_seg[:, None] == group_seg[None, :]) & (order[None, :] <= order[:, None])
        visible = jnp.concatenate([see_cache, see_leaf], axis=1)
        all_keys = jnp.concatenate([flat_keys, group_k.astype(jnp.float32)], axis=0)
        all_values = jnp.concatenate([flat_values, group_v.astype(jnp.float32)], axis=0)
        scores = jnp.einsum('rhe,khe->rhk', group_q.astype(jnp.float32), all_keys) * HD ** (-0.5)
        masked = jnp.where(visible[:, None, :], scores, NEG)
        peak = lax.optimization_barrier(jnp.max(masked, axis=-1, keepdims=True))
        weights = jnp.where(visible[:, None, :], jnp.exp(masked - peak), 0.0)
        weights_low = weights.astype(jnp.bfloat16)
        numer = jnp.einsum('rhk,khe->rhe', weights_low.astype(jnp.float32), all_values)
        return (numer / lax.optimization_barrier(jnp.sum(weights, axis=-1))[..., None]).astype(jnp.bfloat16)
    attended = lax.map(one_group, (queries.reshape(groups, tok_rows, HEADS, HD), keys_new.reshape(groups, tok_rows, HEADS, HD), values_cast.reshape(groups, tok_rows, HEADS, HD), middle, root_node, leaf_segment))
    attended = attended.reshape(groups * tok_rows, HEADS * HD)
    attn_proj = jnp.dot(attended, w_out, preferred_element_type=jnp.float32)
    mid_state = (states_in.astype(jnp.float32) + rms_norm(attn_proj, post_gain[0])).astype(jnp.bfloat16)
    gate_part = jnp.dot(mid_state, w_gate_up[0], preferred_element_type=jnp.float32)
    up_part = jnp.dot(mid_state, w_gate_up[1], preferred_element_type=jnp.float32)
    hidden = (jax.nn.silu(gate_part) * up_part).astype(jnp.bfloat16)
    mlp_proj = jnp.dot(hidden, w_down, preferred_element_type=jnp.float32)
    return (mid_state.astype(jnp.float32) + rms_norm(mlp_proj, post_gain[1])).astype(jnp.bfloat16)
```

```python
import functools

import jax
import jax.numpy as jnp
from jax import lax
from jax.experimental import pallas as pl
from jax.experimental.pallas import tpu as pltpu
from jax.sharding import Mesh, PartitionSpec as P

HD = 128
EPS = 1e-06
THETA = 500000.0
NEG = -1e30
LOG2E = 1.4426950408889634
BF = jnp.bfloat16
F32 = jnp.float32
BLK = ("yhi", "x", "z")
HEAD = ("ylo", "core")


def shift(values, axis, by):
    n = lax.axis_size(axis)
    return lax.ppermute(values, axis, [(i, (i + by) % n) for i in range(n)])


def select_row(table, row):
    return lax.dynamic_index_in_dim(table, row, 0, keepdims=False)


def tree_info(leaf_segment, leaf_node, node_parent, node_length):
    groups, tok_rows = leaf_segment.shape
    leaf_count = leaf_node.shape[1]
    middles = node_parent.shape[0]
    all_nodes = node_length.shape[0]
    tenant_count = all_nodes - middles
    leaf_ids = jnp.arange(leaf_count, dtype=jnp.int32)
    onehot = (leaf_segment[:, :, None] == leaf_ids[None, None, :]).astype(jnp.int32)
    middle = jnp.sum(onehot * leaf_node[:, None, :], axis=-1)
    counts = jnp.sum(onehot, axis=1)
    starts = jnp.sum(jnp.where(leaf_ids[None, :] < leaf_ids[:, None], counts[:, None, :], 0), axis=-1)
    first_at = jnp.sum(onehot * starts[:, None, :], axis=-1)
    middle_ids = jnp.arange(middles, dtype=jnp.int32) + tenant_count
    root_node = jnp.sum(jnp.where(middle[..., None] == middle_ids, node_parent, 0), axis=-1)
    node_ids = jnp.arange(all_nodes, dtype=jnp.int32)
    len_middle = jnp.sum(jnp.where(middle[..., None] == node_ids, node_length, 0), axis=-1)
    len_root = jnp.sum(jnp.where(root_node[..., None] == node_ids, node_length, 0), axis=-1)
    offsets = jnp.arange(tok_rows, dtype=jnp.int32)[None, :] - first_at
    return middle, root_node, len_root + len_middle + offsets


def rms_norm(values_in, gain):
    return (
        values_in * lax.rsqrt(jnp.mean(values_in * values_in, axis=-1, keepdims=True) + EPS) * gain
    )


def attention_body(
    plan,
    nodes_ref, lengths_ref, needed_ref,
    qkv_ref, row_info_ref, seg_ref, *rest,
):
    out_ref, k_all, v_all, state, sems = rest[-5:]
    parts = rest[:-5]
    group = pl.program_id(0)
    slots = k_all.shape[0]
    rows = qkv_ref.shape[2]

    def copies():
        for i, (part, (where, source, target, count)) in enumerate(
            (parts[item[0]], item[1:]) for item in plan
        ):
            whole = v_all if where else k_all
            yield pltpu.make_async_copy(
                part.at[pl.ds(source, count)], whole.at[pl.ds(target, count)], sems.at[i]
            )

    @pl.when(group == 0)
    def _():
        for copy in copies():
            copy.start()

    q = qkv_ref[0, 0]
    scale = HD**-0.5 * LOG2E
    nt = (((1,), (1,)), ((), ()))
    seg_col = row_info_ref[0, :, 2:3]
    seg_row = seg_ref[0]
    row_at = lax.broadcasted_iota(jnp.int32, (rows, rows), 0)
    col_at = lax.broadcasted_iota(jnp.int32, (rows, rows), 1)
    scores = lax.dot_general(q, qkv_ref[0, 1], nt, preferred_element_type=F32) * scale
    scores = jnp.where((seg_col == seg_row) & (col_at <= row_at), scores, NEG)
    peak = jnp.max(scores, axis=1, keepdims=True)
    weights = jnp.exp2(scores - peak)
    state[0] = jnp.broadcast_to(peak, (rows, HD))
    state[1] = jnp.broadcast_to(jnp.sum(weights, axis=1, keepdims=True), (rows, HD))
    state[2] = jnp.dot(weights.astype(BF), qkv_ref[0, 2], preferred_element_type=F32)

    @pl.when(group == 0)
    def _():
        for copy in copies():
            copy.wait()

    middle = row_info_ref[0, :, 0:1]
    root = row_info_ref[0, :, 1:2]
    key_at = lax.broadcasted_iota(jnp.int32, (1, k_all.shape[1]), 1)

    def one_slot(slot, carry):
        @pl.when(needed_ref[group, slot] > 0)
        def _():
            node = nodes_ref[slot]
            row_bias = jnp.where((middle == node) | (root == node), 0.0, NEG)
            col_bias = jnp.where(key_at < lengths_ref[slot], 0.0, NEG)
            scores = lax.dot_general(q, k_all[slot], nt, preferred_element_type=F32) * scale
            scores = scores + (row_bias + col_bias)
            old = state[0][:, 0:1]
            peak = jnp.maximum(old, jnp.max(scores, axis=1, keepdims=True))
            decay = jnp.exp2(old - peak)
            weights = jnp.exp2(scores - peak)
            state[0] = jnp.broadcast_to(peak, (rows, HD))
            state[1] = state[1] * decay + jnp.sum(weights, axis=1, keepdims=True)
            state[2] = state[2] * decay + jnp.dot(
                weights.astype(BF), v_all[slot], preferred_element_type=F32
            )

        return carry

    lax.fori_loop(0, slots, one_slot, 0)
    attended = (state[2] / state[1]).astype(BF)
    quarter = rows // 4
    for part in range(4):
        out_ref[0, part % 2, part // 2] = attended[part * quarter : (part + 1) * quarter]


def attention(nodes, lengths, needed, qkv, row_info, seg_row, parts, plan):
    groups, _, rows, _ = qkv.shape
    slots = nodes.shape[0]
    node_rows = parts[0].shape[1]
    one = lambda shape: pl.BlockSpec((1,) + shape, lambda g, *_: (g,) + (0,) * len(shape))
    return pl.pallas_call(
        functools.partial(attention_body, plan),
        out_shape=jax.ShapeDtypeStruct((groups, 2, 2, rows // 4, HD), BF),
        grid_spec=pltpu.PrefetchScalarGridSpec(
            num_scalar_prefetch=3,
            grid=(groups,),
            in_specs=[one((3, rows, HD)), one((rows, 3)), one((1, rows))]
            + [pl.BlockSpec(memory_space=pl.ANY)] * len(parts),
            out_specs=one((2, 2, rows // 4, HD)),
            scratch_shapes=[
                pltpu.VMEM((slots, node_rows, HD), BF),
                pltpu.VMEM((slots, node_rows, HD), BF),
                pltpu.VMEM((3, rows, HD), F32),
                pltpu.SemaphoreType.DMA((len(plan),)),
            ],
        ),
        compiler_params=pltpu.CompilerParams(vmem_limit_bytes=32 << 20),
    )(nodes, lengths, needed, qkv, row_info, seg_row, *parts)


def on_device(
    states_in,
    w_qkv,
    qk_gain,
    w_out,
    post_gain,
    w_gate_up,
    w_down,
    cache_keys,
    cache_values,
    slot_node,
    node_length,
    node_parent,
    leaf_segment,
    leaf_node,
):
    yhi, x_at, z_at, ylo, core = (lax.axis_index(a) for a in ("yhi", "x", "z", "ylo", "core"))
    n_y, n_x, n_z = (lax.axis_size(a) for a in BLK)
    blk = (yhi * n_x + x_at) * n_z + z_at
    head_index = ylo * 2 + core
    rows = states_in.shape[0]
    heads_here = w_qkv.shape[2] // HD
    columns = w_qkv.shape[2] * 4

    def head_piece(cache, z_to):
        return lax.dynamic_slice_in_dim(cache[0], z_to * HD, HD, 1)

    def along_z(cache):
        got = [head_piece(cache, z_at)]
        for s in range(1, n_z):
            got.append(shift(head_piece(cache, (z_at + s) % n_z), "z", s))
        return jnp.stack(got)

    k4 = along_z(cache_keys)
    v4 = along_z(cache_values)
    k8 = jnp.concatenate([k4, shift(k4, "yhi", 1)])
    k_parts = [k8] + [shift(k8, "x", s) for s in range(1, n_x)]
    v16 = jnp.concatenate([v4] + [shift(v4, "x", s) for s in range(1, n_x)])
    v_parts = [v16, shift(v16, "yhi", 1)]
    k_order = jnp.arange(n_y * n_x * n_z, dtype=jnp.int32)
    sx, sy, sz = k_order // (n_y * n_z), (k_order // n_z) % n_y, k_order % n_z
    slot_from = (
        ((yhi - sy) % n_y) * n_x + (x_at - sx) % n_x
    ) * n_z + (z_at - sz) % n_z
    plan = [(a, 0, 0, a * n_y * n_z, n_y * n_z) for a in range(n_x)]
    plan += [
        (n_x + b, 1, a * n_z, (a * n_y + b) * n_z, n_z) for b in range(n_y) for a in range(n_x)
    ]

    def other_weights(weights):
        there = lax.ppermute(weights, ("yhi", "core"), [(3, 1), (0, 2)])
        return jnp.where(yhi == core, weights, there)

    w_gu = other_weights(w_gate_up)
    w_dn = other_weights(w_down)
    w_out_other = shift(w_out, "core", 1)

    qkv_raw = jnp.einsum("td,cdw->ctw", states_in, w_qkv, preferred_element_type=F32)
    squares = lax.psum(jnp.sum(qkv_raw[:2] * qkv_raw[:2], axis=2), HEAD)
    quad = (yhi * n_x + x_at) * n_z
    seg_quad = lax.dynamic_slice_in_dim(leaf_segment, quad, n_z, 0)
    leaf_quad = lax.dynamic_slice_in_dim(leaf_node, quad, n_z, 0)
    middle, root, position_quad = tree_info(seg_quad, leaf_quad, node_parent, node_length)
    position = select_row(position_quad, z_at)
    half = HD // 2
    frequency = THETA ** (-2.0 * jnp.arange(half, dtype=F32) / HD)
    angles = position.astype(F32)[:, None] * frequency[None, :]
    cosine, sine = jnp.cos(angles)[:, None, :], jnp.sin(angles)[:, None, :]

    def normed(c):
        scaled = qkv_raw[c] * lax.rsqrt(squares[c] / columns + EPS)[:, None] * qk_gain[c]
        scaled = scaled.reshape(rows, heads_here, HD)
        low, high = scaled[..., :half], scaled[..., half:]
        turned = jnp.concatenate([low * cosine - high * sine, high * cosine + low * sine], axis=-1)
        return turned.astype(BF)

    qkv = jnp.stack(
        [normed(0), normed(1), qkv_raw[2].astype(BF).reshape(rows, heads_here, HD)]
    )
    qkv = lax.all_to_all(qkv.transpose(2, 0, 1, 3), "z", 0, 0, tiled=True)

    slot_nodes = jnp.take(slot_node, slot_from)
    slot_lengths = jnp.take(node_length, slot_nodes)
    needed = jnp.any(
        (middle[:, None, :] == slot_nodes[None, :, None])
        | (root[:, None, :] == slot_nodes[None, :, None]),
        axis=-1,
    ).astype(jnp.int32)
    row_info = jnp.stack([middle, root, seg_quad], axis=-1)
    attended = attention(
        slot_nodes, slot_lengths, needed, qkv, row_info, seg_quad[:, None, :], k_parts + v_parts, plan
    )
    attended = lax.all_to_all(
        attended.reshape((n_z * 2,) + attended.shape[2:]), ("z", "core"), 0, 0, tiled=True
    )
    attended = attended.reshape(n_z, 2, rows // 2, HD)

    def of_core(c):
        part = lax.dynamic_index_in_dim(attended, c, 1, keepdims=False)
        return part.transpose(1, 0, 2).reshape(rows // 2, n_z * HD)

    attn_part = jnp.dot(of_core(core), w_out, preferred_element_type=F32) + jnp.dot(
        of_core(1 - core), w_out_other, preferred_element_type=F32
    )
    attn_part = attn_part.reshape(2, rows // 4, -1)
    attn_proj = select_row(attn_part, ylo) + shift(
        select_row(attn_part, 1 - ylo).astype(BF), "ylo", 1
    ).astype(F32)
    own_rows = rows // 4
    state_rows = lax.dynamic_slice_in_dim(states_in, head_index * own_rows, own_rows, 0)
    mid_state = (state_rows.astype(F32) + rms_norm(attn_proj, post_gain[0])).astype(BF)

    cut = own_rows // 2
    upper, lower = mid_state[:cut], mid_state[cut:]
    upper4 = jnp.concatenate([upper] + [shift(upper, "x", s) for s in range(1, n_x)])
    lower4 = jnp.concatenate([lower] + [shift(lower, "z", s) for s in range(1, n_z)])

    def hidden_part(tokens):
        gate = jnp.dot(tokens, w_gu[0], preferred_element_type=F32)
        up = jnp.dot(tokens, w_gu[1], preferred_element_type=F32)
        hidden = (jax.nn.silu(gate) * up).astype(BF)
        return jnp.dot(hidden, w_dn, preferred_element_type=F32)

    upper_sum = lower_sum = 0.0
    for t in (0, 1, 3, 2):
        if t == 0:
            tokens = jnp.concatenate([upper4, lower4])
        else:
            tokens = jnp.concatenate([shift(upper4, "z", t), shift(lower4, "x", t)])
        count = tokens.shape[0]
        part = hidden_part(jnp.concatenate([tokens, shift(tokens, "core", 1)]))
        total = part[:count] + shift(part[count:].astype(BF), "core", 1).astype(F32)
        up_part, low_part = total[: count // 2], total[count // 2 :]
        if t:
            up_part = shift(up_part.astype(BF), "z", n_z - t).astype(F32)
            low_part = shift(low_part.astype(BF), "x", n_x - t).astype(F32)
        upper_sum = upper_sum + up_part
        lower_sum = lower_sum + low_part
    upper_sum = upper_sum.reshape(n_x, cut, -1)
    lower_sum = lower_sum.reshape(n_z, cut, -1)
    upper_out, lower_out = upper_sum[0], lower_sum[0]
    for s in range(1, 4):
        upper_out = upper_out + shift(upper_sum[s].astype(BF), "x", n_x - s).astype(F32)
        lower_out = lower_out + shift(lower_sum[s].astype(BF), "z", n_z - s).astype(F32)
    mlp_proj = jnp.concatenate([upper_out, lower_out])
    return (mid_state.astype(F32) + rms_norm(mlp_proj, post_gain[1])).astype(BF)


def solution(mesh):
    fine = Mesh(mesh.devices.reshape(2, 4, 4, 2, 2), BLK + HEAD)
    placed = (
        P(BLK, None),
        P(None, None, HEAD),
        P(None, HEAD),
        P(HEAD, None),
        P(),
        P(None, None, BLK),
        P(BLK, None),
        P(BLK, None, HEAD),
        P(BLK, None, HEAD),
        P(),
        P(),
        P(),
        P(),
        P(),
    )
    return jax.shard_map(
        on_device, mesh=fine, in_specs=placed, out_specs=P(BLK + HEAD, None), check_vma=False
    )
```

```python
import functools

import jax
import jax.numpy as jnp
from jax import lax
from jax.experimental import pallas as pl
from jax.experimental.pallas import tpu as pltpu
from jax.sharding import Mesh, PartitionSpec as P

HD = 128
EPS = 1e-06
THETA = 500000.0
NEG = -1e30
LOG2E = 1.4426950408889634
BF = jnp.bfloat16
F32 = jnp.float32
BLK = ("yhi", "x", "z")
HEAD = ("ylo", "core")


def shift(values, axis, by):
    n = lax.axis_size(axis)
    return lax.ppermute(values, axis, [(i, (i + by) % n) for i in range(n)])


def select_row(table, row):
    return lax.dynamic_index_in_dim(table, row, 0, keepdims=False)


def tree_info(leaf_segment, leaf_node, node_parent, node_length):
    groups, tok_rows = leaf_segment.shape
    leaf_count = leaf_node.shape[1]
    middles = node_parent.shape[0]
    all_nodes = node_length.shape[0]
    tenant_count = all_nodes - middles
    leaf_ids = jnp.arange(leaf_count, dtype=jnp.int32)
    onehot = (leaf_segment[:, :, None] == leaf_ids[None, None, :]).astype(jnp.int32)
    middle = jnp.sum(onehot * leaf_node[:, None, :], axis=-1)
    counts = jnp.sum(onehot, axis=1)
    starts = jnp.sum(jnp.where(leaf_ids[None, :] < leaf_ids[:, None], counts[:, None, :], 0), axis=-1)
    first_at = jnp.sum(onehot * starts[:, None, :], axis=-1)
    middle_ids = jnp.arange(middles, dtype=jnp.int32) + tenant_count
    root_node = jnp.sum(jnp.where(middle[..., None] == middle_ids, node_parent, 0), axis=-1)
    node_ids = jnp.arange(all_nodes, dtype=jnp.int32)
    len_middle = jnp.sum(jnp.where(middle[..., None] == node_ids, node_length, 0), axis=-1)
    len_root = jnp.sum(jnp.where(root_node[..., None] == node_ids, node_length, 0), axis=-1)
    offsets = jnp.arange(tok_rows, dtype=jnp.int32)[None, :] - first_at
    return middle, root_node, len_root + len_middle + offsets


def rms_norm(values_in, gain):
    return (
        values_in * lax.rsqrt(jnp.mean(values_in * values_in, axis=-1, keepdims=True) + EPS) * gain
    )


def attention_body(
    nodes_ref, lengths_ref, lists_ref, counts_ref,
    *rest,
):
    out_ref, qkv_ref, k_all, v_all, held, sems, qkv_sems = rest[-7:]
    qkv_parts = rest[:4]
    info_ref, seg_ref = rest[4:6]
    parts = rest[6:-7]
    step = pl.program_id(0)
    group = step // 2
    tile = step % 2
    half_rows = out_ref.shape[1]
    rows = 2 * half_rows
    node_rows = k_all.shape[1]
    per_part = parts[0].shape[0]
    batch = held.shape[2] // node_rows

    def copies():
        for i, part in enumerate(qkv_parts):
            yield pltpu.make_async_copy(part, qkv_ref.at[i], qkv_sems.at[i])
        for i, part in enumerate(parts):
            for j in range(per_part):
                yield pltpu.make_async_copy(
                    part.at[j, 0], k_all.at[i * per_part + j], sems.at[0, i, j]
                )
                yield pltpu.make_async_copy(
                    part.at[j, 1], v_all.at[i * per_part + j], sems.at[1, i, j]
                )

    @pl.when(step == 0)
    def _():
        for copy in copies():
            copy.start()
        for copy in copies():
            copy.wait()

    scale = HD**-0.5 * LOG2E
    nt = (((1,), (1,)), ((), ()))
    count = counts_ref[group, tile]

    def work(first):
        q = qkv_ref[group, 0, first : first + half_rows, :]
        seen = first + half_rows
        middle = info_ref[0, first:seen, 0:1]
        root = info_ref[0, first:seen, 1:2]
        seg_col = info_ref[0, first:seen, 2:3]
        seg_row = seg_ref[0][:, :seen]
        row_at = lax.broadcasted_iota(jnp.int32, (half_rows, seen), 0) + first
        col_at = lax.broadcasted_iota(jnp.int32, (half_rows, seen), 1)
        key_at = lax.broadcasted_iota(jnp.int32, (1, node_rows), 1)
        near = lax.dot_general(q, qkv_ref[group, 1, :seen, :], nt, preferred_element_type=F32) * scale
        near = jnp.where((seg_col == seg_row) & (col_at <= row_at), near, NEG)
        top = jnp.max(near, axis=1, keepdims=True)

        def score(i, top):
            best = None
            for j in range(batch):
                slot = lists_ref[group, tile, i * batch + j]
                node = nodes_ref[slot]
                length = jnp.where(i * batch + j < count, lengths_ref[slot], 0)
                s = lax.dot_general(q, k_all[slot], nt, preferred_element_type=F32) * scale
                shown = ((middle == node) | (root == node)) & (key_at < length)
                s = jnp.where(shown, s, NEG)
                held[i, :, j * node_rows : (j + 1) * node_rows] = s
                best = s if best is None else jnp.maximum(best, s)
            return jnp.maximum(top, jnp.max(best, axis=1, keepdims=True))

        batches = (count + batch - 1) // batch
        top = lax.fori_loop(0, batches, score, top)
        weights = jnp.exp2(near - top)
        total = jnp.sum(weights, axis=1, keepdims=True)
        summed = jnp.dot(weights.astype(BF), qkv_ref[group, 2, :seen, :], preferred_element_type=F32)

        def gather(i, carry):
            total, summed = carry
            added = None
            for j in range(batch):
                slot = lists_ref[group, tile, i * batch + j]
                w = jnp.exp2(held[i, :, j * node_rows : (j + 1) * node_rows] - top)
                added = w if added is None else added + w
                summed = summed + jnp.dot(
                    w.astype(BF), v_all[slot], preferred_element_type=F32
                )
            return total + jnp.sum(added, axis=1, keepdims=True), summed

        total, summed = lax.fori_loop(0, batches, gather, (total, summed))
        out_ref[0] = (summed / total).astype(BF)

    for t in range(2):
        @pl.when(tile == t)
        def _(t=t):
            work(t * half_rows)


def attention(nodes, lengths, lists, counts, qkv_parts, row_info, seg_row, parts):
    rows = qkv_parts[0].shape[1]
    groups = len(qkv_parts)
    per_part, _, node_rows, _ = parts[0].shape
    slots = nodes.shape[0]
    batch = 4
    one = lambda shape: pl.BlockSpec((1,) + shape, lambda i, *_: (i // 2,) + (0,) * len(shape))
    return pl.pallas_call(
        attention_body,
        out_shape=jax.ShapeDtypeStruct((groups, rows, HD), BF),
        grid_spec=pltpu.PrefetchScalarGridSpec(
            num_scalar_prefetch=4,
            grid=(groups * 2,),
            in_specs=[pl.BlockSpec(memory_space=pl.ANY)] * groups
            + [one((rows, 3)), one((1, rows))]
            + [pl.BlockSpec(memory_space=pl.ANY)] * len(parts),
            out_specs=pl.BlockSpec((1, rows // 2, HD), lambda i, *_: (i // 2, i % 2, 0)),
            scratch_shapes=[
                pltpu.VMEM((groups, 3, rows, HD), BF),
                pltpu.VMEM((slots, node_rows, HD), BF),
                pltpu.VMEM((slots, node_rows, HD), BF),
                pltpu.VMEM((lists.shape[2] // batch, rows // 2, batch * node_rows), F32),
                pltpu.SemaphoreType.DMA((2, len(parts), per_part)),
                pltpu.SemaphoreType.DMA((groups,)),
            ],
        ),
        compiler_params=pltpu.CompilerParams(vmem_limit_bytes=32 << 20),
        cost_estimate=pl.CostEstimate(
            flops=2 * 10**9, transcendentals=4 * 10**6, bytes_accessed=6 * 10**6
        ),
    )(nodes, lengths, lists, counts, *qkv_parts, row_info, seg_row, *parts)


def feed_forward_body(*refs):
    token_refs = refs[:4]
    gu_ref, dn_ref, own_ref, other_ref, held, sems = refs[4:]

    def copy(i, j):
        return pltpu.make_async_copy(token_refs[j], held.at[i], sems.at[i])

    for i in range(4):
        copy(i, i).start()

    def one(i, carry):
        for side, target in ((0, own_ref), (2, other_ref)):
            copy(i + side, side).wait()
            tokens = held[i + side]
            gate = jnp.dot(tokens, gu_ref[0], preferred_element_type=F32)
            up = jnp.dot(tokens, gu_ref[1], preferred_element_type=F32)
            hidden = (gate / (1.0 + jnp.exp(-gate)) * up).astype(BF)
            target[i] = jnp.dot(hidden, dn_ref[...], preferred_element_type=F32).astype(BF)
        return carry

    lax.fori_loop(0, 2, one, 0)


def feed_forward(parts, w_gu, w_dn):
    rows, width = parts[0].shape
    units = w_dn.shape[0]
    space = pl.BlockSpec(memory_space=pltpu.VMEM)
    out = jax.ShapeDtypeStruct((2, rows, width), BF)
    return pl.pallas_call(
        feed_forward_body,
        out_shape=(out, out),
        in_specs=[pl.BlockSpec(memory_space=pl.ANY)] * 4 + [space] * 2,
        out_specs=(space, space),
        scratch_shapes=[pltpu.VMEM((4, rows, width), BF), pltpu.SemaphoreType.DMA((4,))],
        compiler_params=pltpu.CompilerParams(vmem_limit_bytes=40 << 20),
        cost_estimate=pl.CostEstimate(
            flops=4 * rows * width * units * 6,
            transcendentals=4 * rows * units,
            bytes_accessed=(8 * rows * width + 3 * width * units) * 2,
        ),
    )(*parts, w_gu, w_dn)


def on_device(
    states_in,
    w_qkv,
    qk_gain,
    w_out,
    post_gain,
    w_gate_up,
    w_down,
    cache_keys,
    cache_values,
    slot_node,
    node_length,
    node_parent,
    leaf_segment,
    leaf_node,
):
    yhi, x_at, z_at, ylo, core = (lax.axis_index(a) for a in ("yhi", "x", "z", "ylo", "core"))
    n_y, n_x, n_z = (lax.axis_size(a) for a in BLK)
    blk = (yhi * n_x + x_at) * n_z + z_at
    head_index = ylo * 2 + core
    rows = states_in.shape[0]
    heads_here = w_qkv.shape[2] // HD
    columns = w_qkv.shape[2] * 4

    corner = ("yhi", "z", "core")

    def across(values, s):
        pairs = [
            ((y * n_z + z) * 2 + c, (c * n_z + (z + s) % n_z) * 2 + y)
            for y in range(n_y) for z in range(n_z) for c in range(2)
        ]
        return lax.ppermute(values, corner, pairs)

    def head_piece(s):
        cut = ((z_at + s) % n_z) * HD
        return jnp.stack(
            [lax.dynamic_slice_in_dim(c[0], cut, HD, 1) for c in (cache_keys, cache_values)]
        )

    cached = jnp.stack([across(head_piece(s), s) for s in range(n_z)])
    cached_parts = [cached] + [shift(cached, "x", s) for s in (1, 3, 2)]
    cached_parts = cached_parts + [shift(part, "core", 1) for part in cached_parts]
    slot_from = jnp.stack(
        [
            (jnp.where(c == 0, core, 1 - core) * n_x + (x_at - sx) % n_x) * n_z + (z_at - sz) % n_z
            for c in range(2) for sx in (0, 1, 3, 2) for sz in range(n_z)
        ]
    ).astype(jnp.int32)

    def other_weights(weights):
        there = lax.ppermute(weights, ("yhi", "core"), [(3, 1), (0, 2)])
        return jnp.where(yhi == core, weights, there)

    w_gate_up, w_down, _ = lax.optimization_barrier((w_gate_up, w_down, cached))
    w_gu = other_weights(w_gate_up)
    w_dn = other_weights(w_down)
    w_out = lax.dynamic_slice_in_dim(jnp.concatenate([w_out, w_out]), z_at * HD, w_out.shape[0], 0)

    qkv_raw = jnp.einsum("td,cdw->ctw", states_in, w_qkv, preferred_element_type=F32)
    squares = lax.psum(jnp.sum(qkv_raw[:2] * qkv_raw[:2], axis=2), HEAD)
    group_from = jnp.stack(
        [blk] + [(core * n_x + x_at) * n_z + (z_at - g) % n_z for g in range(n_z)]
    ).astype(jnp.int32)
    segments = jnp.take(leaf_segment, group_from, axis=0)
    middle, root, position = tree_info(
        segments, jnp.take(leaf_node, group_from, axis=0), node_parent, node_length
    )
    position, middle, root, segments = position[0], middle[1:], root[1:], segments[1:]
    half = HD // 2
    frequency = THETA ** (-2.0 * jnp.arange(half, dtype=F32) / HD)
    angles = position.astype(F32)[:, None] * frequency[None, :]
    cosine, sine = jnp.cos(angles)[:, None, :], jnp.sin(angles)[:, None, :]

    def normed(c):
        scaled = qkv_raw[c] * lax.rsqrt(squares[c] / columns + EPS)[:, None] * qk_gain[c]
        scaled = scaled.reshape(rows, heads_here, HD)
        low, high = scaled[..., :half], scaled[..., half:]
        turned = jnp.concatenate([low * cosine - high * sine, high * cosine + low * sine], axis=-1)
        return turned.astype(BF)

    qkv = jnp.stack(
        [normed(0), normed(1), qkv_raw[2].astype(BF).reshape(rows, heads_here, HD)]
    ).transpose(2, 0, 1, 3)
    qkv_parts = [across(select_row(qkv, (z_at + s) % n_z), s) for s in range(n_z)]

    slots = slot_from.shape[0]
    slot_nodes = jnp.take(slot_node, slot_from)
    slot_lengths = jnp.take(node_length, slot_nodes)
    halves = (n_z, 2, rows // 2, 1)
    needed = jnp.any(
        (middle.reshape(halves) == slot_nodes) | (root.reshape(halves) == slot_nodes), axis=2
    )
    before = jnp.arange(slots)[:, None] < jnp.arange(slots)[None, :]
    rank = jnp.sum(jnp.where(needed[..., :, None] & before, 1, 0), axis=2)
    longest = leaf_node.shape[1] + 4
    places = jnp.arange(longest, dtype=jnp.int32)
    lists = jnp.sum(
        jnp.where(
            needed[..., :, None] & (rank[..., :, None] == places),
            jnp.arange(slots, dtype=jnp.int32)[:, None], 0,
        ),
        axis=2,
    )
    counts = jnp.sum(needed.astype(jnp.int32), axis=2)
    row_info = jnp.stack([middle, root, segments], axis=-1)
    attended = attention(
        slot_nodes, slot_lengths, lists, counts, qkv_parts, row_info, segments[:, None, :],
        cached_parts,
    )

    def back(values, s):
        pairs = [
            ((y * n_z + z) * 2 + c, (c * n_z + (z - s) % n_z) * 2 + y)
            for y in range(n_y) for z in range(n_z) for c in range(2)
        ]
        return lax.ppermute(values, corner, pairs)

    attended = jnp.concatenate([back(attended[s], s) for s in range(n_z)], axis=1)
    attn_part = jnp.dot(attended, w_out, preferred_element_type=F32)
    attn_part = attn_part.reshape(2, 2, rows // 4, -1)

    def of_core(c):
        return lax.dynamic_index_in_dim(attn_part, c, 1, keepdims=False)

    attn_part = of_core(core) + shift(of_core(1 - core).astype(BF), "core", 1).astype(F32)
    attn_proj = select_row(attn_part, ylo) + shift(
        select_row(attn_part, 1 - ylo).astype(BF), "ylo", 1
    ).astype(F32)
    own_rows = rows // 4
    state_rows = lax.dynamic_slice_in_dim(states_in, head_index * own_rows, own_rows, 0)
    mid_state = (state_rows.astype(F32) + rms_norm(attn_proj, post_gain[0])).astype(BF)

    cut = own_rows // 2
    upper, lower = mid_state[:cut], mid_state[cut:]
    upper4 = jnp.concatenate([upper] + [shift(upper, "x", s) for s in range(1, n_x)])
    lower4 = jnp.concatenate([lower] + [shift(lower, "z", s) for s in range(1, n_z)])

    upper_sum = lower_sum = 0.0
    for t in (0, 1, 3, 2):
        pair = (upper4, lower4)
        if t:
            pair = (shift(upper4, "z", t), shift(lower4, "x", t))
        own, other = feed_forward(
            pair + (shift(pair[0], "core", 1), shift(pair[1], "core", 1)), w_gu, w_dn
        )
        total = own.astype(F32) + shift(other, "core", 1).astype(F32)
        up_part, low_part = total[0], total[1]
        if t:
            up_part = shift(up_part.astype(BF), "z", n_z - t).astype(F32)
            low_part = shift(low_part.astype(BF), "x", n_x - t).astype(F32)
        upper_sum = upper_sum + up_part
        lower_sum = lower_sum + low_part
    upper_sum = upper_sum.reshape(n_x, cut, -1)
    lower_sum = lower_sum.reshape(n_z, cut, -1)
    upper_out, lower_out = upper_sum[0], lower_sum[0]
    for s in range(1, 4):
        upper_out = upper_out + shift(upper_sum[s].astype(BF), "x", n_x - s).astype(F32)
        lower_out = lower_out + shift(lower_sum[s].astype(BF), "z", n_z - s).astype(F32)
    mlp_proj = jnp.concatenate([upper_out, lower_out])
    return (mid_state.astype(F32) + rms_norm(mlp_proj, post_gain[1])).astype(BF)


def solution(mesh):
    fine = Mesh(mesh.devices.reshape(2, 4, 4, 2, 2), BLK + HEAD)
    placed = (
        P(BLK, None),
        P(None, None, HEAD),
        P(None, HEAD),
        P(HEAD, None),
        P(),
        P(None, None, BLK),
        P(BLK, None),
        P(BLK, None, HEAD),
        P(BLK, None, HEAD),
        P(),
        P(),
        P(),
        P(),
        P(),
    )
    return jax.shard_map(
        on_device, mesh=fine, in_specs=placed, out_specs=P(BLK + HEAD, None), check_vma=False
    )
```

```python
import functools

import jax
import jax.numpy as jnp
from jax import lax
from jax.experimental import pallas as pl
from jax.experimental.pallas import tpu as pltpu
from jax.sharding import Mesh, PartitionSpec as P

HD = 128
EPS = 1e-06
THETA = 500000.0
NEG = -1e30
LOG2E = 1.4426950408889634
BF = jnp.bfloat16
F32 = jnp.float32
BLK = ("yhi", "x", "z")
HEAD = ("ylo", "core")


def shift(values, axis, by):
    n = lax.axis_size(axis)
    return lax.ppermute(values, axis, [(i, (i + by) % n) for i in range(n)])


def spread(values, axes):
    n = 1
    for axis in (axes,) if isinstance(axes, str) else axes:
        n *= lax.axis_size(axis)
    copies = lax.optimization_barrier(jnp.broadcast_to(values, (n,) + values.shape))
    return lax.all_to_all(copies, axes, 0, 0, tiled=True)


def select_row(table, row):
    return lax.dynamic_index_in_dim(table, row, 0, keepdims=False)


def tree_info(leaf_segment, leaf_node, node_parent, node_length):
    groups, tok_rows = leaf_segment.shape
    leaf_count = leaf_node.shape[1]
    middles = node_parent.shape[0]
    all_nodes = node_length.shape[0]
    tenant_count = all_nodes - middles
    leaf_ids = jnp.arange(leaf_count, dtype=jnp.int32)
    onehot = (leaf_segment[:, :, None] == leaf_ids[None, None, :]).astype(jnp.int32)
    middle = jnp.sum(onehot * leaf_node[:, None, :], axis=-1)
    counts = jnp.sum(onehot, axis=1)
    starts = jnp.sum(jnp.where(leaf_ids[None, :] < leaf_ids[:, None], counts[:, None, :], 0), axis=-1)
    first_at = jnp.sum(onehot * starts[:, None, :], axis=-1)
    middle_ids = jnp.arange(middles, dtype=jnp.int32) + tenant_count
    root_node = jnp.sum(jnp.where(middle[..., None] == middle_ids, node_parent, 0), axis=-1)
    node_ids = jnp.arange(all_nodes, dtype=jnp.int32)
    len_middle = jnp.sum(jnp.where(middle[..., None] == node_ids, node_length, 0), axis=-1)
    len_root = jnp.sum(jnp.where(root_node[..., None] == node_ids, node_length, 0), axis=-1)
    offsets = jnp.arange(tok_rows, dtype=jnp.int32)[None, :] - first_at
    return middle, root_node, len_root + len_middle + offsets


def rms_norm(values_in, gain):
    return (
        values_in * lax.rsqrt(jnp.mean(values_in * values_in, axis=-1, keepdims=True) + EPS) * gain
    )


def attention_body(
    nodes_ref, lengths_ref, lists_ref, counts_ref,
    *rest,
):
    out_ref, qkv_ref, k_all, v_all, held, sems, qkv_sems = rest[-7:]
    qkv_parts = rest[:4]
    info_ref, seg_ref = rest[4:6]
    parts = rest[6:-7]
    step = pl.program_id(0)
    group = step // 2
    tile = step % 2
    half_rows = out_ref.shape[1]
    rows = 2 * half_rows
    node_rows = k_all.shape[1]
    per_part = parts[0].shape[0]
    batch = held.shape[2] // node_rows

    def copies():
        for i, part in enumerate(qkv_parts):
            yield pltpu.make_async_copy(part, qkv_ref.at[i], qkv_sems.at[i])
        for i, part in enumerate(parts):
            for j in range(per_part):
                yield pltpu.make_async_copy(
                    part.at[j, 0], k_all.at[i * per_part + j], sems.at[0, i, j]
                )
                yield pltpu.make_async_copy(
                    part.at[j, 1], v_all.at[i * per_part + j], sems.at[1, i, j]
                )

    @pl.when(step == 0)
    def _():
        for copy in copies():
            copy.start()
        for copy in copies():
            copy.wait()

    scale = HD**-0.5 * LOG2E
    nt = (((1,), (1,)), ((), ()))
    count = counts_ref[group, tile]

    def work(first):
        q = qkv_ref[group, 0, first : first + half_rows, :]
        seen = first + half_rows
        middle = info_ref[0, first:seen, 0:1]
        root = info_ref[0, first:seen, 1:2]
        seg_col = info_ref[0, first:seen, 2:3]
        seg_row = seg_ref[0][:, :seen]
        row_at = lax.broadcasted_iota(jnp.int32, (half_rows, seen), 0) + first
        col_at = lax.broadcasted_iota(jnp.int32, (half_rows, seen), 1)
        key_at = lax.broadcasted_iota(jnp.int32, (1, node_rows), 1)
        near = lax.dot_general(q, qkv_ref[group, 1, :seen, :], nt, preferred_element_type=F32) * scale
        near = jnp.where((seg_col == seg_row) & (col_at <= row_at), near, NEG)
        top = jnp.max(near, axis=1, keepdims=True)

        def score(i, top):
            best = None
            for j in range(batch):
                slot = lists_ref[group, tile, i * batch + j]
                node = nodes_ref[slot]
                length = jnp.where(i * batch + j < count, lengths_ref[slot], 0)
                s = lax.dot_general(q, k_all[slot], nt, preferred_element_type=F32) * scale
                shown = ((middle == node) | (root == node)) & (key_at < length)
                s = jnp.where(shown, s, NEG)
                held[i, :, j * node_rows : (j + 1) * node_rows] = s
                best = s if best is None else jnp.maximum(best, s)
            return jnp.maximum(top, jnp.max(best, axis=1, keepdims=True))

        batches = (count + batch - 1) // batch
        top = lax.fori_loop(0, batches, score, top)
        weights = jnp.exp2(near - top)
        total = jnp.sum(weights, axis=1, keepdims=True)
        summed = jnp.dot(weights.astype(BF), qkv_ref[group, 2, :seen, :], preferred_element_type=F32)

        def gather(i, carry):
            total, summed = carry
            added = None
            for j in range(batch):
                slot = lists_ref[group, tile, i * batch + j]
                w = jnp.exp2(held[i, :, j * node_rows : (j + 1) * node_rows] - top)
                added = w if added is None else added + w
                summed = summed + jnp.dot(
                    w.astype(BF), v_all[slot], preferred_element_type=F32
                )
            return total + jnp.sum(added, axis=1, keepdims=True), summed

        total, summed = lax.fori_loop(0, batches, gather, (total, summed))
        out_ref[0] = (summed / total).astype(BF)

    for t in range(2):
        @pl.when(tile == t)
        def _(t=t):
            work(t * half_rows)


def attention(nodes, lengths, lists, counts, qkv_parts, row_info, seg_row, parts):
    rows = qkv_parts[0].shape[1]
    groups = len(qkv_parts)
    per_part, _, node_rows, _ = parts[0].shape
    slots = nodes.shape[0]
    batch = 4
    one = lambda shape: pl.BlockSpec((1,) + shape, lambda i, *_: (i // 2,) + (0,) * len(shape))
    return pl.pallas_call(
        attention_body,
        out_shape=jax.ShapeDtypeStruct((groups, rows, HD), BF),
        grid_spec=pltpu.PrefetchScalarGridSpec(
            num_scalar_prefetch=4,
            grid=(groups * 2,),
            in_specs=[pl.BlockSpec(memory_space=pl.ANY)] * groups
            + [one((rows, 3)), one((1, rows))]
            + [pl.BlockSpec(memory_space=pl.ANY)] * len(parts),
            out_specs=pl.BlockSpec((1, rows // 2, HD), lambda i, *_: (i // 2, i % 2, 0)),
            scratch_shapes=[
                pltpu.VMEM((groups, 3, rows, HD), BF),
                pltpu.VMEM((slots, node_rows, HD), BF),
                pltpu.VMEM((slots, node_rows, HD), BF),
                pltpu.VMEM((lists.shape[2] // batch, rows // 2, batch * node_rows), F32),
                pltpu.SemaphoreType.DMA((2, len(parts), per_part)),
                pltpu.SemaphoreType.DMA((groups,)),
            ],
        ),
        compiler_params=pltpu.CompilerParams(vmem_limit_bytes=32 << 20),
        cost_estimate=pl.CostEstimate(
            flops=2 * 10**9, transcendentals=4 * 10**6, bytes_accessed=6 * 10**6
        ),
    )(nodes, lengths, lists, counts, *qkv_parts, row_info, seg_row, *parts)


def feed_forward_body(
    own_tokens, other_tokens, gu_a, dn_a, gu_b, dn_b, own_ref, other_ref
):
    rows = 128

    def one(i, carry):
        at = pl.ds(i * rows, rows)
        for tokens_ref, target in ((own_tokens, own_ref), (other_tokens, other_ref)):
            tokens = tokens_ref[at, :]
            part = 0.0
            for gu_ref, dn_ref in ((gu_a, dn_a), (gu_b, dn_b)):
                gate = jnp.dot(tokens, gu_ref[0], preferred_element_type=F32)
                up = jnp.dot(tokens, gu_ref[1], preferred_element_type=F32)
                hidden = (gate / (1.0 + jnp.exp(-gate)) * up).astype(BF)
                part = part + jnp.dot(hidden, dn_ref[...], preferred_element_type=F32)
            target[at, :] = part.astype(BF)
        return carry

    lax.fori_loop(0, own_tokens.shape[0] // rows, one, 0)


def feed_forward(own, other, weights):
    rows, width = own.shape
    units = weights[1].shape[0]
    space = pl.BlockSpec(memory_space=pltpu.VMEM)
    out = jax.ShapeDtypeStruct((rows, width), BF)
    return pl.pallas_call(
        feed_forward_body,
        out_shape=(out, out),
        in_specs=[space] * 6,
        out_specs=(space, space),
        compiler_params=pltpu.CompilerParams(vmem_limit_bytes=40 << 20),
        cost_estimate=pl.CostEstimate(
            flops=4 * rows * width * units * 6,
            transcendentals=4 * rows * units,
            bytes_accessed=(4 * rows * width + 6 * width * units) * 2,
        ),
    )(own, other, *weights)


def on_device(
    states_in,
    w_qkv,
    qk_gain,
    w_out,
    post_gain,
    w_gate_up,
    w_down,
    cache_keys,
    cache_values,
    slot_node,
    node_length,
    node_parent,
    leaf_segment,
    leaf_node,
):
    yhi, x_at, z_at, ylo, core = (lax.axis_index(a) for a in ("yhi", "x", "z", "ylo", "core"))
    n_y, n_x, n_z = (lax.axis_size(a) for a in BLK)
    blk = (yhi * n_x + x_at) * n_z + z_at
    head_index = ylo * 2 + core
    rows = states_in.shape[0]
    heads_here = w_qkv.shape[2] // HD
    columns = w_qkv.shape[2] * 4

    corner = ("yhi", "z", "core")

    def across(values, s):
        pairs = [
            ((y * n_z + z) * 2 + c, (c * n_z + (z + s) % n_z) * 2 + y)
            for y in range(n_y) for z in range(n_z) for c in range(2)
        ]
        return lax.ppermute(values, corner, pairs)

    def head_piece(s):
        cut = ((z_at + s) % n_z) * HD
        return jnp.stack(
            [lax.dynamic_slice_in_dim(c[0], cut, HD, 1) for c in (cache_keys, cache_values)]
        )

    cached = jnp.stack([across(head_piece(s), s) for s in range(n_z)])
    states_in, cached = lax.optimization_barrier((states_in, cached))
    cached_own = spread(cached, "x").reshape((n_x * n_z,) + cached.shape[1:])
    cached_parts = [cached_own, shift(cached_own, "core", 1)]
    slot_from = jnp.stack(
        [
            (jnp.where(c == 0, core, 1 - core) * n_x + x) * n_z + (z_at - sz) % n_z
            for c in range(2) for x in range(n_x) for sz in range(n_z)
        ]
    ).astype(jnp.int32)

    w_out = lax.dynamic_slice_in_dim(jnp.concatenate([w_out, w_out]), z_at * HD, w_out.shape[0], 0)

    qkv_raw = jnp.einsum("td,cdw->ctw", states_in, w_qkv, preferred_element_type=F32)
    squares = lax.psum(jnp.sum(qkv_raw[:2] * qkv_raw[:2], axis=2), HEAD)
    group_from = jnp.stack(
        [blk] + [(core * n_x + x_at) * n_z + (z_at - g) % n_z for g in range(n_z)]
    ).astype(jnp.int32)
    segments = jnp.take(leaf_segment, group_from, axis=0)
    middle, root, position = tree_info(
        segments, jnp.take(leaf_node, group_from, axis=0), node_parent, node_length
    )
    position, middle, root, segments = position[0], middle[1:], root[1:], segments[1:]
    half = HD // 2
    frequency = THETA ** (-2.0 * jnp.arange(half, dtype=F32) / HD)
    angles = position.astype(F32)[:, None] * frequency[None, :]
    cosine, sine = jnp.cos(angles)[:, None, :], jnp.sin(angles)[:, None, :]

    def normed(c):
        scaled = qkv_raw[c] * lax.rsqrt(squares[c] / columns + EPS)[:, None] * qk_gain[c]
        scaled = scaled.reshape(rows, heads_here, HD)
        low, high = scaled[..., :half], scaled[..., half:]
        turned = jnp.concatenate([low * cosine - high * sine, high * cosine + low * sine], axis=-1)
        return turned.astype(BF)

    qkv = jnp.stack(
        [normed(0), normed(1), qkv_raw[2].astype(BF).reshape(rows, heads_here, HD)]
    ).transpose(2, 0, 1, 3)
    qkv_parts = [across(select_row(qkv, (z_at + s) % n_z), s) for s in range(n_z)]

    w_gate_up, w_down, qkv_parts = lax.optimization_barrier((w_gate_up, w_down, qkv_parts))

    def ring_weights(weights):
        beside = lax.ppermute(
            weights, ("z", "core"),
            [(z * 2 + c, (z + 1 - 2 * c) % n_z * 2 + c) for z in range(n_z) for c in range(2)],
        )
        far = lax.ppermute(
            weights, ("z", "core"), [(z * 2 + 1, (z + 2) % n_z * 2 + 1) for z in range(n_z)]
        )
        return beside, jnp.where(core == 0, weights, far)

    gu_a, gu_b = ring_weights(w_gate_up)
    dn_a, dn_b = ring_weights(w_down)

    slots = slot_from.shape[0]
    slot_nodes = jnp.take(slot_node, slot_from)
    slot_lengths = jnp.take(node_length, slot_nodes)
    halves = (n_z, 2, rows // 2, 1)
    needed = jnp.any(
        (middle.reshape(halves) == slot_nodes) | (root.reshape(halves) == slot_nodes), axis=2
    )
    before = jnp.arange(slots)[:, None] < jnp.arange(slots)[None, :]
    rank = jnp.sum(jnp.where(needed[..., :, None] & before, 1, 0), axis=2)
    longest = leaf_node.shape[1] + 4
    places = jnp.arange(longest, dtype=jnp.int32)
    lists = jnp.sum(
        jnp.where(
            needed[..., :, None] & (rank[..., :, None] == places),
            jnp.arange(slots, dtype=jnp.int32)[:, None], 0,
        ),
        axis=2,
    )
    counts = jnp.sum(needed.astype(jnp.int32), axis=2)
    row_info = jnp.stack([middle, root, segments], axis=-1)
    attended = attention(
        slot_nodes, slot_lengths, lists, counts, qkv_parts, row_info, segments[:, None, :],
        cached_parts,
    )

    def back(values, s):
        pairs = [
            ((y * n_z + z) * 2 + c, (c * n_z + (z - s) % n_z) * 2 + y)
            for y in range(n_y) for z in range(n_z) for c in range(2)
        ]
        return lax.ppermute(values, corner, pairs)

    attended = jnp.concatenate([back(attended[s], s) for s in range(n_z)], axis=1)
    attn_part = jnp.dot(attended, w_out, preferred_element_type=F32)
    attn_part = attn_part.reshape(2, 2, rows // 4, -1)

    def of_core(c):
        return lax.dynamic_index_in_dim(attn_part, c, 1, keepdims=False)

    attn_part = of_core(core) + shift(of_core(1 - core).astype(BF), "core", 1).astype(F32)
    attn_proj = select_row(attn_part, ylo) + shift(
        select_row(attn_part, 1 - ylo).astype(BF), "ylo", 1
    ).astype(F32)
    own_rows = rows // 4
    state_rows = lax.dynamic_slice_in_dim(states_in, head_index * own_rows, own_rows, 0)
    mid_state = (state_rows.astype(F32) + rms_norm(attn_proj, post_gain[0])).astype(BF)

    chunks = 2
    cut = own_rows // chunks
    plane = ("yhi", "x")
    n_plane = n_y * n_x
    mlp_parts = []
    for i in range(chunks):
        tokens = spread(mid_state[i * cut : (i + 1) * cut], plane).reshape(n_plane * cut, -1)
        own, other = feed_forward(tokens, shift(tokens, "core", 1), (gu_a, dn_a, gu_b, dn_b))
        total = (own.astype(F32) + shift(other, "core", 1).astype(F32)).astype(BF)
        total = lax.all_to_all(total.reshape(n_plane, cut, -1), plane, 0, 0, tiled=True)
        mlp_parts.append(jnp.sum(total.astype(F32), axis=0))
    mlp_proj = jnp.concatenate(mlp_parts)
    return (mid_state.astype(F32) + rms_norm(mlp_proj, post_gain[1])).astype(BF)


def solution(mesh):
    fine = Mesh(mesh.devices.reshape(2, 4, 4, 2, 2), BLK + HEAD)
    placed = (
        P(BLK, None),
        P(None, None, HEAD),
        P(None, HEAD),
        P(HEAD, None),
        P(),
        P(None, None, BLK),
        P(BLK, None),
        P(BLK, None, HEAD),
        P(BLK, None, HEAD),
        P(),
        P(),
        P(),
        P(),
        P(),
    )
    return jax.shard_map(
        on_device, mesh=fine, in_specs=placed, out_specs=P(BLK + HEAD, None), check_vma=False
    )
```

```python
import functools

import jax
import jax.numpy as jnp
from jax import lax
from jax.experimental import pallas as pl
from jax.experimental.pallas import tpu as pltpu
from jax.sharding import Mesh, PartitionSpec as P

HD = 128
EPS = 1e-06
THETA = 500000.0
NEG = -1e30
LOG2E = 1.4426950408889634
BF = jnp.bfloat16
F32 = jnp.float32
BLK = ("yhi", "x", "z")
HEAD = ("ylo", "core")


def shift(values, axis, by):
    n = lax.axis_size(axis)
    return lax.ppermute(values, axis, [(i, (i + by) % n) for i in range(n)])


def spread(values, axes):
    n = 1
    for axis in (axes,) if isinstance(axes, str) else axes:
        n *= lax.axis_size(axis)
    copies = lax.optimization_barrier(jnp.broadcast_to(values, (n,) + values.shape))
    return lax.all_to_all(copies, axes, 0, 0, tiled=True)


def select_row(table, row):
    return lax.dynamic_index_in_dim(table, row, 0, keepdims=False)


def tree_info(leaf_segment, leaf_node, node_parent, node_length):
    groups, tok_rows = leaf_segment.shape
    leaf_count = leaf_node.shape[1]
    middles = node_parent.shape[0]
    all_nodes = node_length.shape[0]
    tenant_count = all_nodes - middles
    leaf_ids = jnp.arange(leaf_count, dtype=jnp.int32)
    onehot = (leaf_segment[:, :, None] == leaf_ids[None, None, :]).astype(jnp.int32)
    middle = jnp.sum(onehot * leaf_node[:, None, :], axis=-1)
    counts = jnp.sum(onehot, axis=1)
    starts = jnp.sum(jnp.where(leaf_ids[None, :] < leaf_ids[:, None], counts[:, None, :], 0), axis=-1)
    first_at = jnp.sum(onehot * starts[:, None, :], axis=-1)
    middle_ids = jnp.arange(middles, dtype=jnp.int32) + tenant_count
    root_node = jnp.sum(jnp.where(middle[..., None] == middle_ids, node_parent, 0), axis=-1)
    node_ids = jnp.arange(all_nodes, dtype=jnp.int32)
    len_middle = jnp.sum(jnp.where(middle[..., None] == node_ids, node_length, 0), axis=-1)
    len_root = jnp.sum(jnp.where(root_node[..., None] == node_ids, node_length, 0), axis=-1)
    offsets = jnp.arange(tok_rows, dtype=jnp.int32)[None, :] - first_at
    return middle, root_node, len_root + len_middle + offsets


def rms_norm(values_in, gain):
    return (
        values_in * lax.rsqrt(jnp.mean(values_in * values_in, axis=-1, keepdims=True) + EPS) * gain
    )


def attention_body(
    nodes_ref, lengths_ref, lists_ref, counts_ref,
    *rest,
):
    out_ref, qkv_ref, k_all, v_all, held, sems, qkv_sems = rest[-7:]
    qkv_parts = rest[:4]
    info_ref, seg_ref = rest[4:6]
    parts = rest[6:-7]
    step = pl.program_id(0)
    group = step // 2
    tile = step % 2
    half_rows = out_ref.shape[1]
    rows = 2 * half_rows
    node_rows = k_all.shape[1]
    per_part = parts[0].shape[0]
    batch = held.shape[2] // node_rows

    def copies():
        for i, part in enumerate(qkv_parts):
            yield pltpu.make_async_copy(part, qkv_ref.at[i], qkv_sems.at[i])
        for i, part in enumerate(parts):
            for j in range(per_part):
                yield pltpu.make_async_copy(
                    part.at[j, 0], k_all.at[i * per_part + j], sems.at[0, i, j]
                )
                yield pltpu.make_async_copy(
                    part.at[j, 1], v_all.at[i * per_part + j], sems.at[1, i, j]
                )

    @pl.when(step == 0)
    def _():
        for copy in copies():
            copy.start()
        for copy in copies():
            copy.wait()

    scale = HD**-0.5 * LOG2E
    nt = (((1,), (1,)), ((), ()))
    count = counts_ref[group, tile]

    def work(first):
        q = qkv_ref[group, 0, first : first + half_rows, :]
        seen = first + half_rows
        middle = info_ref[0, first:seen, 0:1]
        root = info_ref[0, first:seen, 1:2]
        seg_col = info_ref[0, first:seen, 2:3]
        seg_row = seg_ref[0][:, :seen]
        row_at = lax.broadcasted_iota(jnp.int32, (half_rows, seen), 0) + first
        col_at = lax.broadcasted_iota(jnp.int32, (half_rows, seen), 1)
        key_at = lax.broadcasted_iota(jnp.int32, (1, node_rows), 1)
        near = lax.dot_general(q, qkv_ref[group, 1, :seen, :], nt, preferred_element_type=F32) * scale
        near = jnp.where((seg_col == seg_row) & (col_at <= row_at), near, NEG)
        top = jnp.max(near, axis=1, keepdims=True)

        def score(i, top):
            best = None
            for j in range(batch):
                slot = lists_ref[group, tile, i * batch + j]
                node = nodes_ref[slot]
                length = jnp.where(i * batch + j < count, lengths_ref[slot], 0)
                s = lax.dot_general(q, k_all[slot], nt, preferred_element_type=F32) * scale
                shown = ((middle == node) | (root == node)) & (key_at < length)
                s = jnp.where(shown, s, NEG)
                held[i, :, j * node_rows : (j + 1) * node_rows] = s
                best = s if best is None else jnp.maximum(best, s)
            return jnp.maximum(top, jnp.max(best, axis=1, keepdims=True))

        batches = (count + batch - 1) // batch
        top = lax.fori_loop(0, batches, score, top)
        weights = jnp.exp2(near - top)
        total = jnp.sum(weights, axis=1, keepdims=True)
        summed = jnp.dot(weights.astype(BF), qkv_ref[group, 2, :seen, :], preferred_element_type=F32)

        def gather(i, carry):
            total, summed = carry
            added = None
            for j in range(batch):
                slot = lists_ref[group, tile, i * batch + j]
                w = jnp.exp2(held[i, :, j * node_rows : (j + 1) * node_rows] - top)
                added = w if added is None else added + w
                summed = summed + jnp.dot(
                    w.astype(BF), v_all[slot], preferred_element_type=F32
                )
            return total + jnp.sum(added, axis=1, keepdims=True), summed

        total, summed = lax.fori_loop(0, batches, gather, (total, summed))
        out_ref[0] = (summed / total).astype(BF)

    for t in range(2):
        @pl.when(tile == t)
        def _(t=t):
            work(t * half_rows)


def attention(nodes, lengths, lists, counts, qkv_parts, row_info, seg_row, parts):
    rows = qkv_parts[0].shape[1]
    groups = len(qkv_parts)
    per_part, _, node_rows, _ = parts[0].shape
    slots = nodes.shape[0]
    batch = 4
    one = lambda shape: pl.BlockSpec((1,) + shape, lambda i, *_: (i // 2,) + (0,) * len(shape))
    return pl.pallas_call(
        attention_body,
        out_shape=jax.ShapeDtypeStruct((groups, rows, HD), BF),
        grid_spec=pltpu.PrefetchScalarGridSpec(
            num_scalar_prefetch=4,
            grid=(groups * 2,),
            in_specs=[pl.BlockSpec(memory_space=pl.ANY)] * groups
            + [one((rows, 3)), one((1, rows))]
            + [pl.BlockSpec(memory_space=pl.ANY)] * len(parts),
            out_specs=pl.BlockSpec((1, rows // 2, HD), lambda i, *_: (i // 2, i % 2, 0)),
            scratch_shapes=[
                pltpu.VMEM((groups, 3, rows, HD), BF),
                pltpu.VMEM((slots, node_rows, HD), BF),
                pltpu.VMEM((slots, node_rows, HD), BF),
                pltpu.VMEM((lists.shape[2] // batch, rows // 2, batch * node_rows), F32),
                pltpu.SemaphoreType.DMA((2, len(parts), per_part)),
                pltpu.SemaphoreType.DMA((groups,)),
            ],
        ),
        compiler_params=pltpu.CompilerParams(vmem_limit_bytes=32 << 20),
        cost_estimate=pl.CostEstimate(
            flops=2 * 10**9, transcendentals=4 * 10**6, bytes_accessed=6 * 10**6
        ),
    )(nodes, lengths, lists, counts, *qkv_parts, row_info, seg_row, *parts)


def feed_forward_body(
    own_tokens, other_tokens, gu_a, dn_a, gu_b, dn_b, own_ref, other_ref
):
    rows = 128

    def one(i, carry):
        at = pl.ds(i * rows, rows)
        for tokens_ref, target in ((own_tokens, own_ref), (other_tokens, other_ref)):
            tokens = tokens_ref[at, :]
            part = 0.0
            for gu_ref, dn_ref in ((gu_a, dn_a), (gu_b, dn_b)):
                gate = jnp.dot(tokens, gu_ref[0], preferred_element_type=F32)
                up = jnp.dot(tokens, gu_ref[1], preferred_element_type=F32)
                hidden = (gate / (1.0 + jnp.exp(-gate)) * up).astype(BF)
                part = part + jnp.dot(hidden, dn_ref[...], preferred_element_type=F32)
            target[at, :] = part.astype(BF)
        return carry

    lax.fori_loop(0, own_tokens.shape[0] // rows, one, 0)


def feed_forward(own, other, weights):
    rows, width = own.shape
    units = weights[1].shape[0]
    space = pl.BlockSpec(memory_space=pltpu.VMEM)
    out = jax.ShapeDtypeStruct((rows, width), BF)
    return pl.pallas_call(
        feed_forward_body,
        out_shape=(out, out),
        in_specs=[space] * 6,
        out_specs=(space, space),
        compiler_params=pltpu.CompilerParams(vmem_limit_bytes=40 << 20),
        cost_estimate=pl.CostEstimate(
            flops=4 * rows * width * units * 6,
            transcendentals=4 * rows * units,
            bytes_accessed=(4 * rows * width + 6 * width * units) * 2,
        ),
    )(own, other, *weights)


def on_device(
    states_in,
    w_qkv,
    qk_gain,
    w_out,
    post_gain,
    w_gate_up,
    w_down,
    cache_keys,
    cache_values,
    slot_node,
    node_length,
    node_parent,
    leaf_segment,
    leaf_node,
):
    yhi, x_at, z_at, ylo, core = (lax.axis_index(a) for a in ("yhi", "x", "z", "ylo", "core"))
    n_y, n_x, n_z = (lax.axis_size(a) for a in BLK)
    blk = (yhi * n_x + x_at) * n_z + z_at
    head_index = ylo * 2 + core
    rows = states_in.shape[0]
    heads_here = w_qkv.shape[2] // HD
    columns = w_qkv.shape[2] * 4

    corner = ("yhi", "z", "core")

    def across(values, s):
        pairs = [
            ((y * n_z + z) * 2 + c, (c * n_z + (z + s) % n_z) * 2 + y)
            for y in range(n_y) for z in range(n_z) for c in range(2)
        ]
        return lax.ppermute(values, corner, pairs)

    def head_piece(s):
        cut = ((z_at + s) % n_z) * HD
        return jnp.stack(
            [lax.dynamic_slice_in_dim(c[0], cut, HD, 1) for c in (cache_keys, cache_values)]
        )

    cached = jnp.stack([across(head_piece(s), s) for s in range(n_z)])
    slot_from = jnp.stack(
        [
            (jnp.where(c == 0, core, 1 - core) * n_x + x) * n_z + (z_at - sz) % n_z
            for c in range(2) for x in range(n_x) for sz in range(n_z)
        ]
    ).astype(jnp.int32)

    w_out = lax.dynamic_slice_in_dim(jnp.concatenate([w_out, w_out]), z_at * HD, w_out.shape[0], 0)

    qkv_raw = jnp.einsum("td,cdw->ctw", states_in, w_qkv, preferred_element_type=F32)
    squares = lax.psum(jnp.sum(qkv_raw[:2] * qkv_raw[:2], axis=2), HEAD)
    squares, cached = lax.optimization_barrier((squares, cached))
    cached_own = spread(cached, "x").reshape((n_x * n_z,) + cached.shape[1:])
    group_from = jnp.stack(
        [blk] + [(core * n_x + x_at) * n_z + (z_at - g) % n_z for g in range(n_z)]
    ).astype(jnp.int32)
    segments = jnp.take(leaf_segment, group_from, axis=0)
    middle, root, position = tree_info(
        segments, jnp.take(leaf_node, group_from, axis=0), node_parent, node_length
    )
    position, middle, root, segments = position[0], middle[1:], root[1:], segments[1:]
    half = HD // 2
    frequency = THETA ** (-2.0 * jnp.arange(half, dtype=F32) / HD)
    angles = position.astype(F32)[:, None] * frequency[None, :]
    cosine, sine = jnp.cos(angles)[:, None, :], jnp.sin(angles)[:, None, :]

    def normed(c):
        scaled = qkv_raw[c] * lax.rsqrt(squares[c] / columns + EPS)[:, None] * qk_gain[c]
        scaled = scaled.reshape(rows, heads_here, HD)
        low, high = scaled[..., :half], scaled[..., half:]
        turned = jnp.concatenate([low * cosine - high * sine, high * cosine + low * sine], axis=-1)
        return turned.astype(BF)

    qkv = jnp.stack(
        [normed(0), normed(1), qkv_raw[2].astype(BF).reshape(rows, heads_here, HD)]
    ).transpose(2, 0, 1, 3)
    qkv_parts = [across(select_row(qkv, (z_at + s) % n_z), s) for s in range(n_z)]

    cached_own, qkv_parts = lax.optimization_barrier((cached_own, qkv_parts))
    cached_parts = [cached_own, shift(cached_own, "core", 1)]

    def beside(weights):
        return lax.ppermute(
            weights, ("z", "core"),
            [(z * 2 + c, (z + 1 - 2 * c) % n_z * 2 + c) for z in range(n_z) for c in range(2)],
        )

    def beyond(weights):
        far = lax.ppermute(
            weights, ("z", "core"), [(z * 2 + 1, (z + 2) % n_z * 2 + 1) for z in range(n_z)]
        )
        return jnp.where(core == 0, weights, far)

    w_gate_up, w_down, _ = lax.optimization_barrier((w_gate_up, w_down, cached))
    gu_a, dn_a = beside(w_gate_up), beside(w_down)
    w_gate_up, w_down, gu_a, dn_a, qkv_parts = lax.optimization_barrier(
        (w_gate_up, w_down, gu_a, dn_a, qkv_parts)
    )
    gu_b, dn_b = beyond(w_gate_up), beyond(w_down)

    slots = slot_from.shape[0]
    slot_nodes = jnp.take(slot_node, slot_from)
    slot_lengths = jnp.take(node_length, slot_nodes)
    halves = (n_z, 2, rows // 2, 1)
    needed = jnp.any(
        (middle.reshape(halves) == slot_nodes) | (root.reshape(halves) == slot_nodes), axis=2
    )
    before = jnp.arange(slots)[:, None] < jnp.arange(slots)[None, :]
    rank = jnp.sum(jnp.where(needed[..., :, None] & before, 1, 0), axis=2)
    longest = leaf_node.shape[1] + 4
    places = jnp.arange(longest, dtype=jnp.int32)
    lists = jnp.sum(
        jnp.where(
            needed[..., :, None] & (rank[..., :, None] == places),
            jnp.arange(slots, dtype=jnp.int32)[:, None], 0,
        ),
        axis=2,
    )
    counts = jnp.sum(needed.astype(jnp.int32), axis=2)
    row_info = jnp.stack([middle, root, segments], axis=-1)
    attended = attention(
        slot_nodes, slot_lengths, lists, counts, qkv_parts, row_info, segments[:, None, :],
        cached_parts,
    )

    def back(values, s):
        pairs = [
            ((y * n_z + z) * 2 + c, (c * n_z + (z - s) % n_z) * 2 + y)
            for y in range(n_y) for z in range(n_z) for c in range(2)
        ]
        return lax.ppermute(values, corner, pairs)

    attended = jnp.concatenate([back(attended[s], s) for s in range(n_z)], axis=1)
    attended, gu_b, dn_b = lax.optimization_barrier((attended, gu_b, dn_b))
    attn_part = jnp.dot(attended, w_out, preferred_element_type=F32)
    attn_part = attn_part.reshape(2, 2, rows // 4, -1)

    def of_core(c):
        return lax.dynamic_index_in_dim(attn_part, c, 1, keepdims=False)

    attn_part = of_core(core) + shift(of_core(1 - core).astype(BF), "core", 1).astype(F32)
    attn_proj = select_row(attn_part, ylo) + shift(
        select_row(attn_part, 1 - ylo).astype(BF), "ylo", 1
    ).astype(F32)
    own_rows = rows // 4
    state_rows = lax.dynamic_slice_in_dim(states_in, head_index * own_rows, own_rows, 0)
    mid_state = (state_rows.astype(F32) + rms_norm(attn_proj, post_gain[0])).astype(BF)

    chunks = 2
    cut = own_rows // chunks
    plane = ("yhi", "x")
    n_plane = n_y * n_x
    mlp_parts = []
    for i in range(chunks):
        tokens = spread(mid_state[i * cut : (i + 1) * cut], plane).reshape(n_plane * cut, -1)
        own, other = feed_forward(tokens, shift(tokens, "core", 1), (gu_a, dn_a, gu_b, dn_b))
        total = (own.astype(F32) + shift(other, "core", 1).astype(F32)).astype(BF)
        total = lax.all_to_all(total.reshape(n_plane, cut, -1), plane, 0, 0, tiled=True)
        mlp_parts.append(jnp.sum(total.astype(F32), axis=0))
    mlp_proj = jnp.concatenate(mlp_parts)
    return (mid_state.astype(F32) + rms_norm(mlp_proj, post_gain[1])).astype(BF)


def solution(mesh):
    fine = Mesh(mesh.devices.reshape(2, 4, 4, 2, 2), BLK + HEAD)
    placed = (
        P(BLK, None),
        P(None, None, HEAD),
        P(None, HEAD),
        P(HEAD, None),
        P(),
        P(None, None, BLK),
        P(BLK, None),
        P(BLK, None, HEAD),
        P(BLK, None, HEAD),
        P(),
        P(),
        P(),
        P(),
        P(),
    )
    return jax.shard_map(
        on_device, mesh=fine, in_specs=placed, out_specs=P(BLK + HEAD, None), check_vma=False
    )
```

```python
import functools

import jax
import jax.numpy as jnp
from jax import lax
from jax.experimental import pallas as pl
from jax.experimental.pallas import tpu as pltpu
from jax.sharding import Mesh, PartitionSpec as P

HD = 128
EPS = 1e-06
THETA = 500000.0
NEG = -1e30
LOG2E = 1.4426950408889634
BF = jnp.bfloat16
F32 = jnp.float32
BLK = ("yhi", "x", "z")
HEAD = ("ylo", "core")


def shift(values, axis, by):
    n = lax.axis_size(axis)
    return lax.ppermute(values, axis, [(i, (i + by) % n) for i in range(n)])


def spread(values, axes):
    n = 1
    for axis in (axes,) if isinstance(axes, str) else axes:
        n *= lax.axis_size(axis)
    copies = lax.optimization_barrier(jnp.broadcast_to(values, (n,) + values.shape))
    return lax.all_to_all(copies, axes, 0, 0, tiled=True)


def select_row(table, row):
    return lax.dynamic_index_in_dim(table, row, 0, keepdims=False)


def tree_info(leaf_segment, leaf_node, node_parent, node_length):
    groups, tok_rows = leaf_segment.shape
    leaf_count = leaf_node.shape[1]
    middles = node_parent.shape[0]
    all_nodes = node_length.shape[0]
    tenant_count = all_nodes - middles
    leaf_ids = jnp.arange(leaf_count, dtype=jnp.int32)
    onehot = (leaf_segment[:, :, None] == leaf_ids[None, None, :]).astype(jnp.int32)
    middle = jnp.sum(onehot * leaf_node[:, None, :], axis=-1)
    counts = jnp.sum(onehot, axis=1)
    starts = jnp.sum(jnp.where(leaf_ids[None, :] < leaf_ids[:, None], counts[:, None, :], 0), axis=-1)
    first_at = jnp.sum(onehot * starts[:, None, :], axis=-1)
    middle_ids = jnp.arange(middles, dtype=jnp.int32) + tenant_count
    root_node = jnp.sum(jnp.where(middle[..., None] == middle_ids, node_parent, 0), axis=-1)
    node_ids = jnp.arange(all_nodes, dtype=jnp.int32)
    len_middle = jnp.sum(jnp.where(middle[..., None] == node_ids, node_length, 0), axis=-1)
    len_root = jnp.sum(jnp.where(root_node[..., None] == node_ids, node_length, 0), axis=-1)
    offsets = jnp.arange(tok_rows, dtype=jnp.int32)[None, :] - first_at
    return middle, root_node, len_root + len_middle + offsets


def rms_norm(values_in, gain):
    return (
        values_in * lax.rsqrt(jnp.mean(values_in * values_in, axis=-1, keepdims=True) + EPS) * gain
    )


def attention_body(
    nodes_ref, lengths_ref, lists_ref, counts_ref,
    *rest,
):
    out_ref, qkv_ref, k_all, v_all, held, sems, qkv_sems = rest[-7:]
    qkv_parts = rest[:4]
    info_ref, seg_ref = rest[4:6]
    parts = rest[6:-7]
    step = pl.program_id(0)
    group = step // 2
    tile = step % 2
    half_rows = out_ref.shape[1]
    rows = 2 * half_rows
    node_rows = k_all.shape[1]
    per_part = parts[0].shape[0]
    batch = held.shape[2] // node_rows

    def copies():
        for i, part in enumerate(qkv_parts):
            yield pltpu.make_async_copy(part, qkv_ref.at[i], qkv_sems.at[i])
        for i, part in enumerate(parts):
            for j in range(per_part):
                yield pltpu.make_async_copy(
                    part.at[j, 0], k_all.at[i * per_part + j], sems.at[0, i, j]
                )
                yield pltpu.make_async_copy(
                    part.at[j, 1], v_all.at[i * per_part + j], sems.at[1, i, j]
                )

    @pl.when(step == 0)
    def _():
        for copy in copies():
            copy.start()
        for copy in copies():
            copy.wait()

    scale = HD**-0.5 * LOG2E
    nt = (((1,), (1,)), ((), ()))
    count = counts_ref[group, tile]

    def work(first):
        q = qkv_ref[group, 0, first : first + half_rows, :]
        seen = first + half_rows
        middle = info_ref[0, first:seen, 0:1]
        root = info_ref[0, first:seen, 1:2]
        seg_col = info_ref[0, first:seen, 2:3]
        seg_row = seg_ref[0][:, :seen]
        row_at = lax.broadcasted_iota(jnp.int32, (half_rows, seen), 0) + first
        col_at = lax.broadcasted_iota(jnp.int32, (half_rows, seen), 1)
        key_at = lax.broadcasted_iota(jnp.int32, (1, node_rows), 1)
        near = lax.dot_general(q, qkv_ref[group, 1, :seen, :], nt, preferred_element_type=F32) * scale
        near = jnp.where((seg_col == seg_row) & (col_at <= row_at), near, NEG)
        top = jnp.max(near, axis=1, keepdims=True)

        def score(i, top):
            best = None
            for j in range(batch):
                slot = lists_ref[group, tile, i * batch + j]
                node = nodes_ref[slot]
                length = jnp.where(i * batch + j < count, lengths_ref[slot], 0)
                s = lax.dot_general(q, k_all[slot], nt, preferred_element_type=F32) * scale
                shown = ((middle == node) | (root == node)) & (key_at < length)
                s = jnp.where(shown, s, NEG)
                held[i, :, j * node_rows : (j + 1) * node_rows] = s
                best = s if best is None else jnp.maximum(best, s)
            return jnp.maximum(top, jnp.max(best, axis=1, keepdims=True))

        batches = (count + batch - 1) // batch
        top = lax.fori_loop(0, batches, score, top)
        weights = jnp.exp2(near - top)
        total = jnp.sum(weights, axis=1, keepdims=True)
        summed = jnp.dot(weights.astype(BF), qkv_ref[group, 2, :seen, :], preferred_element_type=F32)

        def gather(i, carry):
            total, summed = carry
            added = None
            for j in range(batch):
                slot = lists_ref[group, tile, i * batch + j]
                w = jnp.exp2(held[i, :, j * node_rows : (j + 1) * node_rows] - top)
                added = w if added is None else added + w
                summed = summed + jnp.dot(
                    w.astype(BF), v_all[slot], preferred_element_type=F32
                )
            return total + jnp.sum(added, axis=1, keepdims=True), summed

        total, summed = lax.fori_loop(0, batches, gather, (total, summed))
        out_ref[0] = (summed / total).astype(BF)

    for t in range(2):
        @pl.when(tile == t)
        def _(t=t):
            work(t * half_rows)


def attention(nodes, lengths, lists, counts, qkv_parts, row_info, seg_row, parts):
    rows = qkv_parts[0].shape[1]
    groups = len(qkv_parts)
    per_part, _, node_rows, _ = parts[0].shape
    slots = nodes.shape[0]
    batch = 4
    one = lambda shape: pl.BlockSpec((1,) + shape, lambda i, *_: (i // 2,) + (0,) * len(shape))
    return pl.pallas_call(
        attention_body,
        out_shape=jax.ShapeDtypeStruct((groups, rows, HD), BF),
        grid_spec=pltpu.PrefetchScalarGridSpec(
            num_scalar_prefetch=4,
            grid=(groups * 2,),
            in_specs=[pl.BlockSpec(memory_space=pl.ANY)] * groups
            + [one((rows, 3)), one((1, rows))]
            + [pl.BlockSpec(memory_space=pl.ANY)] * len(parts),
            out_specs=pl.BlockSpec((1, rows // 2, HD), lambda i, *_: (i // 2, i % 2, 0)),
            scratch_shapes=[
                pltpu.VMEM((groups, 3, rows, HD), BF),
                pltpu.VMEM((slots, node_rows, HD), BF),
                pltpu.VMEM((slots, node_rows, HD), BF),
                pltpu.VMEM((lists.shape[2] // batch, rows // 2, batch * node_rows), F32),
                pltpu.SemaphoreType.DMA((2, len(parts), per_part)),
                pltpu.SemaphoreType.DMA((groups,)),
            ],
        ),
        compiler_params=pltpu.CompilerParams(vmem_limit_bytes=32 << 20),
        cost_estimate=pl.CostEstimate(
            flops=2 * 10**9, transcendentals=4 * 10**6, bytes_accessed=6 * 10**6
        ),
    )(nodes, lengths, lists, counts, *qkv_parts, row_info, seg_row, *parts)


def feed_forward_body(core_ref, tokens_ref, gu_own, gu_got, dn_own, dn_got, out_ref):
    rows = 256
    first = core_ref[0] == 0
    cut = dn_own.shape[1]

    def one(i, carry):
        at = pl.ds(i * rows, rows)
        tokens = tokens_ref[at, :]
        part = 0.0
        for share in range(gu_own.shape[0]):
            one_side = jnp.dot(tokens, gu_own[share], preferred_element_type=F32)
            other_side = jnp.dot(tokens, gu_got[share], preferred_element_type=F32)
            gate = jnp.where(first, one_side, other_side)
            up = jnp.where(first, other_side, one_side)
            hidden = gate / (1.0 + jnp.exp(-gate)) * up
            low, high = hidden[:, :cut], hidden[:, cut:]
            part = part + jnp.dot(
                jnp.where(first, low, high).astype(BF), dn_own[share], preferred_element_type=F32
            )
            part = part + jnp.dot(
                jnp.where(first, high, low).astype(BF), dn_got[share], preferred_element_type=F32
            )
        out_ref[at, :] = part.astype(BF)
        return carry

    lax.fori_loop(0, tokens_ref.shape[0] // rows, one, 0)


def feed_forward(core, tokens, weights):
    rows, width = tokens.shape
    units = weights[0].shape[2] * 2
    space = pl.BlockSpec(memory_space=pltpu.VMEM)
    return pl.pallas_call(
        feed_forward_body,
        out_shape=jax.ShapeDtypeStruct((rows, width), BF),
        in_specs=[pl.BlockSpec(memory_space=pltpu.SMEM)] + [space] * 5,
        out_specs=space,
        compiler_params=pltpu.CompilerParams(vmem_limit_bytes=48 << 20),
        cost_estimate=pl.CostEstimate(
            flops=2 * rows * width * units * 3,
            transcendentals=rows * units,
            bytes_accessed=(2 * rows * width + 3 * width * units) * 2,
        ),
    )(core, tokens, *weights)


def on_device(
    states_in,
    w_qkv,
    qk_gain,
    w_out,
    post_gain,
    w_gate_up,
    w_down,
    cache_keys,
    cache_values,
    slot_node,
    node_length,
    node_parent,
    leaf_segment,
    leaf_node,
):
    yhi, x_at, z_at, ylo, core = (lax.axis_index(a) for a in ("yhi", "x", "z", "ylo", "core"))
    n_y, n_x, n_z = (lax.axis_size(a) for a in BLK)
    blk = (yhi * n_x + x_at) * n_z + z_at
    head_index = ylo * 2 + core
    rows = states_in.shape[0]
    heads_here = w_qkv.shape[2] // HD
    columns = w_qkv.shape[2] * 4

    corner = ("yhi", "z", "core")

    def across(values, s):
        pairs = [
            ((y * n_z + z) * 2 + c, (c * n_z + (z + s) % n_z) * 2 + y)
            for y in range(n_y) for z in range(n_z) for c in range(2)
        ]
        return lax.ppermute(values, corner, pairs)

    def head_piece(s):
        cut = ((z_at + s) % n_z) * HD
        return jnp.stack(
            [lax.dynamic_slice_in_dim(c[0], cut, HD, 1) for c in (cache_keys, cache_values)]
        )

    cached = jnp.stack([across(head_piece(s), s) for s in range(n_z)])
    slot_from = jnp.stack(
        [
            (jnp.where(c == 0, core, 1 - core) * n_x + x) * n_z + (z_at - sz) % n_z
            for c in range(2) for x in range(n_x) for sz in range(n_z)
        ]
    ).astype(jnp.int32)

    w_out = lax.dynamic_slice_in_dim(jnp.concatenate([w_out, w_out]), z_at * HD, w_out.shape[0], 0)

    half_units = w_down.shape[0] // 2
    gu_ring = lax.all_gather(select_row(w_gate_up, core), "z")
    dn_ring = lax.all_gather(
        lax.dynamic_slice_in_dim(w_down, core * half_units, half_units, 0), "z"
    )

    qkv_raw = jnp.einsum("td,cdw->ctw", states_in, w_qkv, preferred_element_type=F32)
    squares = lax.psum(jnp.sum(qkv_raw[:2] * qkv_raw[:2], axis=2), HEAD)
    cached_own = spread(cached, "x").reshape((n_x * n_z,) + cached.shape[1:])
    group_from = jnp.stack(
        [blk] + [(core * n_x + x_at) * n_z + (z_at - g) % n_z for g in range(n_z)]
    ).astype(jnp.int32)
    segments = jnp.take(leaf_segment, group_from, axis=0)
    middle, root, position = tree_info(
        segments, jnp.take(leaf_node, group_from, axis=0), node_parent, node_length
    )
    position, middle, root, segments = position[0], middle[1:], root[1:], segments[1:]
    half = HD // 2
    frequency = THETA ** (-2.0 * jnp.arange(half, dtype=F32) / HD)
    angles = position.astype(F32)[:, None] * frequency[None, :]
    cosine, sine = jnp.cos(angles)[:, None, :], jnp.sin(angles)[:, None, :]

    def normed(c):
        scaled = qkv_raw[c] * lax.rsqrt(squares[c] / columns + EPS)[:, None] * qk_gain[c]
        scaled = scaled.reshape(rows, heads_here, HD)
        low, high = scaled[..., :half], scaled[..., half:]
        turned = jnp.concatenate([low * cosine - high * sine, high * cosine + low * sine], axis=-1)
        return turned.astype(BF)

    qkv = jnp.stack(
        [normed(0), normed(1), qkv_raw[2].astype(BF).reshape(rows, heads_here, HD)]
    ).transpose(2, 0, 1, 3)
    qkv_parts = [across(select_row(qkv, (z_at + s) % n_z), s) for s in range(n_z)]

    cached_own, qkv_parts = lax.optimization_barrier((cached_own, qkv_parts))
    cached_parts = [cached_own, shift(cached_own, "core", 1)]

    slots = slot_from.shape[0]
    slot_nodes = jnp.take(slot_node, slot_from)
    slot_lengths = jnp.take(node_length, slot_nodes)
    halves = (n_z, 2, rows // 2, 1)
    needed = jnp.any(
        (middle.reshape(halves) == slot_nodes) | (root.reshape(halves) == slot_nodes), axis=2
    )
    before = jnp.arange(slots)[:, None] < jnp.arange(slots)[None, :]
    rank = jnp.sum(jnp.where(needed[..., :, None] & before, 1, 0), axis=2)
    longest = leaf_node.shape[1] + 4
    places = jnp.arange(longest, dtype=jnp.int32)
    lists = jnp.sum(
        jnp.where(
            needed[..., :, None] & (rank[..., :, None] == places),
            jnp.arange(slots, dtype=jnp.int32)[:, None], 0,
        ),
        axis=2,
    )
    counts = jnp.sum(needed.astype(jnp.int32), axis=2)
    row_info = jnp.stack([middle, root, segments], axis=-1)
    attended = attention(
        slot_nodes, slot_lengths, lists, counts, qkv_parts, row_info, segments[:, None, :],
        cached_parts,
    )

    def back(values, s):
        pairs = [
            ((y * n_z + z) * 2 + c, (c * n_z + (z - s) % n_z) * 2 + y)
            for y in range(n_y) for z in range(n_z) for c in range(2)
        ]
        return lax.ppermute(values, corner, pairs)

    attended = jnp.concatenate([back(attended[s], s) for s in range(n_z)], axis=1)
    attn_part = jnp.dot(attended, w_out, preferred_element_type=F32)
    attn_part = attn_part.reshape(2, 2, rows // 4, -1)

    def of_core(c):
        return lax.dynamic_index_in_dim(attn_part, c, 1, keepdims=False)

    attn_part = of_core(core) + shift(of_core(1 - core).astype(BF), "core", 1).astype(F32)
    attn_proj = select_row(attn_part, ylo) + shift(
        select_row(attn_part, 1 - ylo).astype(BF), "ylo", 1
    ).astype(F32)
    own_rows = rows // 4
    state_rows = lax.dynamic_slice_in_dim(states_in, head_index * own_rows, own_rows, 0)
    mid_state = (state_rows.astype(F32) + rms_norm(attn_proj, post_gain[0])).astype(BF)

    mid_state, gu_ring, dn_ring = lax.optimization_barrier((mid_state, gu_ring, dn_ring))
    plane = ("yhi", "x")

    def shares(ring, c):
        return lax.dynamic_slice_in_dim(ring, c * 2, 2, 0)

    weights = []
    for ring in (gu_ring, dn_ring):
        weights += [shares(ring, core), shift(shares(ring, 1 - core), "core", 1)]
    core_at = core.astype(jnp.int32).reshape(1)
    tokens = spread(mid_state, plane)
    flat = tokens.reshape(-1, tokens.shape[2])
    other = feed_forward(core_at, shift(flat, "core", 1), weights)
    total = feed_forward(core_at, flat, weights).astype(F32) + shift(other, "core", 1).astype(F32)
    total = lax.all_to_all(total.astype(BF).reshape(tokens.shape), plane, 0, 0, tiled=True)
    mlp_proj = jnp.sum(total.astype(F32), axis=0)
    return (mid_state.astype(F32) + rms_norm(mlp_proj, post_gain[1])).astype(BF)


def solution(mesh):
    fine = Mesh(mesh.devices.reshape(2, 4, 4, 2, 2), BLK + HEAD)
    placed = (
        P(BLK, None),
        P(None, None, HEAD),
        P(None, HEAD),
        P(HEAD, None),
        P(),
        P(None, None, BLK),
        P(BLK, None),
        P(BLK, None, HEAD),
        P(BLK, None, HEAD),
        P(),
        P(),
        P(),
        P(),
        P(),
    )
    return jax.shard_map(
        on_device, mesh=fine, in_specs=placed, out_specs=P(BLK + HEAD, None), check_vma=False
    )
```

```python
import functools

import jax
import jax.numpy as jnp
from jax import lax
from jax.experimental import pallas as pl
from jax.experimental.pallas import tpu as pltpu
from jax.sharding import Mesh, PartitionSpec as P

HD = 128
EPS = 1e-06
THETA = 500000.0
NEG = -1e30
LOG2E = 1.4426950408889634
BF = jnp.bfloat16
F32 = jnp.float32
BLK = ("yhi", "x", "z")
HEAD = ("ylo", "core")


def shift(values, axis, by):
    n = lax.axis_size(axis)
    return lax.ppermute(values, axis, [(i, (i + by) % n) for i in range(n)])


def spread(values, axes):
    n = 1
    for axis in (axes,) if isinstance(axes, str) else axes:
        n *= lax.axis_size(axis)
    copies = lax.optimization_barrier(jnp.broadcast_to(values, (n,) + values.shape))
    return lax.all_to_all(copies, axes, 0, 0, tiled=True)


def select_row(table, row):
    return lax.dynamic_index_in_dim(table, row, 0, keepdims=False)


def tree_info(leaf_segment, leaf_node, node_parent, node_length):
    groups, tok_rows = leaf_segment.shape
    leaf_count = leaf_node.shape[1]
    middles = node_parent.shape[0]
    all_nodes = node_length.shape[0]
    tenant_count = all_nodes - middles
    leaf_ids = jnp.arange(leaf_count, dtype=jnp.int32)
    onehot = (leaf_segment[:, :, None] == leaf_ids[None, None, :]).astype(jnp.int32)
    middle = jnp.sum(onehot * leaf_node[:, None, :], axis=-1)
    counts = jnp.sum(onehot, axis=1)
    starts = jnp.sum(jnp.where(leaf_ids[None, :] < leaf_ids[:, None], counts[:, None, :], 0), axis=-1)
    first_at = jnp.sum(onehot * starts[:, None, :], axis=-1)
    middle_ids = jnp.arange(middles, dtype=jnp.int32) + tenant_count
    root_node = jnp.sum(jnp.where(middle[..., None] == middle_ids, node_parent, 0), axis=-1)
    node_ids = jnp.arange(all_nodes, dtype=jnp.int32)
    len_middle = jnp.sum(jnp.where(middle[..., None] == node_ids, node_length, 0), axis=-1)
    len_root = jnp.sum(jnp.where(root_node[..., None] == node_ids, node_length, 0), axis=-1)
    offsets = jnp.arange(tok_rows, dtype=jnp.int32)[None, :] - first_at
    return middle, root_node, len_root + len_middle + offsets


def rms_norm(values_in, gain):
    return (
        values_in * lax.rsqrt(jnp.mean(values_in * values_in, axis=-1, keepdims=True) + EPS) * gain
    )


def attention_body(
    nodes_ref, lengths_ref, lists_ref, counts_ref,
    *rest,
):
    out_ref, qkv_ref, k_all, v_all, held, sems, qkv_sems = rest[-7:]
    qkv_parts = rest[:4]
    info_ref, seg_ref, factor_ref, key_factor_ref = rest[4:8]
    parts = rest[8:-7]
    step = pl.program_id(0)
    group = step // 2
    tile = step % 2
    half_rows = out_ref.shape[1]
    rows = 2 * half_rows
    node_rows = k_all.shape[1]
    per_part = parts[0].shape[0]
    batch = held.shape[2] // node_rows

    def copies():
        for i, part in enumerate(qkv_parts):
            yield pltpu.make_async_copy(part, qkv_ref.at[i], qkv_sems.at[i])
        for i, part in enumerate(parts):
            for j in range(per_part):
                yield pltpu.make_async_copy(
                    part.at[j, 0], k_all.at[i * per_part + j], sems.at[0, i, j]
                )
                yield pltpu.make_async_copy(
                    part.at[j, 1], v_all.at[i * per_part + j], sems.at[1, i, j]
                )

    @pl.when(step == 0)
    def _():
        for copy in copies():
            copy.start()
        for copy in copies():
            copy.wait()

    nt = (((1,), (1,)), ((), ()))
    count = counts_ref[group, tile]

    def work(first):
        q = qkv_ref[group, 0, first : first + half_rows, :]
        seen = first + half_rows
        middle = info_ref[0, first:seen, 0:1]
        root = info_ref[0, first:seen, 1:2]
        seg_col = info_ref[0, first:seen, 2:3]
        seg_row = seg_ref[0][:, :seen]
        row_at = lax.broadcasted_iota(jnp.int32, (half_rows, seen), 0) + first
        col_at = lax.broadcasted_iota(jnp.int32, (half_rows, seen), 1)
        key_at = lax.broadcasted_iota(jnp.int32, (1, node_rows), 1)
        scale = factor_ref[0, first:seen, 0:1] * (HD**-0.5 * LOG2E)
        near = lax.dot_general(q, qkv_ref[group, 1, :seen, :], nt, preferred_element_type=F32)
        near = near * scale * key_factor_ref[0][:, :seen]
        near = jnp.where((seg_col == seg_row) & (col_at <= row_at), near, NEG)
        top = jnp.max(near, axis=1, keepdims=True)

        def score(i, top):
            best = None
            for j in range(batch):
                slot = lists_ref[group, tile, i * batch + j]
                node = nodes_ref[slot]
                length = jnp.where(i * batch + j < count, lengths_ref[slot], 0)
                s = lax.dot_general(q, k_all[slot], nt, preferred_element_type=F32) * scale
                shown = ((middle == node) | (root == node)) & (key_at < length)
                s = jnp.where(shown, s, NEG)
                held[i, :, j * node_rows : (j + 1) * node_rows] = s
                best = s if best is None else jnp.maximum(best, s)
            return jnp.maximum(top, jnp.max(best, axis=1, keepdims=True))

        batches = (count + batch - 1) // batch
        top = lax.fori_loop(0, batches, score, top)
        weights = jnp.exp2(near - top)
        total = jnp.sum(weights, axis=1, keepdims=True)
        summed = jnp.dot(weights.astype(BF), qkv_ref[group, 2, :seen, :], preferred_element_type=F32)

        def gather(i, carry):
            total, summed = carry
            added = None
            for j in range(batch):
                slot = lists_ref[group, tile, i * batch + j]
                w = jnp.exp2(held[i, :, j * node_rows : (j + 1) * node_rows] - top)
                added = w if added is None else added + w
                summed = summed + jnp.dot(
                    w.astype(BF), v_all[slot], preferred_element_type=F32
                )
            return total + jnp.sum(added, axis=1, keepdims=True), summed

        total, summed = lax.fori_loop(0, batches, gather, (total, summed))
        out_ref[0] = (summed / total).astype(BF)

    for t in range(2):
        @pl.when(tile == t)
        def _(t=t):
            work(t * half_rows)


def attention(
    nodes, lengths, lists, counts, qkv_parts, row_info, seg_row, factors, key_factors, parts
):
    rows = qkv_parts[0].shape[1]
    groups = len(qkv_parts)
    per_part, _, node_rows, _ = parts[0].shape
    slots = nodes.shape[0]
    batch = 4
    one = lambda shape: pl.BlockSpec((1,) + shape, lambda i, *_: (i // 2,) + (0,) * len(shape))
    return pl.pallas_call(
        attention_body,
        out_shape=jax.ShapeDtypeStruct((groups, rows, HD), BF),
        grid_spec=pltpu.PrefetchScalarGridSpec(
            num_scalar_prefetch=4,
            grid=(groups * 2,),
            in_specs=[pl.BlockSpec(memory_space=pl.ANY)] * groups
            + [one((rows, 3)), one((1, rows)), one((rows, 2)), one((1, rows))]
            + [pl.BlockSpec(memory_space=pl.ANY)] * len(parts),
            out_specs=pl.BlockSpec((1, rows // 2, HD), lambda i, *_: (i // 2, i % 2, 0)),
            scratch_shapes=[
                pltpu.VMEM((groups, 4, rows, HD), BF),
                pltpu.VMEM((slots, node_rows, HD), BF),
                pltpu.VMEM((slots, node_rows, HD), BF),
                pltpu.VMEM((lists.shape[2] // batch, rows // 2, batch * node_rows), F32),
                pltpu.SemaphoreType.DMA((2, len(parts), per_part)),
                pltpu.SemaphoreType.DMA((groups,)),
            ],
        ),
        compiler_params=pltpu.CompilerParams(vmem_limit_bytes=32 << 20),
        cost_estimate=pl.CostEstimate(
            flops=2 * 10**9, transcendentals=4 * 10**6, bytes_accessed=6 * 10**6
        ),
    )(nodes, lengths, lists, counts, *qkv_parts, row_info, seg_row, factors, key_factors, *parts)


def feed_forward_body(tokens_ref, gu_a, dn_a, gu_b, dn_b, out_ref):
    rows = 256

    def one(i, carry):
        at = pl.ds(i * rows, rows)
        tokens = tokens_ref[at, :]
        part = 0.0
        for gu_ref, dn_ref in ((gu_a, dn_a), (gu_b, dn_b)):
            gate = jnp.dot(tokens, gu_ref[0], preferred_element_type=F32)
            up = jnp.dot(tokens, gu_ref[1], preferred_element_type=F32)
            hidden = (gate / (1.0 + jnp.exp(-gate)) * up).astype(BF)
            part = part + jnp.dot(hidden, dn_ref[...], preferred_element_type=F32)
        out_ref[at, :] = part.astype(BF)
        return carry

    lax.fori_loop(0, tokens_ref.shape[0] // rows, one, 0)


def feed_forward(tokens, weights):
    rows, width = tokens.shape
    units = weights[1].shape[0] * 2
    space = pl.BlockSpec(memory_space=pltpu.VMEM)
    return pl.pallas_call(
        feed_forward_body,
        out_shape=jax.ShapeDtypeStruct((rows, width), BF),
        in_specs=[space] * 5,
        out_specs=space,
        compiler_params=pltpu.CompilerParams(vmem_limit_bytes=48 << 20),
        cost_estimate=pl.CostEstimate(
            flops=2 * rows * width * units * 3,
            transcendentals=rows * units,
            bytes_accessed=(2 * rows * width + 3 * width * units) * 2,
        ),
    )(tokens, *weights)


def on_device(
    states_in,
    w_qkv,
    qk_gain,
    w_out,
    post_gain,
    w_gate_up,
    w_down,
    cache_keys,
    cache_values,
    slot_node,
    node_length,
    node_parent,
    leaf_segment,
    leaf_node,
):
    yhi, x_at, z_at, ylo, core = (lax.axis_index(a) for a in ("yhi", "x", "z", "ylo", "core"))
    n_y, n_x, n_z = (lax.axis_size(a) for a in BLK)
    blk = (yhi * n_x + x_at) * n_z + z_at
    head_index = ylo * 2 + core
    rows = states_in.shape[0]
    heads_here = w_qkv.shape[2] // HD
    columns = w_qkv.shape[2] * 4

    corner = ("yhi", "z", "core")

    def across(values, s):
        pairs = [
            ((y * n_z + z) * 2 + c, (c * n_z + (z + s) % n_z) * 2 + y)
            for y in range(n_y) for z in range(n_z) for c in range(2)
        ]
        return lax.ppermute(values, corner, pairs)

    def head_piece(s):
        cut = ((z_at + s) % n_z) * HD
        return jnp.stack(
            [lax.dynamic_slice_in_dim(c[0], cut, HD, 1) for c in (cache_keys, cache_values)]
        )

    cached = jnp.stack([across(head_piece(s), s) for s in range(n_z)])
    slot_from = jnp.stack(
        [
            (jnp.where(c == 0, core, 1 - core) * n_x + x) * n_z + (z_at - sz) % n_z
            for c in range(2) for x in range(n_x) for sz in range(n_z)
        ]
    ).astype(jnp.int32)

    w_out = lax.dynamic_slice_in_dim(jnp.concatenate([w_out, w_out]), z_at * HD, w_out.shape[0], 0)

    qkv_raw = jnp.einsum("td,cdw->ctw", states_in, w_qkv, preferred_element_type=F32)
    squares = jnp.sum(qkv_raw[:2] * qkv_raw[:2], axis=2)
    cached_own = spread(cached, "x").reshape((n_x * n_z,) + cached.shape[1:])
    group_from = jnp.stack(
        [blk] + [(core * n_x + x_at) * n_z + (z_at - g) % n_z for g in range(n_z)]
    ).astype(jnp.int32)
    segments = jnp.take(leaf_segment, group_from, axis=0)
    middle, root, position = tree_info(
        segments, jnp.take(leaf_node, group_from, axis=0), node_parent, node_length
    )
    position, middle, root, segments = position[0], middle[1:], root[1:], segments[1:]
    half = HD // 2
    frequency = THETA ** (-2.0 * jnp.arange(half, dtype=F32) / HD)
    angles = position.astype(F32)[:, None] * frequency[None, :]
    cosine, sine = jnp.cos(angles)[:, None, :], jnp.sin(angles)[:, None, :]

    def turned(c):
        scaled = (qkv_raw[c] * qk_gain[c]).reshape(rows, heads_here, HD)
        low, high = scaled[..., :half], scaled[..., half:]
        both = jnp.concatenate([low * cosine - high * sine, high * cosine + low * sine], axis=-1)
        return both.astype(BF)

    terms = []
    left = squares
    for _ in range(3):
        terms.append(lax.reduce_precision(left, 8, 7))
        left = left - terms[-1]
    terms = jnp.stack(terms).reshape(6, rows).astype(BF).T
    terms = jnp.pad(terms, ((0, 0), (0, HD - 6)))
    qkv = jnp.stack(
        [
            turned(0), turned(1), qkv_raw[2].astype(BF).reshape(rows, heads_here, HD),
            jnp.broadcast_to(terms[:, None], (rows, heads_here, HD)),
        ]
    ).transpose(2, 0, 1, 3)
    qkv_parts = [across(select_row(qkv, (z_at + s) % n_z), s) for s in range(n_z)]
    terms = jnp.stack([part[3, :, :6] for part in qkv_parts]).astype(F32)
    squares = jnp.sum(terms.reshape(n_z, rows, 3, 2), axis=2)
    factors = lax.rsqrt(lax.psum(squares, ("yhi", "ylo")) / columns + EPS)
    cached_own, factors = lax.optimization_barrier((cached_own, factors))
    cached_parts = [cached_own, shift(cached_own, "core", 1)]

    def beside(weights):
        return lax.ppermute(
            weights, ("z", "core"),
            [(z * 2 + c, (z + 1 - 2 * c) % n_z * 2 + c) for z in range(n_z) for c in range(2)],
        )

    def beyond(weights):
        far = lax.ppermute(
            weights, ("z", "core"), [(z * 2 + 1, (z + 2) % n_z * 2 + 1) for z in range(n_z)]
        )
        return jnp.where(core == 0, weights, far)

    w_gate_up, w_down, factors = lax.optimization_barrier((w_gate_up, w_down, factors))
    gu_a, dn_a = beside(w_gate_up), beside(w_down)

    slots = slot_from.shape[0]
    slot_nodes = jnp.take(slot_node, slot_from)
    slot_lengths = jnp.take(node_length, slot_nodes)
    halves = (n_z, 2, rows // 2, 1)
    needed = jnp.any(
        (middle.reshape(halves) == slot_nodes) | (root.reshape(halves) == slot_nodes), axis=2
    )
    before = jnp.arange(slots)[:, None] < jnp.arange(slots)[None, :]
    rank = jnp.sum(jnp.where(needed[..., :, None] & before, 1, 0), axis=2)
    longest = leaf_node.shape[1] + 4
    places = jnp.arange(longest, dtype=jnp.int32)
    lists = jnp.sum(
        jnp.where(
            needed[..., :, None] & (rank[..., :, None] == places),
            jnp.arange(slots, dtype=jnp.int32)[:, None], 0,
        ),
        axis=2,
    )
    counts = jnp.sum(needed.astype(jnp.int32), axis=2)
    row_info = jnp.stack([middle, root, segments], axis=-1)
    attended = attention(
        slot_nodes, slot_lengths, lists, counts, qkv_parts, row_info, segments[:, None, :],
        factors, factors[:, None, :, 1], cached_parts,
    )

    def back(values, s):
        pairs = [
            ((y * n_z + z) * 2 + c, (c * n_z + (z - s) % n_z) * 2 + y)
            for y in range(n_y) for z in range(n_z) for c in range(2)
        ]
        return lax.ppermute(values, corner, pairs)

    attended = jnp.concatenate([back(attended[s], s) for s in range(n_z)], axis=1)
    attended, gu_a, dn_a, w_gate_up, w_down = lax.optimization_barrier(
        (attended, gu_a, dn_a, w_gate_up, w_down)
    )
    gu_b, dn_b = beyond(w_gate_up), beyond(w_down)
    attn_part = jnp.dot(attended, w_out, preferred_element_type=F32)
    attn_part = attn_part.reshape(2, 2, rows // 4, -1)

    def of_core(c):
        return lax.dynamic_index_in_dim(attn_part, c, 1, keepdims=False)

    attn_part = of_core(core) + shift(of_core(1 - core).astype(BF), "core", 1).astype(F32)
    attn_proj = select_row(attn_part, ylo) + shift(
        select_row(attn_part, 1 - ylo).astype(BF), "ylo", 1
    ).astype(F32)
    own_rows = rows // 4
    state_rows = lax.dynamic_slice_in_dim(states_in, head_index * own_rows, own_rows, 0)
    mid_state = (state_rows.astype(F32) + rms_norm(attn_proj, post_gain[0])).astype(BF)

    plane = ("yhi", "x")
    weights = (gu_a, dn_a, gu_b, dn_b)
    tokens = spread(mid_state, plane)
    flat = tokens.reshape(-1, tokens.shape[2])
    other = feed_forward(shift(flat, "core", 1), weights)
    total = feed_forward(flat, weights).astype(F32) + shift(other, "core", 1).astype(F32)
    total = lax.all_to_all(total.astype(BF).reshape(tokens.shape), plane, 0, 0, tiled=True)
    mlp_proj = jnp.sum(total.astype(F32), axis=0)
    return (mid_state.astype(F32) + rms_norm(mlp_proj, post_gain[1])).astype(BF)


def solution(mesh):
    fine = Mesh(mesh.devices.reshape(2, 4, 4, 2, 2), BLK + HEAD)
    placed = (
        P(BLK, None),
        P(None, None, HEAD),
        P(None, HEAD),
        P(HEAD, None),
        P(),
        P(None, None, BLK),
        P(BLK, None),
        P(BLK, None, HEAD),
        P(BLK, None, HEAD),
        P(),
        P(),
        P(),
        P(),
        P(),
    )
    return jax.shard_map(
        on_device, mesh=fine, in_specs=placed, out_specs=P(BLK + HEAD, None), check_vma=False
    )
```

```python
import functools

import jax
import jax.numpy as jnp
from jax import lax
from jax.experimental import pallas as pl
from jax.experimental.pallas import tpu as pltpu
from jax.sharding import Mesh, PartitionSpec as P

HD = 128
EPS = 1e-06
THETA = 500000.0
NEG = -1e30
LOG2E = 1.4426950408889634
BF = jnp.bfloat16
F32 = jnp.float32
BLK = ("yhi", "x", "z")
HEAD = ("ylo", "core")


def shift(values, axis, by):
    n = lax.axis_size(axis)
    return lax.ppermute(values, axis, [(i, (i + by) % n) for i in range(n)])


def spread(values, axes):
    n = 1
    for axis in (axes,) if isinstance(axes, str) else axes:
        n *= lax.axis_size(axis)
    copies = lax.optimization_barrier(jnp.broadcast_to(values, (n,) + values.shape))
    return lax.all_to_all(copies, axes, 0, 0, tiled=True)


def select_row(table, row):
    return lax.dynamic_index_in_dim(table, row, 0, keepdims=False)


def tree_info(leaf_segment, leaf_node, node_parent, node_length):
    groups, tok_rows = leaf_segment.shape
    leaf_count = leaf_node.shape[1]
    middles = node_parent.shape[0]
    all_nodes = node_length.shape[0]
    tenant_count = all_nodes - middles
    leaf_ids = jnp.arange(leaf_count, dtype=jnp.int32)
    onehot = (leaf_segment[:, :, None] == leaf_ids[None, None, :]).astype(jnp.int32)
    middle = jnp.sum(onehot * leaf_node[:, None, :], axis=-1)
    counts = jnp.sum(onehot, axis=1)
    starts = jnp.sum(jnp.where(leaf_ids[None, :] < leaf_ids[:, None], counts[:, None, :], 0), axis=-1)
    first_at = jnp.sum(onehot * starts[:, None, :], axis=-1)
    middle_ids = jnp.arange(middles, dtype=jnp.int32) + tenant_count
    root_node = jnp.sum(jnp.where(middle[..., None] == middle_ids, node_parent, 0), axis=-1)
    node_ids = jnp.arange(all_nodes, dtype=jnp.int32)
    len_middle = jnp.sum(jnp.where(middle[..., None] == node_ids, node_length, 0), axis=-1)
    len_root = jnp.sum(jnp.where(root_node[..., None] == node_ids, node_length, 0), axis=-1)
    offsets = jnp.arange(tok_rows, dtype=jnp.int32)[None, :] - first_at
    return middle, root_node, len_root + len_middle + offsets


def rms_norm(values_in, gain):
    return (
        values_in * lax.rsqrt(jnp.mean(values_in * values_in, axis=-1, keepdims=True) + EPS) * gain
    )


def attention_body(
    nodes_ref, lengths_ref, lists_ref, counts_ref,
    *rest,
):
    out_ref, qkv_ref, k_all, v_all, held, sems, qkv_sems = rest[-7:]
    qkv_parts = rest[:4]
    info_ref, seg_ref, factor_ref, key_factor_ref = rest[4:8]
    parts = rest[8:-7]
    step = pl.program_id(0)
    group = step // 2
    tile = step % 2
    half_rows = out_ref.shape[1]
    rows = 2 * half_rows
    node_rows = k_all.shape[1]
    per_part = parts[0].shape[0]
    batch = held.shape[2] // node_rows

    def copies():
        for i, part in enumerate(qkv_parts):
            yield pltpu.make_async_copy(part, qkv_ref.at[i], qkv_sems.at[i])
        for i, part in enumerate(parts):
            for j in range(per_part):
                yield pltpu.make_async_copy(
                    part.at[j, 0], k_all.at[i * per_part + j], sems.at[0, i, j]
                )
                yield pltpu.make_async_copy(
                    part.at[j, 1], v_all.at[i * per_part + j], sems.at[1, i, j]
                )

    @pl.when(step == 0)
    def _():
        for copy in copies():
            copy.start()
        for copy in copies():
            copy.wait()

    nt = (((1,), (1,)), ((), ()))
    count = counts_ref[group, tile]

    def work(first):
        q = qkv_ref[group, first : first + half_rows, :]
        seen = first + half_rows
        middle = info_ref[0, first:seen, 0:1]
        root = info_ref[0, first:seen, 1:2]
        seg_col = info_ref[0, first:seen, 2:3]
        seg_row = seg_ref[0][:, :seen]
        row_at = lax.broadcasted_iota(jnp.int32, (half_rows, seen), 0) + first
        col_at = lax.broadcasted_iota(jnp.int32, (half_rows, seen), 1)
        key_at = lax.broadcasted_iota(jnp.int32, (1, node_rows), 1)
        scale = factor_ref[0, first:seen, 0:1] * (HD**-0.5 * LOG2E)
        near = lax.dot_general(q, qkv_ref[group, rows : rows + seen, :], nt, preferred_element_type=F32)
        near = near * scale * key_factor_ref[0][:, :seen]
        near = jnp.where((seg_col == seg_row) & (col_at <= row_at), near, NEG)
        top = jnp.max(near, axis=1, keepdims=True)

        def score(i, top):
            best = None
            for j in range(batch):
                slot = lists_ref[group, tile, i * batch + j]
                node = nodes_ref[slot]
                length = jnp.where(i * batch + j < count, lengths_ref[slot], 0)
                s = lax.dot_general(q, k_all[slot], nt, preferred_element_type=F32) * scale
                shown = ((middle == node) | (root == node)) & (key_at < length)
                s = jnp.where(shown, s, NEG)
                held[i, :, j * node_rows : (j + 1) * node_rows] = s
                best = s if best is None else jnp.maximum(best, s)
            return jnp.maximum(top, jnp.max(best, axis=1, keepdims=True))

        batches = (count + batch - 1) // batch
        top = lax.fori_loop(0, batches, score, top)
        weights = jnp.exp2(near - top)
        total = jnp.sum(weights, axis=1, keepdims=True)
        summed = jnp.dot(weights.astype(BF), qkv_ref[group, 2 * rows : 2 * rows + seen, :], preferred_element_type=F32)

        def gather(i, carry):
            total, summed = carry
            added = None
            for j in range(batch):
                slot = lists_ref[group, tile, i * batch + j]
                w = jnp.exp2(held[i, :, j * node_rows : (j + 1) * node_rows] - top)
                added = w if added is None else added + w
                summed = summed + jnp.dot(
                    w.astype(BF), v_all[slot], preferred_element_type=F32
                )
            return total + jnp.sum(added, axis=1, keepdims=True), summed

        total, summed = lax.fori_loop(0, batches, gather, (total, summed))
        out_ref[0] = (summed / total).astype(BF)

    for t in range(2):
        @pl.when(tile == t)
        def _(t=t):
            work(t * half_rows)


def attention(
    nodes, lengths, lists, counts, qkv_parts, row_info, seg_row, factors, key_factors, parts
):
    rows = row_info.shape[1]
    groups = len(qkv_parts)
    per_part, _, node_rows, _ = parts[0].shape
    slots = nodes.shape[0]
    batch = 4
    one = lambda shape: pl.BlockSpec((1,) + shape, lambda i, *_: (i // 2,) + (0,) * len(shape))
    return pl.pallas_call(
        attention_body,
        out_shape=jax.ShapeDtypeStruct((groups, rows, HD), BF),
        grid_spec=pltpu.PrefetchScalarGridSpec(
            num_scalar_prefetch=4,
            grid=(groups * 2,),
            in_specs=[pl.BlockSpec(memory_space=pl.ANY)] * groups
            + [one((rows, 3)), one((1, rows)), one((rows, 2)), one((1, rows))]
            + [pl.BlockSpec(memory_space=pl.ANY)] * len(parts),
            out_specs=pl.BlockSpec((1, rows // 2, HD), lambda i, *_: (i // 2, i % 2, 0)),
            scratch_shapes=[
                pltpu.VMEM((groups,) + qkv_parts[0].shape, BF),
                pltpu.VMEM((slots, node_rows, HD), BF),
                pltpu.VMEM((slots, node_rows, HD), BF),
                pltpu.VMEM((lists.shape[2] // batch, rows // 2, batch * node_rows), F32),
                pltpu.SemaphoreType.DMA((2, len(parts), per_part)),
                pltpu.SemaphoreType.DMA((groups,)),
            ],
        ),
        compiler_params=pltpu.CompilerParams(vmem_limit_bytes=32 << 20),
        cost_estimate=pl.CostEstimate(
            flops=2 * 10**9, transcendentals=4 * 10**6, bytes_accessed=6 * 10**6
        ),
    )(nodes, lengths, lists, counts, *qkv_parts, row_info, seg_row, factors, key_factors, *parts)


def feed_forward_body(tokens_ref, gu_a, dn_a, gu_b, dn_b, out_ref, tokens, gu, dn, made, sems):
    rows = 256
    blocks = tokens.shape[0] // rows

    def block(ref, i):
        return ref.at[pl.ds(i * rows, rows)]

    def fetch(i):
        return pltpu.make_async_copy(block(tokens_ref, i), block(tokens, i), sems.at[0, i])

    def store(i):
        return pltpu.make_async_copy(block(made, i), block(out_ref, i), sems.at[1, i])

    loads = [
        pltpu.make_async_copy(source, target, sems.at[2 + j, k])
        for k, pair in enumerate(((gu_a, dn_a), (gu_b, dn_b)))
        for j, (source, target) in enumerate(((pair[0], gu.at[k]), (pair[1], dn.at[k])))
    ]
    fetch(0).start()
    for load in loads:
        load.start()
    for i in range(1, blocks):
        fetch(i).start()
    for i in range(blocks):
        fetch(i).wait()
        part = 0.0
        for k in range(2):
            if i == 0:
                loads[2 * k].wait()
            values = tokens[i * rows : (i + 1) * rows, :]
            gate = jnp.dot(values, gu[k, 0], preferred_element_type=F32)
            up = jnp.dot(values, gu[k, 1], preferred_element_type=F32)
            hidden = (gate / (1.0 + jnp.exp(-gate)) * up).astype(BF)
            if i == 0:
                loads[2 * k + 1].wait()
            part = part + jnp.dot(hidden, dn[k], preferred_element_type=F32)
        made[i * rows : (i + 1) * rows, :] = part.astype(BF)
        store(i).start()
    for i in range(blocks):
        store(i).wait()


def feed_forward(tokens, weights):
    rows, width = tokens.shape
    units = weights[1].shape[0]
    return pl.pallas_call(
        feed_forward_body,
        out_shape=jax.ShapeDtypeStruct((rows, width), BF),
        in_specs=[pl.BlockSpec(memory_space=pl.ANY)] * 5,
        out_specs=pl.BlockSpec(memory_space=pl.ANY),
        scratch_shapes=[
            pltpu.VMEM((rows, width), BF),
            pltpu.VMEM((2, 2, width, units), BF),
            pltpu.VMEM((2, units, width), BF),
            pltpu.VMEM((rows, width), BF),
            pltpu.SemaphoreType.DMA((4, 2)),
        ],
        compiler_params=pltpu.CompilerParams(vmem_limit_bytes=48 << 20),
        cost_estimate=pl.CostEstimate(
            flops=2 * rows * width * units * 6,
            transcendentals=2 * rows * units,
            bytes_accessed=(2 * rows * width + 6 * width * units) * 2,
        ),
    )(tokens, *weights)


def on_device(
    states_in,
    w_qkv,
    qk_gain,
    w_out,
    post_gain,
    w_gate_up,
    w_down,
    cache_keys,
    cache_values,
    slot_node,
    node_length,
    node_parent,
    leaf_segment,
    leaf_node,
):
    yhi, x_at, z_at, ylo, core = (lax.axis_index(a) for a in ("yhi", "x", "z", "ylo", "core"))
    n_y, n_x, n_z = (lax.axis_size(a) for a in BLK)
    blk = (yhi * n_x + x_at) * n_z + z_at
    head_index = ylo * 2 + core
    rows = states_in.shape[0]
    heads_here = w_qkv.shape[2] // HD
    columns = w_qkv.shape[2] * 4

    corner = ("yhi", "z", "core")

    def across(values, s):
        pairs = [
            ((y * n_z + z) * 2 + c, (c * n_z + (z + s) % n_z) * 2 + y)
            for y in range(n_y) for z in range(n_z) for c in range(2)
        ]
        return lax.ppermute(values, corner, pairs)

    def head_piece(s):
        cut = ((z_at + s) % n_z) * HD
        return jnp.stack(
            [lax.dynamic_slice_in_dim(c[0], cut, HD, 1) for c in (cache_keys, cache_values)]
        )

    cached = jnp.stack([across(head_piece(s), s) for s in range(n_z)])
    slot_from = jnp.stack(
        [
            (jnp.where(c == 0, core, 1 - core) * n_x + x) * n_z + (z_at - sz) % n_z
            for c in range(2) for x in range(n_x) for sz in range(n_z)
        ]
    ).astype(jnp.int32)

    w_out = lax.dynamic_slice_in_dim(jnp.concatenate([w_out, w_out]), z_at * HD, w_out.shape[0], 0)

    def beside(weights):
        return lax.ppermute(
            weights, ("z", "core"),
            [(z * 2 + c, (z + 1 - 2 * c) % n_z * 2 + c) for z in range(n_z) for c in range(2)],
        )

    def beyond(weights):
        return lax.ppermute(
            weights, ("z", "core"), [(z * 2 + 1, (z + 2) % n_z * 2 + 1) for z in range(n_z)]
        )

    gu_a = beside(w_gate_up)

    qkv_raw = jnp.einsum("td,cdw->ctw", states_in, w_qkv, preferred_element_type=F32)
    squares = jnp.sum(qkv_raw[:2] * qkv_raw[:2], axis=2)
    cached_own = spread(cached, "x").reshape((n_x * n_z,) + cached.shape[1:])
    group_from = jnp.stack(
        [blk] + [(core * n_x + x_at) * n_z + (z_at - g) % n_z for g in range(n_z)]
    ).astype(jnp.int32)
    segments = jnp.take(leaf_segment, group_from, axis=0)
    middle, root, position = tree_info(
        segments, jnp.take(leaf_node, group_from, axis=0), node_parent, node_length
    )
    position, middle, root, segments = position[0], middle[1:], root[1:], segments[1:]
    half = HD // 2
    frequency = THETA ** (-2.0 * jnp.arange(half, dtype=F32) / HD)
    angles = position.astype(F32)[:, None] * frequency[None, :]
    cosine, sine = jnp.cos(angles)[:, None, :], jnp.sin(angles)[:, None, :]

    def turned(c):
        scaled = (qkv_raw[c] * qk_gain[c]).reshape(rows, heads_here, HD)
        low, high = scaled[..., :half], scaled[..., half:]
        both = jnp.concatenate([low * cosine - high * sine, high * cosine + low * sine], axis=-1)
        return both.astype(BF)

    terms = []
    left = squares
    for _ in range(3):
        terms.append(lax.reduce_precision(left, 8, 7))
        left = left - terms[-1]
    terms = jnp.stack(terms).reshape(-1, HD).astype(BF)
    term_rows = terms.shape[0]
    terms = jnp.pad(terms, ((0, -term_rows % 16), (0, 0)))
    qkv = jnp.stack(
        [turned(0), turned(1), qkv_raw[2].astype(BF).reshape(rows, heads_here, HD)]
    ).transpose(2, 0, 1, 3).reshape(heads_here, 3 * rows, HD)
    qkv = jnp.concatenate([qkv, jnp.broadcast_to(terms, (heads_here,) + terms.shape)], axis=1)
    qkv, gu_a = lax.optimization_barrier((qkv, gu_a))
    qkv_parts = [across(select_row(qkv, (z_at + s) % n_z), s) for s in range(n_z)]
    terms = jnp.stack([part[3 * rows : 3 * rows + term_rows] for part in qkv_parts]).astype(F32)
    squares = jnp.sum(terms.reshape(n_z, 3, 2, rows), axis=1).transpose(0, 2, 1)
    factors = lax.rsqrt(lax.psum(squares, ("yhi", "ylo")) / columns + EPS)
    w_gate_up, w_down, qkv_parts = lax.optimization_barrier((w_gate_up, w_down, qkv_parts))
    cached_own, qkv_parts = lax.optimization_barrier((cached_own, qkv_parts))
    cached_parts = [cached_own, shift(cached_own, "core", 1)]

    dn_a, gu_b, dn_b = beside(w_down), beyond(w_gate_up), beyond(w_down)

    slots = slot_from.shape[0]
    slot_nodes = jnp.take(slot_node, slot_from)
    slot_lengths = jnp.take(node_length, slot_nodes)
    halves = (n_z, 2, rows // 2, 1)
    needed = jnp.any(
        (middle.reshape(halves) == slot_nodes) | (root.reshape(halves) == slot_nodes), axis=2
    )
    before = jnp.arange(slots)[:, None] < jnp.arange(slots)[None, :]
    rank = jnp.sum(jnp.where(needed[..., :, None] & before, 1, 0), axis=2)
    longest = leaf_node.shape[1] + 4
    places = jnp.arange(longest, dtype=jnp.int32)
    lists = jnp.sum(
        jnp.where(
            needed[..., :, None] & (rank[..., :, None] == places),
            jnp.arange(slots, dtype=jnp.int32)[:, None], 0,
        ),
        axis=2,
    )
    counts = jnp.sum(needed.astype(jnp.int32), axis=2)
    row_info = jnp.stack([middle, root, segments], axis=-1)
    attended = attention(
        slot_nodes, slot_lengths, lists, counts, qkv_parts, row_info, segments[:, None, :],
        factors, factors[:, None, :, 1], cached_parts,
    )

    def back(values, s):
        pairs = [
            ((y * n_z + z) * 2 + c, (c * n_z + (z - s) % n_z) * 2 + y)
            for y in range(n_y) for z in range(n_z) for c in range(2)
        ]
        return lax.ppermute(values, corner, pairs)

    attended = jnp.concatenate([back(attended[s], s) for s in range(n_z)], axis=1)
    attended, dn_a, gu_b, dn_b = lax.optimization_barrier((attended, dn_a, gu_b, dn_b))
    attn_part = jnp.dot(attended, w_out, preferred_element_type=F32)
    attn_part = attn_part.reshape(2, 2, rows // 4, -1)

    def of_core(c):
        return lax.dynamic_index_in_dim(attn_part, c, 1, keepdims=False)

    attn_part = of_core(core) + shift(of_core(1 - core).astype(BF), "core", 1).astype(F32)
    attn_proj = select_row(attn_part, ylo) + shift(
        select_row(attn_part, 1 - ylo).astype(BF), "ylo", 1
    ).astype(F32)
    own_rows = rows // 4
    state_rows = lax.dynamic_slice_in_dim(states_in, head_index * own_rows, own_rows, 0)
    mid_state = (state_rows.astype(F32) + rms_norm(attn_proj, post_gain[0])).astype(BF)

    plane = ("yhi", "x")
    weights = (
        gu_a, dn_a, jnp.where(core == 0, w_gate_up, gu_b), jnp.where(core == 0, w_down, dn_b)
    )
    tokens = spread(mid_state, plane)
    flat = tokens.reshape(-1, tokens.shape[2])
    other = feed_forward(shift(flat, "core", 1), weights)
    total = feed_forward(flat, weights).astype(F32) + shift(other, "core", 1).astype(F32)
    total = lax.all_to_all(total.astype(BF).reshape(tokens.shape), plane, 0, 0, tiled=True)
    mlp_proj = jnp.sum(total.astype(F32), axis=0)
    return (mid_state.astype(F32) + rms_norm(mlp_proj, post_gain[1])).astype(BF)


def solution(mesh):
    fine = Mesh(mesh.devices.reshape(2, 4, 4, 2, 2), BLK + HEAD)
    placed = (
        P(BLK, None),
        P(None, None, HEAD),
        P(None, HEAD),
        P(HEAD, None),
        P(),
        P(None, None, BLK),
        P(BLK, None),
        P(BLK, None, HEAD),
        P(BLK, None, HEAD),
        P(),
        P(),
        P(),
        P(),
        P(),
    )
    return jax.shard_map(
        on_device, mesh=fine, in_specs=placed, out_specs=P(BLK + HEAD, None), check_vma=False
    )
```

```python
import functools

import jax
import jax.numpy as jnp
from jax import lax
from jax.experimental import pallas as pl
from jax.experimental.pallas import tpu as pltpu
from jax.sharding import Mesh, PartitionSpec as P

HD = 128
EPS = 1e-06
THETA = 500000.0
NEG = -1e30
LOG2E = 1.4426950408889634
BF = jnp.bfloat16
F32 = jnp.float32
BLK = ("yhi", "x", "z")
HEAD = ("ylo", "core")


def shift(values, axis, by):
    n = lax.axis_size(axis)
    return lax.ppermute(values, axis, [(i, (i + by) % n) for i in range(n)])


def spread(values, axes):
    n = 1
    for axis in (axes,) if isinstance(axes, str) else axes:
        n *= lax.axis_size(axis)
    copies = lax.optimization_barrier(jnp.broadcast_to(values, (n,) + values.shape))
    return lax.all_to_all(copies, axes, 0, 0, tiled=True)


def select_row(table, row):
    return lax.dynamic_index_in_dim(table, row, 0, keepdims=False)


def tree_info(leaf_segment, leaf_node, node_parent, node_length):
    groups, tok_rows = leaf_segment.shape
    leaf_count = leaf_node.shape[1]
    middles = node_parent.shape[0]
    all_nodes = node_length.shape[0]
    tenant_count = all_nodes - middles
    leaf_ids = jnp.arange(leaf_count, dtype=jnp.int32)
    onehot = (leaf_segment[:, :, None] == leaf_ids[None, None, :]).astype(jnp.int32)
    middle = jnp.sum(onehot * leaf_node[:, None, :], axis=-1)
    counts = jnp.sum(onehot, axis=1)
    starts = jnp.sum(jnp.where(leaf_ids[None, :] < leaf_ids[:, None], counts[:, None, :], 0), axis=-1)
    first_at = jnp.sum(onehot * starts[:, None, :], axis=-1)
    middle_ids = jnp.arange(middles, dtype=jnp.int32) + tenant_count
    root_node = jnp.sum(jnp.where(middle[..., None] == middle_ids, node_parent, 0), axis=-1)
    node_ids = jnp.arange(all_nodes, dtype=jnp.int32)
    len_middle = jnp.sum(jnp.where(middle[..., None] == node_ids, node_length, 0), axis=-1)
    len_root = jnp.sum(jnp.where(root_node[..., None] == node_ids, node_length, 0), axis=-1)
    offsets = jnp.arange(tok_rows, dtype=jnp.int32)[None, :] - first_at
    return middle, root_node, len_root + len_middle + offsets


def rms_norm(values_in, gain):
    return (
        values_in * lax.rsqrt(jnp.mean(values_in * values_in, axis=-1, keepdims=True) + EPS) * gain
    )


def attention_body(
    nodes_ref, lengths_ref, lists_ref, counts_ref,
    *rest,
):
    out_ref, qkv_ref, k_all, v_all, held, sems, qkv_sems = rest[-7:]
    qkv_parts = rest[:4]
    info_ref, seg_ref, factor_ref, key_factor_ref = rest[4:8]
    parts = rest[8:-7]
    step = pl.program_id(0)
    group = step // 2
    tile = step % 2
    half_rows = out_ref.shape[1]
    rows = 2 * half_rows
    node_rows = k_all.shape[1]
    per_part = parts[0].shape[0]
    batch = held.shape[2] // node_rows

    def copies():
        for i, part in enumerate(qkv_parts):
            yield pltpu.make_async_copy(part, qkv_ref.at[i], qkv_sems.at[i])
        for i, part in enumerate(parts):
            for j in range(per_part):
                yield pltpu.make_async_copy(
                    part.at[j, 0], k_all.at[i * per_part + j], sems.at[0, i, j]
                )
                yield pltpu.make_async_copy(
                    part.at[j, 1], v_all.at[i * per_part + j], sems.at[1, i, j]
                )

    @pl.when(step == 0)
    def _():
        for copy in copies():
            copy.start()
        for copy in copies():
            copy.wait()

    nt = (((1,), (1,)), ((), ()))
    count = counts_ref[group, tile]

    def work(first):
        q = qkv_ref[group, first : first + half_rows, :]
        seen = first + half_rows
        middle = info_ref[0, first:seen, 0:1]
        root = info_ref[0, first:seen, 1:2]
        seg_col = info_ref[0, first:seen, 2:3]
        seg_row = seg_ref[0][:, :seen]
        row_at = lax.broadcasted_iota(jnp.int32, (half_rows, seen), 0) + first
        col_at = lax.broadcasted_iota(jnp.int32, (half_rows, seen), 1)
        key_at = lax.broadcasted_iota(jnp.int32, (1, node_rows), 1)
        scale = factor_ref[0, first:seen, 0:1] * (HD**-0.5 * LOG2E)
        near = lax.dot_general(q, qkv_ref[group, rows : rows + seen, :], nt, preferred_element_type=F32)
        near = near * scale * key_factor_ref[0][:, :seen]
        near = jnp.where((seg_col == seg_row) & (col_at <= row_at), near, NEG)
        top = jnp.max(near, axis=1, keepdims=True)

        def score(i, top):
            best = None
            for j in range(batch):
                slot = lists_ref[group, tile, i * batch + j]
                node = nodes_ref[slot]
                length = jnp.where(i * batch + j < count, lengths_ref[slot], 0)
                s = lax.dot_general(q, k_all[slot], nt, preferred_element_type=F32) * scale
                shown = ((middle == node) | (root == node)) & (key_at < length)
                s = jnp.where(shown, s, NEG)
                held[i, :, j * node_rows : (j + 1) * node_rows] = s
                best = s if best is None else jnp.maximum(best, s)
            return jnp.maximum(top, jnp.max(best, axis=1, keepdims=True))

        batches = (count + batch - 1) // batch
        top = lax.fori_loop(0, batches, score, top)
        weights = jnp.exp2(near - top)
        total = jnp.sum(weights, axis=1, keepdims=True)
        summed = jnp.dot(weights.astype(BF), qkv_ref[group, 2 * rows : 2 * rows + seen, :], preferred_element_type=F32)

        def gather(i, carry):
            total, summed = carry
            added = None
            for j in range(batch):
                slot = lists_ref[group, tile, i * batch + j]
                w = jnp.exp2(held[i, :, j * node_rows : (j + 1) * node_rows] - top)
                added = w if added is None else added + w
                summed = summed + jnp.dot(
                    w.astype(BF), v_all[slot], preferred_element_type=F32
                )
            return total + jnp.sum(added, axis=1, keepdims=True), summed

        total, summed = lax.fori_loop(0, batches, gather, (total, summed))
        out_ref[0] = (summed / total).astype(BF)

    for t in range(2):
        @pl.when(tile == t)
        def _(t=t):
            work(t * half_rows)


def attention(
    nodes, lengths, lists, counts, qkv_parts, row_info, seg_row, factors, key_factors, parts
):
    rows = row_info.shape[1]
    groups = len(qkv_parts)
    per_part, _, node_rows, _ = parts[0].shape
    slots = nodes.shape[0]
    batch = 4
    one = lambda shape: pl.BlockSpec((1,) + shape, lambda i, *_: (i // 2,) + (0,) * len(shape))
    return pl.pallas_call(
        attention_body,
        out_shape=jax.ShapeDtypeStruct((groups, rows, HD), BF),
        grid_spec=pltpu.PrefetchScalarGridSpec(
            num_scalar_prefetch=4,
            grid=(groups * 2,),
            in_specs=[pl.BlockSpec(memory_space=pl.ANY)] * groups
            + [one((rows, 3)), one((1, rows)), one((rows, 2)), one((1, rows))]
            + [pl.BlockSpec(memory_space=pl.ANY)] * len(parts),
            out_specs=pl.BlockSpec((1, rows // 2, HD), lambda i, *_: (i // 2, i % 2, 0)),
            scratch_shapes=[
                pltpu.VMEM((groups,) + qkv_parts[0].shape, BF),
                pltpu.VMEM((slots, node_rows, HD), BF),
                pltpu.VMEM((slots, node_rows, HD), BF),
                pltpu.VMEM((lists.shape[2] // batch, rows // 2, batch * node_rows), F32),
                pltpu.SemaphoreType.DMA((2, len(parts), per_part)),
                pltpu.SemaphoreType.DMA((groups,)),
            ],
        ),
        compiler_params=pltpu.CompilerParams(vmem_limit_bytes=32 << 20),
        cost_estimate=pl.CostEstimate(
            flops=2 * 10**9, transcendentals=4 * 10**6, bytes_accessed=6 * 10**6
        ),
    )(nodes, lengths, lists, counts, *qkv_parts, row_info, seg_row, factors, key_factors, *parts)


def feed_forward_body(
    tokens_ref, gu_a, dn_a, gate_b, up_b, dn_b, out_ref, tokens, gu, dn, made, sems
):
    rows, width = tokens.shape
    units = dn.shape[0] // 2
    blocks = 2

    def fetch():
        return pltpu.make_async_copy(tokens_ref, tokens, sems.at[0])

    gu_loads, dn_loads = [], []
    pairs = ((gu_a.at[0], gu_a.at[1]), (gate_b, up_b))
    for k, (pair, dn_ref) in enumerate(zip(pairs, (dn_a, dn_b))):
        for j in range(2):
            gu_loads.append(
                pltpu.make_async_copy(
                    pair[j],
                    gu.at[:, pl.ds((2 * k + j) * units, units)],
                    sems.at[1 + 2 * k + j],
                )
            )
        dn_loads.append(
            pltpu.make_async_copy(dn_ref, dn.at[pl.ds(k * units, units)], sems.at[5 + k])
        )

    def store(i):
        part = pl.ds(i * (width // blocks), width // blocks)
        return pltpu.make_async_copy(made.at[:, part], out_ref.at[:, part], sems.at[7 + i])

    fetch().start()
    for load in gu_loads + dn_loads:
        load.start()
    fetch().wait()
    hidden = []
    for k in range(2):
        for load in gu_loads[2 * k : 2 * k + 2]:
            load.wait()
        both = jnp.dot(
            tokens[...], gu[:, 2 * k * units : (2 * k + 2) * units], preferred_element_type=F32
        )
        gate, up = both[:, :units], both[:, units:]
        hidden.append((gate / (1.0 + jnp.exp(-gate)) * up).astype(BF))
    hidden = jnp.concatenate(hidden, axis=1)
    for load in dn_loads:
        load.wait()
    for i in range(blocks):
        part = slice(i * (width // blocks), (i + 1) * (width // blocks))
        made[:, part] = jnp.dot(hidden, dn[:, part], preferred_element_type=F32).astype(BF)
        store(i).start()
    for i in range(blocks):
        store(i).wait()


def feed_forward(tokens, weights):
    rows, width = tokens.shape
    units = weights[1].shape[0]
    return pl.pallas_call(
        feed_forward_body,
        out_shape=jax.ShapeDtypeStruct((rows, width), BF),
        in_specs=[pl.BlockSpec(memory_space=pl.ANY)] * 6,
        out_specs=pl.BlockSpec(memory_space=pl.ANY),
        scratch_shapes=[
            pltpu.VMEM((rows, width), BF),
            pltpu.VMEM((width, 4 * units), BF),
            pltpu.VMEM((2 * units, width), BF),
            pltpu.VMEM((rows, width), BF),
            pltpu.SemaphoreType.DMA((9,)),
        ],
        compiler_params=pltpu.CompilerParams(vmem_limit_bytes=48 << 20),
        cost_estimate=pl.CostEstimate(
            flops=2 * rows * width * units * 6,
            transcendentals=2 * rows * units,
            bytes_accessed=(2 * rows * width + 6 * width * units) * 2,
        ),
    )(tokens, *weights)


def on_device(
    states_in,
    w_qkv,
    qk_gain,
    w_out,
    post_gain,
    w_gate_up,
    w_down,
    cache_keys,
    cache_values,
    slot_node,
    node_length,
    node_parent,
    leaf_segment,
    leaf_node,
):
    yhi, x_at, z_at, ylo, core = (lax.axis_index(a) for a in ("yhi", "x", "z", "ylo", "core"))
    n_y, n_x, n_z = (lax.axis_size(a) for a in BLK)
    blk = (yhi * n_x + x_at) * n_z + z_at
    head_index = ylo * 2 + core
    rows = states_in.shape[0]
    heads_here = w_qkv.shape[2] // HD
    columns = w_qkv.shape[2] * 4

    corner = ("yhi", "z", "core")

    def across(values, s):
        pairs = [
            ((y * n_z + z) * 2 + c, (c * n_z + (z + s) % n_z) * 2 + y)
            for y in range(n_y) for z in range(n_z) for c in range(2)
        ]
        return lax.ppermute(values, corner, pairs)

    def head_piece(s):
        cut = ((z_at + s) % n_z) * HD
        return jnp.stack(
            [lax.dynamic_slice_in_dim(c[0], cut, HD, 1) for c in (cache_keys, cache_values)]
        )

    cached = jnp.stack([across(head_piece(s), s) for s in range(n_z)])
    slot_from = jnp.stack(
        [
            (jnp.where(c == 0, core, 1 - core) * n_x + x) * n_z + (z_at - sz) % n_z
            for c in range(2) for x in range(n_x) for sz in range(n_z)
        ]
    ).astype(jnp.int32)

    w_out = lax.dynamic_slice_in_dim(jnp.concatenate([w_out, w_out]), z_at * HD, w_out.shape[0], 0)

    def beside(weights):
        return lax.ppermute(
            weights, ("z", "core"),
            [(z * 2 + c, (z + 1 - 2 * c) % n_z * 2 + c) for z in range(n_z) for c in range(2)],
        )

    def beyond(weights):
        return lax.ppermute(
            weights, ("z", "core"), [(z * 2 + 1, (z + 2) % n_z * 2 + 1) for z in range(n_z)]
        )

    qkv_raw = jnp.einsum("td,cdw->ctw", states_in, w_qkv, preferred_element_type=F32)
    squares = jnp.sum(qkv_raw[:2] * qkv_raw[:2], axis=2)
    for axis in ("core", "ylo"):
        squares = squares + shift(squares, axis, 1)
    cached_own = spread(cached, "x").reshape((n_x * n_z,) + cached.shape[1:])
    def own_group(table):
        return lax.dynamic_slice_in_dim(table, blk, 1, 0)

    position = tree_info(
        own_group(leaf_segment), own_group(leaf_node), node_parent, node_length
    )[2][0]
    half = HD // 2
    frequency = THETA ** (-2.0 * jnp.arange(half, dtype=F32) / HD)
    angles = position.astype(F32)[:, None] * frequency[None, :]
    cosine, sine = jnp.cos(angles)[:, None, :], jnp.sin(angles)[:, None, :]

    def turned(c):
        scaled = (qkv_raw[c] * qk_gain[c]).reshape(rows, heads_here, HD)
        low, high = scaled[..., :half], scaled[..., half:]
        both = jnp.concatenate([low * cosine - high * sine, high * cosine + low * sine], axis=-1)
        return both.astype(BF)

    terms = []
    left = squares
    for _ in range(3):
        terms.append(lax.reduce_precision(left, 8, 7))
        left = left - terms[-1]
    terms = jnp.stack(terms).reshape(-1, HD).astype(BF)
    term_rows = terms.shape[0]
    terms = jnp.pad(terms, ((0, -term_rows % 16), (0, 0)))
    qkv = jnp.stack(
        [turned(0), turned(1), qkv_raw[2].astype(BF).reshape(rows, heads_here, HD)]
    ).transpose(2, 0, 1, 3).reshape(heads_here, 3 * rows, HD)
    qkv = jnp.concatenate([qkv, jnp.broadcast_to(terms, (heads_here,) + terms.shape)], axis=1)
    qkv, slot_node, node_length, node_parent, leaf_segment, leaf_node = (
        lax.optimization_barrier(
            (qkv, slot_node, node_length, node_parent, leaf_segment, leaf_node)
        )
    )
    qkv_parts = [across(select_row(qkv, (z_at + s) % n_z), s) for s in range(n_z)]

    group_from = jnp.stack(
        [(core * n_x + x_at) * n_z + (z_at - g) % n_z for g in range(n_z)]
    ).astype(jnp.int32)
    segments = jnp.take(leaf_segment, group_from, axis=0)
    middle, root, _ = tree_info(
        segments, jnp.take(leaf_node, group_from, axis=0), node_parent, node_length
    )
    slots = slot_from.shape[0]
    slot_nodes = jnp.take(slot_node, slot_from)
    slot_lengths = jnp.take(node_length, slot_nodes)
    halves = (n_z, 2, rows // 2, 1)
    needed = jnp.any(
        (middle.reshape(halves) == slot_nodes) | (root.reshape(halves) == slot_nodes), axis=2
    )
    before = jnp.arange(slots)[:, None] < jnp.arange(slots)[None, :]
    rank = jnp.sum(jnp.where(needed[..., :, None] & before, 1, 0), axis=2)
    longest = leaf_node.shape[1] + 4
    places = jnp.arange(longest, dtype=jnp.int32)
    lists = jnp.sum(
        jnp.where(
            needed[..., :, None] & (rank[..., :, None] == places),
            jnp.arange(slots, dtype=jnp.int32)[:, None], 0,
        ),
        axis=2,
    )
    counts = jnp.sum(needed.astype(jnp.int32), axis=2)
    row_info = jnp.stack([middle, root, segments], axis=-1)

    terms = jnp.stack([part[3 * rows : 3 * rows + term_rows] for part in qkv_parts]).astype(F32)
    squares = jnp.sum(terms.reshape(n_z, 3, 2, rows), axis=1).transpose(0, 2, 1)
    factors = lax.rsqrt(squares / columns + EPS)
    w_gate_up, w_down, qkv_parts = lax.optimization_barrier((w_gate_up, w_down, qkv_parts))
    cached_own, qkv_parts, slot_nodes, slot_lengths, lists, counts, row_info, factors = (
        lax.optimization_barrier(
            (cached_own, qkv_parts, slot_nodes, slot_lengths, lists, counts, row_info, factors)
        )
    )
    cached_parts = [cached_own, shift(cached_own, "core", 1)]

    gu_a = beside(w_gate_up)

    attended = attention(
        slot_nodes, slot_lengths, lists, counts, qkv_parts, row_info, segments[:, None, :],
        factors, factors[:, None, :, 1], cached_parts,
    )

    attended, gu_a, w_gate_up, w_down = lax.optimization_barrier(
        (attended, gu_a, w_gate_up, w_down)
    )
    gate_b = beyond(w_gate_up[0])

    def back(values, s):
        pairs = [
            ((y * n_z + z) * 2 + c, (c * n_z + (z - s) % n_z) * 2 + y)
            for y in range(n_y) for z in range(n_z) for c in range(2)
        ]
        return lax.ppermute(values, corner, pairs)

    attended = jnp.concatenate([back(attended[s], s) for s in range(n_z)], axis=1)
    attn_part = jnp.dot(attended, w_out, preferred_element_type=F32)
    attn_part = attn_part.reshape(2, 2, rows // 4, -1)

    def of_core(c):
        return lax.dynamic_index_in_dim(attn_part, c, 1, keepdims=False)

    attn_part = of_core(core) + shift(of_core(1 - core).astype(BF), "core", 1).astype(F32)
    attn_proj = select_row(attn_part, ylo) + shift(
        select_row(attn_part, 1 - ylo).astype(BF), "ylo", 1
    ).astype(F32)
    own_rows = rows // 4
    state_rows = lax.dynamic_slice_in_dim(states_in, head_index * own_rows, own_rows, 0)
    mid_state = (state_rows.astype(F32) + rms_norm(attn_proj, post_gain[0])).astype(BF)

    plane = ("yhi", "x")
    mid_state, gate_b, w_gate_up, w_down = lax.optimization_barrier(
        (mid_state, gate_b, w_gate_up, w_down)
    )
    up_b, dn_a, dn_b = beyond(w_gate_up[1]), beside(w_down), beyond(w_down)
    tokens = spread(mid_state, plane)
    tokens, up_b, dn_a, dn_b = lax.optimization_barrier((tokens, up_b, dn_a, dn_b))

    def second(own, far):
        return jnp.where(core == 0, own, far)

    weights = (
        gu_a, dn_a, second(w_gate_up[0], gate_b), second(w_gate_up[1], up_b), second(w_down, dn_b)
    )
    flat = tokens.reshape(-1, tokens.shape[2])
    other = feed_forward(shift(flat, "core", 1), weights)
    total = feed_forward(flat, weights).astype(F32) + shift(other, "core", 1).astype(F32)
    total = lax.all_to_all(total.astype(BF).reshape(tokens.shape), plane, 0, 0, tiled=True)
    mlp_proj = jnp.sum(total.astype(F32), axis=0)
    return (mid_state.astype(F32) + rms_norm(mlp_proj, post_gain[1])).astype(BF)


def solution(mesh):
    fine = Mesh(mesh.devices.reshape(2, 4, 4, 2, 2), BLK + HEAD)
    placed = (
        P(BLK, None),
        P(None, None, HEAD),
        P(None, HEAD),
        P(HEAD, None),
        P(),
        P(None, None, BLK),
        P(BLK, None),
        P(BLK, None, HEAD),
        P(BLK, None, HEAD),
        P(),
        P(),
        P(),
        P(),
        P(),
    )
    return jax.shard_map(
        on_device, mesh=fine, in_specs=placed, out_specs=P(BLK + HEAD, None), check_vma=False
    )
```

```python
import functools

import jax
import jax.numpy as jnp
from jax import lax
from jax.experimental import pallas as pl
from jax.experimental.pallas import tpu as pltpu
from jax.sharding import Mesh, PartitionSpec as P

HD = 128
EPS = 1e-06
THETA = 500000.0
NEG = -1e30
LOG2E = 1.4426950408889634
BF = jnp.bfloat16
F32 = jnp.float32
BLK = ("yhi", "x", "z")
HEAD = ("ylo", "core")


def shift(values, axis, by):
    n = lax.axis_size(axis)
    return lax.ppermute(values, axis, [(i, (i + by) % n) for i in range(n)])


def spread(values, axes):
    n = 1
    for axis in (axes,) if isinstance(axes, str) else axes:
        n *= lax.axis_size(axis)
    copies = lax.optimization_barrier(jnp.broadcast_to(values, (n,) + values.shape))
    return lax.all_to_all(copies, axes, 0, 0, tiled=True)


def select_row(table, row):
    return lax.dynamic_index_in_dim(table, row, 0, keepdims=False)


def tree_info(leaf_segment, leaf_node, node_parent, node_length):
    groups, tok_rows = leaf_segment.shape
    leaf_count = leaf_node.shape[1]
    middles = node_parent.shape[0]
    all_nodes = node_length.shape[0]
    tenant_count = all_nodes - middles
    leaf_ids = jnp.arange(leaf_count, dtype=jnp.int32)
    onehot = (leaf_segment[:, :, None] == leaf_ids[None, None, :]).astype(jnp.int32)
    middle = jnp.sum(onehot * leaf_node[:, None, :], axis=-1)
    counts = jnp.sum(onehot, axis=1)
    starts = jnp.sum(jnp.where(leaf_ids[None, :] < leaf_ids[:, None], counts[:, None, :], 0), axis=-1)
    first_at = jnp.sum(onehot * starts[:, None, :], axis=-1)
    middle_ids = jnp.arange(middles, dtype=jnp.int32) + tenant_count
    root_node = jnp.sum(jnp.where(middle[..., None] == middle_ids, node_parent, 0), axis=-1)
    node_ids = jnp.arange(all_nodes, dtype=jnp.int32)
    len_middle = jnp.sum(jnp.where(middle[..., None] == node_ids, node_length, 0), axis=-1)
    len_root = jnp.sum(jnp.where(root_node[..., None] == node_ids, node_length, 0), axis=-1)
    offsets = jnp.arange(tok_rows, dtype=jnp.int32)[None, :] - first_at
    return middle, root_node, len_root + len_middle + offsets


def rms_norm(values_in, gain):
    return (
        values_in * lax.rsqrt(jnp.mean(values_in * values_in, axis=-1, keepdims=True) + EPS) * gain
    )


def attention_body(
    nodes_ref, lengths_ref, lists_ref, counts_ref,
    *rest,
):
    out_ref, qkv_ref, k_all, v_all, held, sems, qkv_sems = rest[-7:]
    qkv_parts = rest[:4]
    info_ref, seg_ref, factor_ref, key_factor_ref = rest[4:8]
    parts = rest[8:-7]
    step = pl.program_id(0)
    group = step // 2
    tile = step % 2
    half_rows = out_ref.shape[1]
    rows = 2 * half_rows
    node_rows = k_all.shape[1]
    per_part = parts[0].shape[0]
    batch = held.shape[2] // node_rows

    def copies():
        for i, part in enumerate(qkv_parts):
            yield pltpu.make_async_copy(part, qkv_ref.at[i], qkv_sems.at[i])
        for i, part in enumerate(parts):
            for j in range(per_part):
                yield pltpu.make_async_copy(
                    part.at[j, 0], k_all.at[i * per_part + j], sems.at[0, i, j]
                )
                yield pltpu.make_async_copy(
                    part.at[j, 1], v_all.at[i * per_part + j], sems.at[1, i, j]
                )

    @pl.when(step == 0)
    def _():
        for copy in copies():
            copy.start()
        for copy in copies():
            copy.wait()

    nt = (((1,), (1,)), ((), ()))
    count = counts_ref[group, tile]

    def work(first):
        q = qkv_ref[group, first : first + half_rows, :]
        seen = first + half_rows
        middle = info_ref[0, first:seen, 0:1]
        root = info_ref[0, first:seen, 1:2]
        seg_col = info_ref[0, first:seen, 2:3]
        seg_row = seg_ref[0][:, :seen]
        row_at = lax.broadcasted_iota(jnp.int32, (half_rows, seen), 0) + first
        col_at = lax.broadcasted_iota(jnp.int32, (half_rows, seen), 1)
        key_at = lax.broadcasted_iota(jnp.int32, (1, node_rows), 1)
        scale = factor_ref[0, first:seen, 0:1] * (HD**-0.5 * LOG2E)
        near = lax.dot_general(q, qkv_ref[group, rows : rows + seen, :], nt, preferred_element_type=F32)
        near = near * scale * key_factor_ref[0][:, :seen]
        near = jnp.where((seg_col == seg_row) & (col_at <= row_at), near, NEG)
        top = jnp.max(near, axis=1, keepdims=True)

        def score(i, top):
            best = None
            for j in range(batch):
                slot = lists_ref[group, tile, i * batch + j]
                node = nodes_ref[slot]
                length = jnp.where(i * batch + j < count, lengths_ref[slot], 0)
                s = lax.dot_general(q, k_all[slot], nt, preferred_element_type=F32) * scale
                shown = ((middle == node) | (root == node)) & (key_at < length)
                s = jnp.where(shown, s, NEG)
                held[i, :, j * node_rows : (j + 1) * node_rows] = s
                best = s if best is None else jnp.maximum(best, s)
            return jnp.maximum(top, jnp.max(best, axis=1, keepdims=True))

        batches = (count + batch - 1) // batch
        top = lax.fori_loop(0, batches, score, top)
        weights = jnp.exp2(near - top)
        total = jnp.sum(weights, axis=1, keepdims=True)
        summed = jnp.dot(weights.astype(BF), qkv_ref[group, 2 * rows : 2 * rows + seen, :], preferred_element_type=F32)

        def gather(i, carry):
            total, summed = carry
            added = None
            for j in range(batch):
                slot = lists_ref[group, tile, i * batch + j]
                w = jnp.exp2(held[i, :, j * node_rows : (j + 1) * node_rows] - top)
                added = w if added is None else added + w
                summed = summed + jnp.dot(
                    w.astype(BF), v_all[slot], preferred_element_type=F32
                )
            return total + jnp.sum(added, axis=1, keepdims=True), summed

        total, summed = lax.fori_loop(0, batches, gather, (total, summed))
        out_ref[0] = (summed / total).astype(BF)

    for t in range(2):
        @pl.when(tile == t)
        def _(t=t):
            work(t * half_rows)


def attention(
    nodes, lengths, lists, counts, qkv_parts, row_info, seg_row, factors, key_factors, parts
):
    rows = row_info.shape[1]
    groups = len(qkv_parts)
    per_part, _, node_rows, _ = parts[0].shape
    slots = nodes.shape[0]
    batch = 4
    one = lambda shape: pl.BlockSpec((1,) + shape, lambda i, *_: (i // 2,) + (0,) * len(shape))
    return pl.pallas_call(
        attention_body,
        out_shape=jax.ShapeDtypeStruct((groups, rows, HD), BF),
        grid_spec=pltpu.PrefetchScalarGridSpec(
            num_scalar_prefetch=4,
            grid=(groups * 2,),
            in_specs=[pl.BlockSpec(memory_space=pl.ANY)] * groups
            + [one((rows, 3)), one((1, rows)), one((rows, 2)), one((1, rows))]
            + [pl.BlockSpec(memory_space=pl.ANY)] * len(parts),
            out_specs=pl.BlockSpec((1, rows // 2, HD), lambda i, *_: (i // 2, i % 2, 0)),
            scratch_shapes=[
                pltpu.VMEM((groups,) + qkv_parts[0].shape, BF),
                pltpu.VMEM((slots, node_rows, HD), BF),
                pltpu.VMEM((slots, node_rows, HD), BF),
                pltpu.VMEM((lists.shape[2] // batch, rows // 2, batch * node_rows), F32),
                pltpu.SemaphoreType.DMA((2, len(parts), per_part)),
                pltpu.SemaphoreType.DMA((groups,)),
            ],
        ),
        compiler_params=pltpu.CompilerParams(vmem_limit_bytes=32 << 20),
        cost_estimate=pl.CostEstimate(
            flops=2 * 10**9, transcendentals=4 * 10**6, bytes_accessed=6 * 10**6
        ),
    )(nodes, lengths, lists, counts, *qkv_parts, row_info, seg_row, factors, key_factors, *parts)


def feed_forward_body(tokens_ref, gu_a, dn_a, gu_b, dn_b, out_ref, tokens, gu, dn, made, sems):
    rows = 256
    blocks = tokens.shape[0] // rows

    def block(ref, i):
        return ref.at[pl.ds(i * rows, rows)]

    def fetch(i):
        return pltpu.make_async_copy(block(tokens_ref, i), block(tokens, i), sems.at[0, i])

    def store(i):
        return pltpu.make_async_copy(block(made, i), block(out_ref, i), sems.at[1, i])

    loads = [
        pltpu.make_async_copy(source, target, sems.at[2 + j, k])
        for k, pair in enumerate(((gu_a, dn_a), (gu_b, dn_b)))
        for j, (source, target) in enumerate(((pair[0], gu.at[k]), (pair[1], dn.at[k])))
    ]
    fetch(0).start()
    for load in loads:
        load.start()
    for i in range(1, blocks):
        fetch(i).start()
    for i in range(blocks):
        fetch(i).wait()
        part = 0.0
        for k in range(2):
            if i == 0:
                loads[2 * k].wait()
            values = tokens[i * rows : (i + 1) * rows, :]
            gate = jnp.dot(values, gu[k, 0], preferred_element_type=F32)
            up = jnp.dot(values, gu[k, 1], preferred_element_type=F32)
            hidden = (gate / (1.0 + jnp.exp(-gate)) * up).astype(BF)
            if i == 0:
                loads[2 * k + 1].wait()
            part = part + jnp.dot(hidden, dn[k], preferred_element_type=F32)
        made[i * rows : (i + 1) * rows, :] = part.astype(BF)
        store(i).start()
    for i in range(blocks):
        store(i).wait()


def feed_forward(tokens, weights):
    rows, width = tokens.shape
    units = weights[1].shape[0]
    return pl.pallas_call(
        feed_forward_body,
        out_shape=jax.ShapeDtypeStruct((rows, width), BF),
        in_specs=[pl.BlockSpec(memory_space=pl.ANY)] * 5,
        out_specs=pl.BlockSpec(memory_space=pl.ANY),
        scratch_shapes=[
            pltpu.VMEM((rows, width), BF),
            pltpu.VMEM((2, 2, width, units), BF),
            pltpu.VMEM((2, units, width), BF),
            pltpu.VMEM((rows, width), BF),
            pltpu.SemaphoreType.DMA((4, 2)),
        ],
        compiler_params=pltpu.CompilerParams(vmem_limit_bytes=48 << 20),
        cost_estimate=pl.CostEstimate(
            flops=2 * rows * width * units * 6,
            transcendentals=2 * rows * units,
            bytes_accessed=(2 * rows * width + 6 * width * units) * 2,
        ),
    )(tokens, *weights)


def on_device(
    states_in,
    w_qkv,
    qk_gain,
    w_out,
    post_gain,
    w_gate_up,
    w_down,
    cache_keys,
    cache_values,
    slot_node,
    node_length,
    node_parent,
    leaf_segment,
    leaf_node,
):
    yhi, x_at, z_at, ylo, core = (lax.axis_index(a) for a in ("yhi", "x", "z", "ylo", "core"))
    n_y, n_x, n_z = (lax.axis_size(a) for a in BLK)
    blk = (yhi * n_x + x_at) * n_z + z_at
    head_index = ylo * 2 + core
    rows = states_in.shape[0]
    heads_here = w_qkv.shape[2] // HD
    columns = w_qkv.shape[2] * 4

    corner = ("yhi", "z", "core")

    def across(values, s):
        pairs = [
            ((y * n_z + z) * 2 + c, (c * n_z + (z + s) % n_z) * 2 + y)
            for y in range(n_y) for z in range(n_z) for c in range(2)
        ]
        return lax.ppermute(values, corner, pairs)

    def head_piece(s):
        cut = ((z_at + s) % n_z) * HD
        return jnp.stack(
            [lax.dynamic_slice_in_dim(c[0], cut, HD, 1) for c in (cache_keys, cache_values)]
        )

    cached = jnp.stack([across(head_piece(s), s) for s in range(n_z)])
    slot_from = jnp.stack(
        [
            (jnp.where(c == 0, core, 1 - core) * n_x + x) * n_z + (z_at - sz) % n_z
            for c in range(2) for x in range(n_x) for sz in range(n_z)
        ]
    ).astype(jnp.int32)

    w_out = lax.dynamic_slice_in_dim(jnp.concatenate([w_out, w_out]), z_at * HD, w_out.shape[0], 0)

    def beside(weights):
        return lax.ppermute(
            weights, ("z", "core"),
            [(z * 2 + c, (z + 1 - 2 * c) % n_z * 2 + c) for z in range(n_z) for c in range(2)],
        )

    def beyond(weights):
        return lax.ppermute(
            weights, ("z", "core"), [(z * 2 + 1, (z + 2) % n_z * 2 + 1) for z in range(n_z)]
        )

    qkv_raw = jnp.einsum("td,cdw->ctw", states_in, w_qkv, preferred_element_type=F32)
    squares = jnp.sum(qkv_raw[:2] * qkv_raw[:2], axis=2)
    for axis in ("core", "ylo"):
        squares = squares + shift(squares, axis, 1)
    cached_own = spread(cached, "x").reshape((n_x * n_z,) + cached.shape[1:])
    def own_group(table):
        return lax.dynamic_slice_in_dim(table, blk, 1, 0)

    position = tree_info(
        own_group(leaf_segment), own_group(leaf_node), node_parent, node_length
    )[2][0]
    half = HD // 2
    frequency = THETA ** (-2.0 * jnp.arange(half, dtype=F32) / HD)
    angles = position.astype(F32)[:, None] * frequency[None, :]
    cosine, sine = jnp.cos(angles)[:, None, :], jnp.sin(angles)[:, None, :]

    def turned(c):
        scaled = (qkv_raw[c] * qk_gain[c]).reshape(rows, heads_here, HD)
        low, high = scaled[..., :half], scaled[..., half:]
        both = jnp.concatenate([low * cosine - high * sine, high * cosine + low * sine], axis=-1)
        return both.astype(BF)

    terms = []
    left = squares
    for _ in range(3):
        terms.append(lax.reduce_precision(left, 8, 7))
        left = left - terms[-1]
    terms = jnp.stack(terms).reshape(-1, HD).astype(BF)
    term_rows = terms.shape[0]
    terms = jnp.pad(terms, ((0, -term_rows % 16), (0, 0)))
    qkv = jnp.stack(
        [turned(0), turned(1), qkv_raw[2].astype(BF).reshape(rows, heads_here, HD)]
    ).transpose(2, 0, 1, 3).reshape(heads_here, 3 * rows, HD)
    qkv = jnp.concatenate([qkv, jnp.broadcast_to(terms, (heads_here,) + terms.shape)], axis=1)
    qkv, slot_node, node_length, node_parent, leaf_segment, leaf_node = (
        lax.optimization_barrier(
            (qkv, slot_node, node_length, node_parent, leaf_segment, leaf_node)
        )
    )
    qkv_parts = [across(select_row(qkv, (z_at + s) % n_z), s) for s in range(n_z)]

    group_from = jnp.stack(
        [(core * n_x + x_at) * n_z + (z_at - g) % n_z for g in range(n_z)]
    ).astype(jnp.int32)
    segments = jnp.take(leaf_segment, group_from, axis=0)
    middle, root, _ = tree_info(
        segments, jnp.take(leaf_node, group_from, axis=0), node_parent, node_length
    )
    slots = slot_from.shape[0]
    slot_nodes = jnp.take(slot_node, slot_from)
    slot_lengths = jnp.take(node_length, slot_nodes)
    halves = (n_z, 2, rows // 2, 1)
    needed = jnp.any(
        (middle.reshape(halves) == slot_nodes) | (root.reshape(halves) == slot_nodes), axis=2
    )
    before = jnp.arange(slots)[:, None] < jnp.arange(slots)[None, :]
    rank = jnp.sum(jnp.where(needed[..., :, None] & before, 1, 0), axis=2)
    longest = leaf_node.shape[1] + 4
    places = jnp.arange(longest, dtype=jnp.int32)
    lists = jnp.sum(
        jnp.where(
            needed[..., :, None] & (rank[..., :, None] == places),
            jnp.arange(slots, dtype=jnp.int32)[:, None], 0,
        ),
        axis=2,
    )
    counts = jnp.sum(needed.astype(jnp.int32), axis=2)
    row_info = jnp.stack([middle, root, segments], axis=-1)

    terms = jnp.stack([part[3 * rows : 3 * rows + term_rows] for part in qkv_parts]).astype(F32)
    squares = jnp.sum(terms.reshape(n_z, 3, 2, rows), axis=1).transpose(0, 2, 1)
    factors = lax.rsqrt(squares / columns + EPS)
    w_gate_up, w_down, qkv_parts = lax.optimization_barrier((w_gate_up, w_down, qkv_parts))
    cached_own, qkv_parts, slot_nodes, slot_lengths, lists, counts, row_info, factors = (
        lax.optimization_barrier(
            (cached_own, qkv_parts, slot_nodes, slot_lengths, lists, counts, row_info, factors)
        )
    )
    cached_parts = [cached_own, shift(cached_own, "core", 1)]

    gu_a = beside(w_gate_up)

    attended = attention(
        slot_nodes, slot_lengths, lists, counts, qkv_parts, row_info, segments[:, None, :],
        factors, factors[:, None, :, 1], cached_parts,
    )

    attended, gu_a, w_gate_up, w_down = lax.optimization_barrier(
        (attended, gu_a, w_gate_up, w_down)
    )
    gu_b = beyond(w_gate_up)

    def back(values, s):
        pairs = [
            ((y * n_z + z) * 2 + c, (c * n_z + (z - s) % n_z) * 2 + y)
            for y in range(n_y) for z in range(n_z) for c in range(2)
        ]
        return lax.ppermute(values, corner, pairs)

    attended = jnp.concatenate([back(attended[s], s) for s in range(n_z)], axis=1)
    attn_part = jnp.dot(attended, w_out, preferred_element_type=F32)
    attn_part = attn_part.reshape(2, 2, rows // 4, -1)

    def of_core(c):
        return lax.dynamic_index_in_dim(attn_part, c, 1, keepdims=False)

    attn_part = of_core(core) + shift(of_core(1 - core).astype(BF), "core", 1).astype(F32)
    attn_part, gu_b, w_down = lax.optimization_barrier((attn_part, gu_b, w_down))
    attn_proj = select_row(attn_part, ylo) + shift(
        select_row(attn_part, 1 - ylo).astype(BF), "ylo", 1
    ).astype(F32)
    own_rows = rows // 4
    state_rows = lax.dynamic_slice_in_dim(states_in, head_index * own_rows, own_rows, 0)
    mid_state = (state_rows.astype(F32) + rms_norm(attn_proj, post_gain[0])).astype(BF)

    plane = ("yhi", "x")
    mid_state, w_down = lax.optimization_barrier((mid_state, w_down))
    dn_a, dn_b = beside(w_down), beyond(w_down)
    tokens = spread(mid_state, plane)
    tokens, dn_a, dn_b = lax.optimization_barrier((tokens, dn_a, dn_b))
    weights = (
        gu_a, dn_a, jnp.where(core == 0, w_gate_up, gu_b), jnp.where(core == 0, w_down, dn_b)
    )
    flat = tokens.reshape(-1, tokens.shape[2])
    other = feed_forward(shift(flat, "core", 1), weights)
    total = feed_forward(flat, weights).astype(F32) + shift(other, "core", 1).astype(F32)
    total = lax.all_to_all(total.astype(BF).reshape(tokens.shape), plane, 0, 0, tiled=True)
    mlp_proj = jnp.sum(total.astype(F32), axis=0)
    return (mid_state.astype(F32) + rms_norm(mlp_proj, post_gain[1])).astype(BF)


def solution(mesh):
    fine = Mesh(mesh.devices.reshape(2, 4, 4, 2, 2), BLK + HEAD)
    placed = (
        P(BLK, None),
        P(None, None, HEAD),
        P(None, HEAD),
        P(HEAD, None),
        P(),
        P(None, None, BLK),
        P(BLK, None),
        P(BLK, None, HEAD),
        P(BLK, None, HEAD),
        P(),
        P(),
        P(),
        P(),
        P(),
    )
    return jax.shard_map(
        on_device, mesh=fine, in_specs=placed, out_specs=P(BLK + HEAD, None), check_vma=False
    )
```

```python
import functools

import jax
import jax.numpy as jnp
from jax import lax
from jax.experimental import pallas as pl
from jax.experimental.pallas import tpu as pltpu
from jax.sharding import Mesh, PartitionSpec as P

HD = 128
EPS = 1e-06
THETA = 500000.0
NEG = -1e30
LOG2E = 1.4426950408889634
BF = jnp.bfloat16
F32 = jnp.float32
BLK = ("yhi", "x", "z")
HEAD = ("ylo", "core")


def shift(values, axis, by):
    n = lax.axis_size(axis)
    return lax.ppermute(values, axis, [(i, (i + by) % n) for i in range(n)])


def spread(values, axes):
    n = 1
    for axis in (axes,) if isinstance(axes, str) else axes:
        n *= lax.axis_size(axis)
    copies = lax.optimization_barrier(jnp.broadcast_to(values, (n,) + values.shape))
    return lax.all_to_all(copies, axes, 0, 0, tiled=True)


def select_row(table, row):
    return lax.dynamic_index_in_dim(table, row, 0, keepdims=False)


def tree_info(leaf_segment, leaf_node, node_parent, node_length):
    groups, tok_rows = leaf_segment.shape
    leaf_count = leaf_node.shape[1]
    middles = node_parent.shape[0]
    all_nodes = node_length.shape[0]
    tenant_count = all_nodes - middles
    leaf_ids = jnp.arange(leaf_count, dtype=jnp.int32)
    onehot = (leaf_segment[:, :, None] == leaf_ids[None, None, :]).astype(jnp.int32)
    middle = jnp.sum(onehot * leaf_node[:, None, :], axis=-1)
    counts = jnp.sum(onehot, axis=1)
    starts = jnp.sum(jnp.where(leaf_ids[None, :] < leaf_ids[:, None], counts[:, None, :], 0), axis=-1)
    first_at = jnp.sum(onehot * starts[:, None, :], axis=-1)
    middle_ids = jnp.arange(middles, dtype=jnp.int32) + tenant_count
    root_node = jnp.sum(jnp.where(middle[..., None] == middle_ids, node_parent, 0), axis=-1)
    node_ids = jnp.arange(all_nodes, dtype=jnp.int32)
    len_middle = jnp.sum(jnp.where(middle[..., None] == node_ids, node_length, 0), axis=-1)
    len_root = jnp.sum(jnp.where(root_node[..., None] == node_ids, node_length, 0), axis=-1)
    offsets = jnp.arange(tok_rows, dtype=jnp.int32)[None, :] - first_at
    return middle, root_node, len_root + len_middle + offsets


def rms_norm(values_in, gain):
    return (
        values_in * lax.rsqrt(jnp.mean(values_in * values_in, axis=-1, keepdims=True) + EPS) * gain
    )


def attention_body(
    nodes_ref, lengths_ref, lists_ref, counts_ref,
    *rest,
):
    out_ref, qkv_ref, k_all, v_all, held, sems, qkv_sems = rest[-7:]
    qkv_parts = rest[:4]
    info_ref, seg_ref, factor_ref, key_factor_ref = rest[4:8]
    parts = rest[8:-7]
    step = pl.program_id(0)
    group = step // 2
    tile = step % 2
    half_rows = out_ref.shape[1]
    rows = 2 * half_rows
    node_rows = k_all.shape[1]
    per_part = parts[0].shape[0]
    batch = held.shape[2] // node_rows

    def copies():
        for i, part in enumerate(qkv_parts):
            yield pltpu.make_async_copy(part, qkv_ref.at[i], qkv_sems.at[i])
        for i, part in enumerate(parts):
            for j in range(per_part):
                yield pltpu.make_async_copy(
                    part.at[j, 0], k_all.at[i * per_part + j], sems.at[0, i, j]
                )
                yield pltpu.make_async_copy(
                    part.at[j, 1], v_all.at[i * per_part + j], sems.at[1, i, j]
                )

    @pl.when(step == 0)
    def _():
        for copy in copies():
            copy.start()
        for copy in copies():
            copy.wait()

    nt = (((1,), (1,)), ((), ()))
    count = counts_ref[group, tile]

    def work(first):
        q = qkv_ref[group, first : first + half_rows, :]
        seen = first + half_rows
        middle = info_ref[0, first:seen, 0:1]
        root = info_ref[0, first:seen, 1:2]
        seg_col = info_ref[0, first:seen, 2:3]
        seg_row = seg_ref[0][:, :seen]
        row_at = lax.broadcasted_iota(jnp.int32, (half_rows, seen), 0) + first
        col_at = lax.broadcasted_iota(jnp.int32, (half_rows, seen), 1)
        key_at = lax.broadcasted_iota(jnp.int32, (1, node_rows), 1)
        scale = factor_ref[0, first:seen, 0:1] * (HD**-0.5 * LOG2E)
        near = lax.dot_general(q, qkv_ref[group, rows : rows + seen, :], nt, preferred_element_type=F32)
        near = near * scale * key_factor_ref[0][:, :seen]
        near = jnp.where((seg_col == seg_row) & (col_at <= row_at), near, NEG)
        top = jnp.max(near, axis=1, keepdims=True)

        def score(i, top):
            best = None
            for j in range(batch):
                slot = lists_ref[group, tile, i * batch + j]
                node = nodes_ref[slot]
                length = jnp.where(i * batch + j < count, lengths_ref[slot], 0)
                s = lax.dot_general(q, k_all[slot], nt, preferred_element_type=F32) * scale
                shown = ((middle == node) | (root == node)) & (key_at < length)
                s = jnp.where(shown, s, NEG)
                held[i, :, j * node_rows : (j + 1) * node_rows] = s
                best = s if best is None else jnp.maximum(best, s)
            return jnp.maximum(top, jnp.max(best, axis=1, keepdims=True))

        batches = (count + batch - 1) // batch
        top = lax.fori_loop(0, batches, score, top)
        weights = jnp.exp2(near - top)
        total = jnp.sum(weights, axis=1, keepdims=True)
        summed = jnp.dot(weights.astype(BF), qkv_ref[group, 2 * rows : 2 * rows + seen, :], preferred_element_type=F32)

        def gather(i, carry):
            total, summed = carry
            added = None
            for j in range(batch):
                slot = lists_ref[group, tile, i * batch + j]
                w = jnp.exp2(held[i, :, j * node_rows : (j + 1) * node_rows] - top)
                added = w if added is None else added + w
                summed = summed + jnp.dot(
                    w.astype(BF), v_all[slot], preferred_element_type=F32
                )
            return total + jnp.sum(added, axis=1, keepdims=True), summed

        total, summed = lax.fori_loop(0, batches, gather, (total, summed))
        out_ref[0] = (summed / total).astype(BF)

    for t in range(2):
        @pl.when(tile == t)
        def _(t=t):
            work(t * half_rows)


def attention(
    nodes, lengths, lists, counts, qkv_parts, row_info, seg_row, factors, key_factors, parts
):
    rows = row_info.shape[1]
    groups = len(qkv_parts)
    per_part, _, node_rows, _ = parts[0].shape
    slots = nodes.shape[0]
    batch = 4
    one = lambda shape: pl.BlockSpec((1,) + shape, lambda i, *_: (i // 2,) + (0,) * len(shape))
    return pl.pallas_call(
        attention_body,
        out_shape=jax.ShapeDtypeStruct((groups, rows, HD), BF),
        grid_spec=pltpu.PrefetchScalarGridSpec(
            num_scalar_prefetch=4,
            grid=(groups * 2,),
            in_specs=[pl.BlockSpec(memory_space=pl.ANY)] * groups
            + [one((rows, 3)), one((1, rows)), one((rows, 2)), one((1, rows))]
            + [pl.BlockSpec(memory_space=pl.ANY)] * len(parts),
            out_specs=pl.BlockSpec((1, rows // 2, HD), lambda i, *_: (i // 2, i % 2, 0)),
            scratch_shapes=[
                pltpu.VMEM((groups,) + qkv_parts[0].shape, BF),
                pltpu.VMEM((slots, node_rows, HD), BF),
                pltpu.VMEM((slots, node_rows, HD), BF),
                pltpu.VMEM((lists.shape[2] // batch, rows // 2, batch * node_rows), F32),
                pltpu.SemaphoreType.DMA((2, len(parts), per_part)),
                pltpu.SemaphoreType.DMA((groups,)),
            ],
        ),
        compiler_params=pltpu.CompilerParams(vmem_limit_bytes=32 << 20),
        cost_estimate=pl.CostEstimate(
            flops=2 * 10**9, transcendentals=4 * 10**6, bytes_accessed=6 * 10**6
        ),
    )(nodes, lengths, lists, counts, *qkv_parts, row_info, seg_row, factors, key_factors, *parts)


def feed_forward_body(tokens_ref, gu_a, dn_a, gu_b, dn_b, out_ref, tokens, gu, dn, made, sems):
    rows = 256
    blocks = tokens.shape[0] // rows

    def block(ref, i):
        return ref.at[pl.ds(i * rows, rows)]

    def fetch(i):
        return pltpu.make_async_copy(block(tokens_ref, i), block(tokens, i), sems.at[0, i])

    def store(i):
        return pltpu.make_async_copy(block(made, i), block(out_ref, i), sems.at[1, i])

    loads = [
        pltpu.make_async_copy(source, target, sems.at[2 + j, k])
        for k, pair in enumerate(((gu_a, dn_a), (gu_b, dn_b)))
        for j, (source, target) in enumerate(((pair[0], gu.at[k]), (pair[1], dn.at[k])))
    ]
    fetch(0).start()
    for load in loads:
        load.start()
    for i in range(1, blocks):
        fetch(i).start()
    for i in range(blocks):
        fetch(i).wait()
        part = 0.0
        for k in range(2):
            if i == 0:
                loads[2 * k].wait()
            values = tokens[i * rows : (i + 1) * rows, :]
            gate = jnp.dot(values, gu[k, 0], preferred_element_type=F32)
            up = jnp.dot(values, gu[k, 1], preferred_element_type=F32)
            hidden = (gate / (1.0 + jnp.exp(-gate)) * up).astype(BF)
            if i == 0:
                loads[2 * k + 1].wait()
            part = part + jnp.dot(hidden, dn[k], preferred_element_type=F32)
        made[i * rows : (i + 1) * rows, :] = part.astype(BF)
        store(i).start()
    for i in range(blocks):
        store(i).wait()


def feed_forward(tokens, weights):
    rows, width = tokens.shape
    units = weights[1].shape[0]
    return pl.pallas_call(
        feed_forward_body,
        out_shape=jax.ShapeDtypeStruct((rows, width), BF),
        in_specs=[pl.BlockSpec(memory_space=pl.ANY)] * 5,
        out_specs=pl.BlockSpec(memory_space=pl.ANY),
        scratch_shapes=[
            pltpu.VMEM((rows, width), BF),
            pltpu.VMEM((2, 2, width, units), BF),
            pltpu.VMEM((2, units, width), BF),
            pltpu.VMEM((rows, width), BF),
            pltpu.SemaphoreType.DMA((4, 2)),
        ],
        compiler_params=pltpu.CompilerParams(vmem_limit_bytes=48 << 20),
        cost_estimate=pl.CostEstimate(
            flops=2 * rows * width * units * 6,
            transcendentals=2 * rows * units,
            bytes_accessed=(2 * rows * width + 6 * width * units) * 2,
        ),
    )(tokens, *weights)


def on_device(
    states_in,
    w_qkv,
    qk_gain,
    w_out,
    post_gain,
    w_gate_up,
    w_down,
    cache_keys,
    cache_values,
    slot_node,
    node_length,
    node_parent,
    leaf_segment,
    leaf_node,
):
    yhi, x_at, z_at, ylo, core = (lax.axis_index(a) for a in ("yhi", "x", "z", "ylo", "core"))
    n_y, n_x, n_z = (lax.axis_size(a) for a in BLK)
    blk = (yhi * n_x + x_at) * n_z + z_at
    head_index = ylo * 2 + core
    rows = states_in.shape[0]
    heads_here = w_qkv.shape[2] // HD
    columns = w_qkv.shape[2] * 4

    corner = ("yhi", "z", "core")

    def across(values, s):
        pairs = [
            ((y * n_z + z) * 2 + c, (c * n_z + (z + s) % n_z) * 2 + y)
            for y in range(n_y) for z in range(n_z) for c in range(2)
        ]
        return lax.ppermute(values, corner, pairs)

    def head_piece(s):
        cut = ((z_at + s) % n_z) * HD
        return jnp.stack(
            [lax.dynamic_slice_in_dim(c[0], cut, HD, 1) for c in (cache_keys, cache_values)]
        )

    cached = jnp.stack([across(head_piece(s), s) for s in range(n_z)])
    slot_from = jnp.stack(
        [
            (jnp.where(c == 0, core, 1 - core) * n_x + x) * n_z + (z_at - sz) % n_z
            for c in range(2) for x in range(n_x) for sz in range(n_z)
        ]
    ).astype(jnp.int32)

    w_out = lax.dynamic_slice_in_dim(jnp.concatenate([w_out, w_out]), z_at * HD, w_out.shape[0], 0)

    def beside(weights):
        return lax.ppermute(
            weights, ("z", "core"),
            [(z * 2 + c, (z + 1 - 2 * c) % n_z * 2 + c) for z in range(n_z) for c in range(2)],
        )

    def beyond(weights):
        return lax.ppermute(
            weights, ("z", "core"), [(z * 2 + 1, (z + 2) % n_z * 2 + 1) for z in range(n_z)]
        )

    gu_a = beside(w_gate_up)

    qkv_raw = jnp.einsum("td,cdw->ctw", states_in, w_qkv, preferred_element_type=F32)
    squares = jnp.sum(qkv_raw[:2] * qkv_raw[:2], axis=2)
    squares = jnp.sum(spread(squares, HEAD), axis=0)
    cached_own = spread(cached, "x").reshape((n_x * n_z,) + cached.shape[1:])
    def own_group(table):
        return lax.dynamic_slice_in_dim(table, blk, 1, 0)

    position = tree_info(
        own_group(leaf_segment), own_group(leaf_node), node_parent, node_length
    )[2][0]
    half = HD // 2
    frequency = THETA ** (-2.0 * jnp.arange(half, dtype=F32) / HD)
    angles = position.astype(F32)[:, None] * frequency[None, :]
    cosine, sine = jnp.cos(angles)[:, None, :], jnp.sin(angles)[:, None, :]

    def turned(c):
        scaled = (qkv_raw[c] * qk_gain[c]).reshape(rows, heads_here, HD)
        low, high = scaled[..., :half], scaled[..., half:]
        both = jnp.concatenate([low * cosine - high * sine, high * cosine + low * sine], axis=-1)
        return both.astype(BF)

    terms = []
    left = squares
    for _ in range(3):
        terms.append(lax.reduce_precision(left, 8, 7))
        left = left - terms[-1]
    terms = jnp.stack(terms).reshape(-1, HD).astype(BF)
    term_rows = terms.shape[0]
    terms = jnp.pad(terms, ((0, -term_rows % 16), (0, 0)))
    qkv = jnp.stack(
        [turned(0), turned(1), qkv_raw[2].astype(BF).reshape(rows, heads_here, HD)]
    ).transpose(2, 0, 1, 3).reshape(heads_here, 3 * rows, HD)
    qkv = jnp.concatenate([qkv, jnp.broadcast_to(terms, (heads_here,) + terms.shape)], axis=1)
    qkv, gu_a, slot_node, node_length, node_parent, leaf_segment, leaf_node = (
        lax.optimization_barrier(
            (qkv, gu_a, slot_node, node_length, node_parent, leaf_segment, leaf_node)
        )
    )
    qkv_parts = [across(select_row(qkv, (z_at + s) % n_z), s) for s in range(n_z)]

    group_from = jnp.stack(
        [(core * n_x + x_at) * n_z + (z_at - g) % n_z for g in range(n_z)]
    ).astype(jnp.int32)
    segments = jnp.take(leaf_segment, group_from, axis=0)
    middle, root, _ = tree_info(
        segments, jnp.take(leaf_node, group_from, axis=0), node_parent, node_length
    )
    slots = slot_from.shape[0]
    slot_nodes = jnp.take(slot_node, slot_from)
    slot_lengths = jnp.take(node_length, slot_nodes)
    halves = (n_z, 2, rows // 2, 1)
    needed = jnp.any(
        (middle.reshape(halves) == slot_nodes) | (root.reshape(halves) == slot_nodes), axis=2
    )
    before = jnp.arange(slots)[:, None] < jnp.arange(slots)[None, :]
    rank = jnp.sum(jnp.where(needed[..., :, None] & before, 1, 0), axis=2)
    longest = leaf_node.shape[1] + 4
    places = jnp.arange(longest, dtype=jnp.int32)
    lists = jnp.sum(
        jnp.where(
            needed[..., :, None] & (rank[..., :, None] == places),
            jnp.arange(slots, dtype=jnp.int32)[:, None], 0,
        ),
        axis=2,
    )
    counts = jnp.sum(needed.astype(jnp.int32), axis=2)
    row_info = jnp.stack([middle, root, segments], axis=-1)

    terms = jnp.stack([part[3 * rows : 3 * rows + term_rows] for part in qkv_parts]).astype(F32)
    squares = jnp.sum(terms.reshape(n_z, 3, 2, rows), axis=1).transpose(0, 2, 1)
    factors = lax.rsqrt(squares / columns + EPS)
    w_gate_up, w_down, qkv_parts = lax.optimization_barrier((w_gate_up, w_down, qkv_parts))
    cached_own, qkv_parts, slot_nodes, slot_lengths, lists, counts, row_info, factors = (
        lax.optimization_barrier(
            (cached_own, qkv_parts, slot_nodes, slot_lengths, lists, counts, row_info, factors)
        )
    )
    cached_parts = [cached_own, shift(cached_own, "core", 1)]


    gu_b, dn_b = beyond(w_gate_up), beyond(w_down)

    attended = attention(
        slot_nodes, slot_lengths, lists, counts, qkv_parts, row_info, segments[:, None, :],
        factors, factors[:, None, :, 1], cached_parts,
    )

    def back(values, s):
        pairs = [
            ((y * n_z + z) * 2 + c, (c * n_z + (z - s) % n_z) * 2 + y)
            for y in range(n_y) for z in range(n_z) for c in range(2)
        ]
        return lax.ppermute(values, corner, pairs)

    attended = jnp.concatenate([back(attended[s], s) for s in range(n_z)], axis=1)
    attended, gu_b, dn_b = lax.optimization_barrier((attended, gu_b, dn_b))
    attn_part = jnp.dot(attended, w_out, preferred_element_type=F32)
    attn_part = attn_part.reshape(2, 2, rows // 4, -1)

    def of_core(c):
        return lax.dynamic_index_in_dim(attn_part, c, 1, keepdims=False)

    attn_part = of_core(core) + shift(of_core(1 - core).astype(BF), "core", 1).astype(F32)
    attn_proj = select_row(attn_part, ylo) + shift(
        select_row(attn_part, 1 - ylo).astype(BF), "ylo", 1
    ).astype(F32)
    own_rows = rows // 4
    state_rows = lax.dynamic_slice_in_dim(states_in, head_index * own_rows, own_rows, 0)
    mid_state = (state_rows.astype(F32) + rms_norm(attn_proj, post_gain[0])).astype(BF)

    plane = ("yhi", "x")
    mid_state, w_down = lax.optimization_barrier((mid_state, w_down))
    dn_a = beside(w_down)
    tokens = spread(mid_state, plane)
    tokens, dn_a = lax.optimization_barrier((tokens, dn_a))
    weights = (
        gu_a, dn_a, jnp.where(core == 0, w_gate_up, gu_b), jnp.where(core == 0, w_down, dn_b)
    )
    flat = tokens.reshape(-1, tokens.shape[2])
    other = feed_forward(shift(flat, "core", 1), weights)
    total = feed_forward(flat, weights).astype(F32) + shift(other, "core", 1).astype(F32)
    total = lax.all_to_all(total.astype(BF).reshape(tokens.shape), plane, 0, 0, tiled=True)
    mlp_proj = jnp.sum(total.astype(F32), axis=0)
    return (mid_state.astype(F32) + rms_norm(mlp_proj, post_gain[1])).astype(BF)


def solution(mesh):
    fine = Mesh(mesh.devices.reshape(2, 4, 4, 2, 2), BLK + HEAD)
    placed = (
        P(BLK, None),
        P(None, None, HEAD),
        P(None, HEAD),
        P(HEAD, None),
        P(),
        P(None, None, BLK),
        P(BLK, None),
        P(BLK, None, HEAD),
        P(BLK, None, HEAD),
        P(),
        P(),
        P(),
        P(),
        P(),
    )
    return jax.shard_map(
        on_device, mesh=fine, in_specs=placed, out_specs=P(BLK + HEAD, None), check_vma=False
    )
```

```python
import functools

import jax
import jax.numpy as jnp
from jax import lax
from jax.experimental import pallas as pl
from jax.experimental.pallas import tpu as pltpu
from jax.sharding import Mesh, PartitionSpec as P

HD = 128
EPS = 1e-06
THETA = 500000.0
NEG = -1e30
LOG2E = 1.4426950408889634
BF = jnp.bfloat16
F32 = jnp.float32
BLK = ("yhi", "x", "z")
HEAD = ("ylo", "core")


def shift(values, axis, by):
    n = lax.axis_size(axis)
    return lax.ppermute(values, axis, [(i, (i + by) % n) for i in range(n)])


def spread(values, axes):
    n = 1
    for axis in (axes,) if isinstance(axes, str) else axes:
        n *= lax.axis_size(axis)
    copies = lax.optimization_barrier(jnp.broadcast_to(values, (n,) + values.shape))
    return lax.all_to_all(copies, axes, 0, 0, tiled=True)


def select_row(table, row):
    return lax.dynamic_index_in_dim(table, row, 0, keepdims=False)


def tree_info(leaf_segment, leaf_node, node_parent, node_length):
    groups, tok_rows = leaf_segment.shape
    leaf_count = leaf_node.shape[1]
    middles = node_parent.shape[0]
    all_nodes = node_length.shape[0]
    tenant_count = all_nodes - middles
    leaf_ids = jnp.arange(leaf_count, dtype=jnp.int32)
    onehot = (leaf_segment[:, :, None] == leaf_ids[None, None, :]).astype(jnp.int32)
    middle = jnp.sum(onehot * leaf_node[:, None, :], axis=-1)
    counts = jnp.sum(onehot, axis=1)
    starts = jnp.sum(jnp.where(leaf_ids[None, :] < leaf_ids[:, None], counts[:, None, :], 0), axis=-1)
    first_at = jnp.sum(onehot * starts[:, None, :], axis=-1)
    middle_ids = jnp.arange(middles, dtype=jnp.int32) + tenant_count
    root_node = jnp.sum(jnp.where(middle[..., None] == middle_ids, node_parent, 0), axis=-1)
    node_ids = jnp.arange(all_nodes, dtype=jnp.int32)
    len_middle = jnp.sum(jnp.where(middle[..., None] == node_ids, node_length, 0), axis=-1)
    len_root = jnp.sum(jnp.where(root_node[..., None] == node_ids, node_length, 0), axis=-1)
    offsets = jnp.arange(tok_rows, dtype=jnp.int32)[None, :] - first_at
    return middle, root_node, len_root + len_middle + offsets


def rms_norm(values_in, gain):
    return (
        values_in * lax.rsqrt(jnp.mean(values_in * values_in, axis=-1, keepdims=True) + EPS) * gain
    )


def attention_body(
    nodes_ref, lengths_ref, lists_ref, counts_ref,
    *rest,
):
    out_ref, qkv_ref, k_all, v_all, held, sems, qkv_sems = rest[-7:]
    qkv_parts = rest[:4]
    info_ref, seg_ref, factor_ref, key_factor_ref = rest[4:8]
    parts = rest[8:-7]
    step = pl.program_id(0)
    group = step // 2
    tile = step % 2
    half_rows = out_ref.shape[1]
    rows = 2 * half_rows
    node_rows = k_all.shape[1]
    per_part = parts[0].shape[0]
    batch = held.shape[2] // node_rows

    def copies():
        for i, part in enumerate(qkv_parts):
            yield pltpu.make_async_copy(part, qkv_ref.at[i], qkv_sems.at[i])
        for i, part in enumerate(parts):
            for j in range(per_part):
                yield pltpu.make_async_copy(
                    part.at[j, 0], k_all.at[i * per_part + j], sems.at[0, i, j]
                )
                yield pltpu.make_async_copy(
                    part.at[j, 1], v_all.at[i * per_part + j], sems.at[1, i, j]
                )

    @pl.when(step == 0)
    def _():
        for copy in copies():
            copy.start()
        for copy in copies():
            copy.wait()

    nt = (((1,), (1,)), ((), ()))
    count = counts_ref[group, tile]

    def work(first):
        q = qkv_ref[group, first : first + half_rows, :]
        seen = first + half_rows
        middle = info_ref[0, first:seen, 0:1]
        root = info_ref[0, first:seen, 1:2]
        seg_col = info_ref[0, first:seen, 2:3]
        seg_row = seg_ref[0][:, :seen]
        row_at = lax.broadcasted_iota(jnp.int32, (half_rows, seen), 0) + first
        col_at = lax.broadcasted_iota(jnp.int32, (half_rows, seen), 1)
        key_at = lax.broadcasted_iota(jnp.int32, (1, node_rows), 1)
        scale = factor_ref[0, first:seen, 0:1] * (HD**-0.5 * LOG2E)
        near = lax.dot_general(q, qkv_ref[group, rows : rows + seen, :], nt, preferred_element_type=F32)
        near = near * scale * key_factor_ref[0][:, :seen]
        near = jnp.where((seg_col == seg_row) & (col_at <= row_at), near, NEG)
        top = jnp.max(near, axis=1, keepdims=True)

        def score(i, top):
            best = None
            for j in range(batch):
                slot = lists_ref[group, tile, i * batch + j]
                node = nodes_ref[slot]
                length = jnp.where(i * batch + j < count, lengths_ref[slot], 0)
                s = lax.dot_general(q, k_all[slot], nt, preferred_element_type=F32) * scale
                shown = ((middle == node) | (root == node)) & (key_at < length)
                s = jnp.where(shown, s, NEG)
                held[i, :, j * node_rows : (j + 1) * node_rows] = s
                best = s if best is None else jnp.maximum(best, s)
            return jnp.maximum(top, jnp.max(best, axis=1, keepdims=True))

        batches = (count + batch - 1) // batch
        top = lax.fori_loop(0, batches, score, top)
        weights = jnp.exp2(near - top)
        total = jnp.sum(weights, axis=1, keepdims=True)
        summed = jnp.dot(weights.astype(BF), qkv_ref[group, 2 * rows : 2 * rows + seen, :], preferred_element_type=F32)

        def gather(i, carry):
            total, summed = carry
            added = None
            for j in range(batch):
                slot = lists_ref[group, tile, i * batch + j]
                w = jnp.exp2(held[i, :, j * node_rows : (j + 1) * node_rows] - top)
                added = w if added is None else added + w
                summed = summed + jnp.dot(
                    w.astype(BF), v_all[slot], preferred_element_type=F32
                )
            return total + jnp.sum(added, axis=1, keepdims=True), summed

        total, summed = lax.fori_loop(0, batches, gather, (total, summed))
        out_ref[0] = (summed / total).astype(BF)

    for t in range(2):
        @pl.when(tile == t)
        def _(t=t):
            work(t * half_rows)


def attention(
    nodes, lengths, lists, counts, qkv_parts, row_info, seg_row, factors, key_factors, parts
):
    rows = row_info.shape[1]
    groups = len(qkv_parts)
    per_part, _, node_rows, _ = parts[0].shape
    slots = nodes.shape[0]
    batch = 4
    one = lambda shape: pl.BlockSpec((1,) + shape, lambda i, *_: (i // 2,) + (0,) * len(shape))
    return pl.pallas_call(
        attention_body,
        out_shape=jax.ShapeDtypeStruct((groups, rows, HD), BF),
        grid_spec=pltpu.PrefetchScalarGridSpec(
            num_scalar_prefetch=4,
            grid=(groups * 2,),
            in_specs=[pl.BlockSpec(memory_space=pl.ANY)] * groups
            + [one((rows, 3)), one((1, rows)), one((rows, 2)), one((1, rows))]
            + [pl.BlockSpec(memory_space=pl.ANY)] * len(parts),
            out_specs=pl.BlockSpec((1, rows // 2, HD), lambda i, *_: (i // 2, i % 2, 0)),
            scratch_shapes=[
                pltpu.VMEM((groups,) + qkv_parts[0].shape, BF),
                pltpu.VMEM((slots, node_rows, HD), BF),
                pltpu.VMEM((slots, node_rows, HD), BF),
                pltpu.VMEM((lists.shape[2] // batch, rows // 2, batch * node_rows), F32),
                pltpu.SemaphoreType.DMA((2, len(parts), per_part)),
                pltpu.SemaphoreType.DMA((groups,)),
            ],
        ),
        compiler_params=pltpu.CompilerParams(vmem_limit_bytes=32 << 20),
        cost_estimate=pl.CostEstimate(
            flops=2 * 10**9, transcendentals=4 * 10**6, bytes_accessed=6 * 10**6
        ),
    )(nodes, lengths, lists, counts, *qkv_parts, row_info, seg_row, factors, key_factors, *parts)


def feed_forward_body(tokens_ref, gu_a, dn_a, gu_b, dn_b, out_ref, tokens, gu, dn, made, sems):
    rows = 256
    blocks = tokens.shape[0] // rows

    def block(ref, i):
        return ref.at[pl.ds(i * rows, rows)]

    def fetch(i):
        return pltpu.make_async_copy(block(tokens_ref, i), block(tokens, i), sems.at[0, i])

    def store(i):
        return pltpu.make_async_copy(block(made, i), block(out_ref, i), sems.at[1, i])

    loads = [
        pltpu.make_async_copy(source, target, sems.at[2 + j, k])
        for k, pair in enumerate(((gu_a, dn_a), (gu_b, dn_b)))
        for j, (source, target) in enumerate(((pair[0], gu.at[k]), (pair[1], dn.at[k])))
    ]
    fetch(0).start()
    for load in loads:
        load.start()
    for i in range(1, blocks):
        fetch(i).start()
    for i in range(blocks):
        fetch(i).wait()
        part = 0.0
        for k in range(2):
            if i == 0:
                loads[2 * k].wait()
            values = tokens[i * rows : (i + 1) * rows, :]
            gate = jnp.dot(values, gu[k, 0], preferred_element_type=F32)
            up = jnp.dot(values, gu[k, 1], preferred_element_type=F32)
            hidden = (gate / (1.0 + jnp.exp(-gate)) * up).astype(BF)
            if i == 0:
                loads[2 * k + 1].wait()
            part = part + jnp.dot(hidden, dn[k], preferred_element_type=F32)
        made[i * rows : (i + 1) * rows, :] = part.astype(BF)
        store(i).start()
    for i in range(blocks):
        store(i).wait()


def feed_forward(tokens, weights):
    rows, width = tokens.shape
    units = weights[1].shape[0]
    return pl.pallas_call(
        feed_forward_body,
        out_shape=jax.ShapeDtypeStruct((rows, width), BF),
        in_specs=[pl.BlockSpec(memory_space=pl.ANY)] * 5,
        out_specs=pl.BlockSpec(memory_space=pl.ANY),
        scratch_shapes=[
            pltpu.VMEM((rows, width), BF),
            pltpu.VMEM((2, 2, width, units), BF),
            pltpu.VMEM((2, units, width), BF),
            pltpu.VMEM((rows, width), BF),
            pltpu.SemaphoreType.DMA((4, 2)),
        ],
        compiler_params=pltpu.CompilerParams(vmem_limit_bytes=48 << 20),
        cost_estimate=pl.CostEstimate(
            flops=2 * rows * width * units * 6,
            transcendentals=2 * rows * units,
            bytes_accessed=(2 * rows * width + 6 * width * units) * 2,
        ),
    )(tokens, *weights)


def on_device(
    states_in,
    w_qkv,
    qk_gain,
    w_out,
    post_gain,
    w_gate_up,
    w_down,
    cache_keys,
    cache_values,
    slot_node,
    node_length,
    node_parent,
    leaf_segment,
    leaf_node,
):
    yhi, x_at, z_at, ylo, core = (lax.axis_index(a) for a in ("yhi", "x", "z", "ylo", "core"))
    n_y, n_x, n_z = (lax.axis_size(a) for a in BLK)
    blk = (yhi * n_x + x_at) * n_z + z_at
    head_index = ylo * 2 + core
    rows = states_in.shape[0]
    heads_here = w_qkv.shape[2] // HD
    columns = w_qkv.shape[2] * 4

    corner = ("yhi", "z", "core")

    def across(values, s):
        pairs = [
            ((y * n_z + z) * 2 + c, (c * n_z + (z + s) % n_z) * 2 + y)
            for y in range(n_y) for z in range(n_z) for c in range(2)
        ]
        return lax.ppermute(values, corner, pairs)

    def head_piece(s):
        cut = ((z_at + s) % n_z) * HD
        return jnp.stack(
            [lax.dynamic_slice_in_dim(c[0], cut, HD, 1) for c in (cache_keys, cache_values)]
        )

    cached = jnp.stack([across(head_piece(s), s) for s in range(n_z)])
    slot_from = jnp.stack(
        [
            (jnp.where(c == 0, core, 1 - core) * n_x + x) * n_z + (z_at - sz) % n_z
            for c in range(2) for x in range(n_x) for sz in range(n_z)
        ]
    ).astype(jnp.int32)

    w_out = lax.dynamic_slice_in_dim(jnp.concatenate([w_out, w_out]), z_at * HD, w_out.shape[0], 0)

    def beside(weights):
        return lax.ppermute(
            weights, ("z", "core"),
            [(z * 2 + c, (z + 1 - 2 * c) % n_z * 2 + c) for z in range(n_z) for c in range(2)],
        )

    def beyond(weights):
        return lax.ppermute(
            weights, ("z", "core"), [(z * 2 + 1, (z + 2) % n_z * 2 + 1) for z in range(n_z)]
        )

    gu_a = beside(w_gate_up)

    qkv_raw = jnp.einsum("td,cdw->ctw", states_in, w_qkv, preferred_element_type=F32)
    squares = jnp.sum(qkv_raw[:2] * qkv_raw[:2], axis=2)
    cached_own = spread(cached, "x").reshape((n_x * n_z,) + cached.shape[1:])
    def own_group(table):
        return lax.dynamic_slice_in_dim(table, blk, 1, 0)

    position = tree_info(
        own_group(leaf_segment), own_group(leaf_node), node_parent, node_length
    )[2][0]
    half = HD // 2
    frequency = THETA ** (-2.0 * jnp.arange(half, dtype=F32) / HD)
    angles = position.astype(F32)[:, None] * frequency[None, :]
    cosine, sine = jnp.cos(angles)[:, None, :], jnp.sin(angles)[:, None, :]

    def turned(c):
        scaled = (qkv_raw[c] * qk_gain[c]).reshape(rows, heads_here, HD)
        low, high = scaled[..., :half], scaled[..., half:]
        both = jnp.concatenate([low * cosine - high * sine, high * cosine + low * sine], axis=-1)
        return both.astype(BF)

    terms = []
    left = squares
    for _ in range(3):
        terms.append(lax.reduce_precision(left, 8, 7))
        left = left - terms[-1]
    terms = jnp.stack(terms).reshape(-1, HD).astype(BF)
    term_rows = terms.shape[0]
    terms = jnp.pad(terms, ((0, -term_rows % 16), (0, 0)))
    qkv = jnp.stack(
        [turned(0), turned(1), qkv_raw[2].astype(BF).reshape(rows, heads_here, HD)]
    ).transpose(2, 0, 1, 3).reshape(heads_here, 3 * rows, HD)
    qkv = jnp.concatenate([qkv, jnp.broadcast_to(terms, (heads_here,) + terms.shape)], axis=1)
    qkv, gu_a = lax.optimization_barrier((qkv, gu_a))
    qkv_parts = [across(select_row(qkv, (z_at + s) % n_z), s) for s in range(n_z)]

    terms = jnp.stack([part[3 * rows : 3 * rows + term_rows] for part in qkv_parts]).astype(F32)
    squares = jnp.sum(terms.reshape(n_z, 3, 2, rows), axis=1).transpose(0, 2, 1)
    for axis in ("yhi", "ylo"):
        squares = squares + shift(squares, axis, 1)
    factors = lax.rsqrt(squares / columns + EPS)
    w_gate_up, w_down, qkv_parts = lax.optimization_barrier((w_gate_up, w_down, qkv_parts))
    cached_own, qkv_parts, slot_node, node_length, node_parent, leaf_segment, leaf_node = (
        lax.optimization_barrier(
            (cached_own, qkv_parts, slot_node, node_length, node_parent, leaf_segment, leaf_node)
        )
    )
    cached_parts = [cached_own, shift(cached_own, "core", 1)]


    gu_b, dn_b = beyond(w_gate_up), beyond(w_down)

    group_from = jnp.stack(
        [(core * n_x + x_at) * n_z + (z_at - g) % n_z for g in range(n_z)]
    ).astype(jnp.int32)
    segments = jnp.take(leaf_segment, group_from, axis=0)
    middle, root, _ = tree_info(
        segments, jnp.take(leaf_node, group_from, axis=0), node_parent, node_length
    )
    slots = slot_from.shape[0]
    slot_nodes = jnp.take(slot_node, slot_from)
    slot_lengths = jnp.take(node_length, slot_nodes)
    halves = (n_z, 2, rows // 2, 1)
    needed = jnp.any(
        (middle.reshape(halves) == slot_nodes) | (root.reshape(halves) == slot_nodes), axis=2
    )
    before = jnp.arange(slots)[:, None] < jnp.arange(slots)[None, :]
    rank = jnp.sum(jnp.where(needed[..., :, None] & before, 1, 0), axis=2)
    longest = leaf_node.shape[1] + 4
    places = jnp.arange(longest, dtype=jnp.int32)
    lists = jnp.sum(
        jnp.where(
            needed[..., :, None] & (rank[..., :, None] == places),
            jnp.arange(slots, dtype=jnp.int32)[:, None], 0,
        ),
        axis=2,
    )
    counts = jnp.sum(needed.astype(jnp.int32), axis=2)
    row_info = jnp.stack([middle, root, segments], axis=-1)

    attended = attention(
        slot_nodes, slot_lengths, lists, counts, qkv_parts, row_info, segments[:, None, :],
        factors, factors[:, None, :, 1], cached_parts,
    )

    def back(values, s):
        pairs = [
            ((y * n_z + z) * 2 + c, (c * n_z + (z - s) % n_z) * 2 + y)
            for y in range(n_y) for z in range(n_z) for c in range(2)
        ]
        return lax.ppermute(values, corner, pairs)

    attended = jnp.concatenate([back(attended[s], s) for s in range(n_z)], axis=1)
    attended, gu_b, dn_b = lax.optimization_barrier((attended, gu_b, dn_b))
    attn_part = jnp.dot(attended, w_out, preferred_element_type=F32)
    attn_part = attn_part.reshape(2, 2, rows // 4, -1)

    def of_core(c):
        return lax.dynamic_index_in_dim(attn_part, c, 1, keepdims=False)

    attn_part = of_core(core) + shift(of_core(1 - core).astype(BF), "core", 1).astype(F32)
    attn_proj = select_row(attn_part, ylo) + shift(
        select_row(attn_part, 1 - ylo).astype(BF), "ylo", 1
    ).astype(F32)
    own_rows = rows // 4
    state_rows = lax.dynamic_slice_in_dim(states_in, head_index * own_rows, own_rows, 0)
    mid_state = (state_rows.astype(F32) + rms_norm(attn_proj, post_gain[0])).astype(BF)

    plane = ("yhi", "x")
    mid_state, w_down = lax.optimization_barrier((mid_state, w_down))
    dn_a = beside(w_down)
    tokens = spread(mid_state, plane)
    tokens, dn_a = lax.optimization_barrier((tokens, dn_a))
    weights = (
        gu_a, dn_a, jnp.where(core == 0, w_gate_up, gu_b), jnp.where(core == 0, w_down, dn_b)
    )
    flat = tokens.reshape(-1, tokens.shape[2])
    other = feed_forward(shift(flat, "core", 1), weights)
    total = feed_forward(flat, weights).astype(F32) + shift(other, "core", 1).astype(F32)
    total = lax.all_to_all(total.astype(BF).reshape(tokens.shape), plane, 0, 0, tiled=True)
    mlp_proj = jnp.sum(total.astype(F32), axis=0)
    return (mid_state.astype(F32) + rms_norm(mlp_proj, post_gain[1])).astype(BF)


def solution(mesh):
    fine = Mesh(mesh.devices.reshape(2, 4, 4, 2, 2), BLK + HEAD)
    placed = (
        P(BLK, None),
        P(None, None, HEAD),
        P(None, HEAD),
        P(HEAD, None),
        P(),
        P(None, None, BLK),
        P(BLK, None),
        P(BLK, None, HEAD),
        P(BLK, None, HEAD),
        P(),
        P(),
        P(),
        P(),
        P(),
    )
    return jax.shard_map(
        on_device, mesh=fine, in_specs=placed, out_specs=P(BLK + HEAD, None), check_vma=False
    )
```

```python
import functools

import jax
import jax.numpy as jnp
from jax import lax
from jax.experimental import pallas as pl
from jax.experimental.pallas import tpu as pltpu
from jax.sharding import Mesh, PartitionSpec as P

HD = 128
EPS = 1e-06
THETA = 500000.0
NEG = -1e30
LOG2E = 1.4426950408889634
BF = jnp.bfloat16
F32 = jnp.float32
BLK = ("yhi", "x", "z")
HEAD = ("ylo", "core")


def shift(values, axis, by):
    n = lax.axis_size(axis)
    return lax.ppermute(values, axis, [(i, (i + by) % n) for i in range(n)])


def spread(values, axes):
    n = 1
    for axis in (axes,) if isinstance(axes, str) else axes:
        n *= lax.axis_size(axis)
    copies = lax.optimization_barrier(jnp.broadcast_to(values, (n,) + values.shape))
    return lax.all_to_all(copies, axes, 0, 0, tiled=True)


def select_row(table, row):
    return lax.dynamic_index_in_dim(table, row, 0, keepdims=False)


def tree_info(leaf_segment, leaf_node, node_parent, node_length):
    groups, tok_rows = leaf_segment.shape
    leaf_count = leaf_node.shape[1]
    middles = node_parent.shape[0]
    all_nodes = node_length.shape[0]
    tenant_count = all_nodes - middles
    leaf_ids = jnp.arange(leaf_count, dtype=jnp.int32)
    onehot = (leaf_segment[:, :, None] == leaf_ids[None, None, :]).astype(jnp.int32)
    middle = jnp.sum(onehot * leaf_node[:, None, :], axis=-1)
    counts = jnp.sum(onehot, axis=1)
    starts = jnp.sum(jnp.where(leaf_ids[None, :] < leaf_ids[:, None], counts[:, None, :], 0), axis=-1)
    first_at = jnp.sum(onehot * starts[:, None, :], axis=-1)
    middle_ids = jnp.arange(middles, dtype=jnp.int32) + tenant_count
    root_node = jnp.sum(jnp.where(middle[..., None] == middle_ids, node_parent, 0), axis=-1)
    node_ids = jnp.arange(all_nodes, dtype=jnp.int32)
    len_middle = jnp.sum(jnp.where(middle[..., None] == node_ids, node_length, 0), axis=-1)
    len_root = jnp.sum(jnp.where(root_node[..., None] == node_ids, node_length, 0), axis=-1)
    offsets = jnp.arange(tok_rows, dtype=jnp.int32)[None, :] - first_at
    return middle, root_node, len_root + len_middle + offsets


def rms_norm(values_in, gain):
    return (
        values_in * lax.rsqrt(jnp.mean(values_in * values_in, axis=-1, keepdims=True) + EPS) * gain
    )


def attention_body(
    nodes_ref, lengths_ref, lists_ref, counts_ref,
    *rest,
):
    out_ref, qkv_ref, k_all, v_all, held, sems, qkv_sems = rest[-7:]
    qkv_parts = rest[:4]
    info_ref, seg_ref, factor_ref, key_factor_ref = rest[4:8]
    parts = rest[8:-7]
    step = pl.program_id(0)
    group = step // 2
    tile = step % 2
    half_rows = out_ref.shape[1]
    rows = 2 * half_rows
    node_rows = k_all.shape[1]
    per_part = parts[0].shape[0]
    batch = held.shape[2] // node_rows

    def new_copies():
        for i, part in enumerate(qkv_parts):
            yield pltpu.make_async_copy(part, qkv_ref.at[i], qkv_sems.at[i])

    def cached_copies():
        for i, part in enumerate(parts):
            for j in range(per_part):
                yield pltpu.make_async_copy(
                    part.at[j, 0], k_all.at[i * per_part + j], sems.at[0, i, j]
                )
                yield pltpu.make_async_copy(
                    part.at[j, 1], v_all.at[i * per_part + j], sems.at[1, i, j]
                )

    @pl.when(step == 0)
    def _():
        for copy in new_copies():
            copy.start()
        for copy in cached_copies():
            copy.start()
        for copy in new_copies():
            copy.wait()

    nt = (((1,), (1,)), ((), ()))
    count = counts_ref[group, tile]

    def work(first):
        q = qkv_ref[group, first : first + half_rows, :]
        seen = first + half_rows
        middle = info_ref[0, first:seen, 0:1]
        root = info_ref[0, first:seen, 1:2]
        seg_col = info_ref[0, first:seen, 2:3]
        seg_row = seg_ref[0][:, :seen]
        row_at = lax.broadcasted_iota(jnp.int32, (half_rows, seen), 0) + first
        col_at = lax.broadcasted_iota(jnp.int32, (half_rows, seen), 1)
        key_at = lax.broadcasted_iota(jnp.int32, (1, node_rows), 1)
        scale = factor_ref[0, first:seen, 0:1] * (HD**-0.5 * LOG2E)
        near = lax.dot_general(q, qkv_ref[group, rows : rows + seen, :], nt, preferred_element_type=F32)
        near = near * scale * key_factor_ref[0][:, :seen]
        near = jnp.where((seg_col == seg_row) & (col_at <= row_at), near, NEG)
        top = jnp.max(near, axis=1, keepdims=True)

        if first == 0:
            @pl.when(step == 0)
            def _():
                for copy in cached_copies():
                    copy.wait()

        def score(i, top):
            best = None
            for j in range(batch):
                slot = lists_ref[group, tile, i * batch + j]
                node = nodes_ref[slot]
                length = jnp.where(i * batch + j < count, lengths_ref[slot], 0)
                s = lax.dot_general(q, k_all[slot], nt, preferred_element_type=F32) * scale
                shown = ((middle == node) | (root == node)) & (key_at < length)
                s = jnp.where(shown, s, NEG)
                held[i, :, j * node_rows : (j + 1) * node_rows] = s
                best = s if best is None else jnp.maximum(best, s)
            return jnp.maximum(top, jnp.max(best, axis=1, keepdims=True))

        batches = (count + batch - 1) // batch
        top = lax.fori_loop(0, batches, score, top)
        weights = jnp.exp2(near - top)
        total = jnp.sum(weights, axis=1, keepdims=True)
        summed = jnp.dot(weights.astype(BF), qkv_ref[group, 2 * rows : 2 * rows + seen, :], preferred_element_type=F32)

        def gather(i, carry):
            total, summed = carry
            added = None
            for j in range(batch):
                slot = lists_ref[group, tile, i * batch + j]
                w = jnp.exp2(held[i, :, j * node_rows : (j + 1) * node_rows] - top)
                added = w if added is None else added + w
                summed = summed + jnp.dot(
                    w.astype(BF), v_all[slot], preferred_element_type=F32
                )
            return total + jnp.sum(added, axis=1, keepdims=True), summed

        total, summed = lax.fori_loop(0, batches, gather, (total, summed))
        out_ref[0] = (summed / total).astype(BF)

    for t in range(2):
        @pl.when(tile == t)
        def _(t=t):
            work(t * half_rows)


def in_hbm(arrays):
    return [pltpu.with_memory_space_constraint(a, pltpu.MemorySpace.HBM) for a in arrays]


def attention(
    nodes, lengths, lists, counts, qkv_parts, row_info, seg_row, factors, key_factors, parts
):
    rows = row_info.shape[1]
    groups = len(qkv_parts)
    per_part, _, node_rows, _ = parts[0].shape
    slots = nodes.shape[0]
    batch = 4
    one = lambda shape: pl.BlockSpec((1,) + shape, lambda i, *_: (i // 2,) + (0,) * len(shape))
    return pl.pallas_call(
        attention_body,
        out_shape=jax.ShapeDtypeStruct((groups, rows, HD), BF),
        grid_spec=pltpu.PrefetchScalarGridSpec(
            num_scalar_prefetch=4,
            grid=(groups * 2,),
            in_specs=[pl.BlockSpec(memory_space=pltpu.MemorySpace.HBM)] * groups
            + [one((rows, 3)), one((1, rows)), one((rows, 2)), one((1, rows))]
            + [pl.BlockSpec(memory_space=pltpu.MemorySpace.HBM)] * len(parts),
            out_specs=pl.BlockSpec((1, rows // 2, HD), lambda i, *_: (i // 2, i % 2, 0)),
            scratch_shapes=[
                pltpu.VMEM((groups,) + qkv_parts[0].shape, BF),
                pltpu.VMEM((slots, node_rows, HD), BF),
                pltpu.VMEM((slots, node_rows, HD), BF),
                pltpu.VMEM((lists.shape[2] // batch, rows // 2, batch * node_rows), F32),
                pltpu.SemaphoreType.DMA((2, len(parts), per_part)),
                pltpu.SemaphoreType.DMA((groups,)),
            ],
        ),
        compiler_params=pltpu.CompilerParams(vmem_limit_bytes=32 << 20),
        cost_estimate=pl.CostEstimate(
            flops=2 * 10**9, transcendentals=4 * 10**6, bytes_accessed=6 * 10**6
        ),
    )(nodes, lengths, lists, counts, *in_hbm(qkv_parts), row_info, seg_row, factors, key_factors, *in_hbm(parts))


def feed_forward_body(tokens_ref, gu_a, dn_a, gu_b, dn_b, out_ref, tokens, gu, dn, made, sems):
    rows = 256
    blocks = tokens.shape[0] // rows

    def block(ref, i):
        return ref.at[pl.ds(i * rows, rows)]

    def fetch(i):
        return pltpu.make_async_copy(block(tokens_ref, i), block(tokens, i), sems.at[0, i])

    def store(i):
        return pltpu.make_async_copy(block(made, i), block(out_ref, i), sems.at[1, i])

    loads = [
        pltpu.make_async_copy(source, target, sems.at[2 + j, k])
        for k, pair in enumerate(((gu_a, dn_a), (gu_b, dn_b)))
        for j, (source, target) in enumerate(((pair[0], gu.at[k]), (pair[1], dn.at[k])))
    ]
    fetch(0).start()
    for load in loads:
        load.start()
    for i in range(1, blocks):
        fetch(i).start()
    for i in range(blocks):
        fetch(i).wait()
        part = 0.0
        for k in range(2):
            if i == 0:
                loads[2 * k].wait()
            values = tokens[i * rows : (i + 1) * rows, :]
            gate = jnp.dot(values, gu[k, 0], preferred_element_type=F32)
            up = jnp.dot(values, gu[k, 1], preferred_element_type=F32)
            hidden = (gate / (1.0 + jnp.exp(-gate)) * up).astype(BF)
            if i == 0:
                loads[2 * k + 1].wait()
            part = part + jnp.dot(hidden, dn[k], preferred_element_type=F32)
        made[i * rows : (i + 1) * rows, :] = part.astype(BF)
        store(i).start()
    for i in range(blocks):
        store(i).wait()


def feed_forward(tokens, weights):
    rows, width = tokens.shape
    units = weights[1].shape[0]
    return pl.pallas_call(
        feed_forward_body,
        out_shape=jax.ShapeDtypeStruct((rows, width), BF),
        in_specs=[pl.BlockSpec(memory_space=pltpu.MemorySpace.HBM)] * 5,
        out_specs=pl.BlockSpec(memory_space=pltpu.MemorySpace.HBM),
        scratch_shapes=[
            pltpu.VMEM((rows, width), BF),
            pltpu.VMEM((2, 2, width, units), BF),
            pltpu.VMEM((2, units, width), BF),
            pltpu.VMEM((rows, width), BF),
            pltpu.SemaphoreType.DMA((4, 2)),
        ],
        compiler_params=pltpu.CompilerParams(vmem_limit_bytes=48 << 20),
        cost_estimate=pl.CostEstimate(
            flops=2 * rows * width * units * 6,
            transcendentals=2 * rows * units,
            bytes_accessed=(2 * rows * width + 6 * width * units) * 2,
        ),
    )(tokens, *weights)


def on_device(
    states_in,
    w_qkv,
    qk_gain,
    w_out,
    post_gain,
    w_gate_up,
    w_down,
    cache_keys,
    cache_values,
    slot_node,
    node_length,
    node_parent,
    leaf_segment,
    leaf_node,
):
    yhi, x_at, z_at, ylo, core = (lax.axis_index(a) for a in ("yhi", "x", "z", "ylo", "core"))
    n_y, n_x, n_z = (lax.axis_size(a) for a in BLK)
    blk = (yhi * n_x + x_at) * n_z + z_at
    head_index = ylo * 2 + core
    rows = states_in.shape[0]
    heads_here = w_qkv.shape[2] // HD
    columns = w_qkv.shape[2] * 4

    corner = ("yhi", "z", "core")

    def across(values, s):
        pairs = [
            ((y * n_z + z) * 2 + c, (c * n_z + (z + s) % n_z) * 2 + y)
            for y in range(n_y) for z in range(n_z) for c in range(2)
        ]
        return lax.ppermute(values, corner, pairs)

    def head_piece(s):
        cut = ((z_at + s) % n_z) * HD
        return jnp.stack(
            [lax.dynamic_slice_in_dim(c[0], cut, HD, 1) for c in (cache_keys, cache_values)]
        )

    cached = jnp.stack([across(head_piece(s), s) for s in range(n_z)])
    slot_from = jnp.stack(
        [
            (jnp.where(c == 0, core, 1 - core) * n_x + x) * n_z + (z_at - sz) % n_z
            for c in range(2) for x in range(n_x) for sz in range(n_z)
        ]
    ).astype(jnp.int32)

    w_out = lax.dynamic_slice_in_dim(jnp.concatenate([w_out, w_out]), z_at * HD, w_out.shape[0], 0)

    def beside(weights):
        return lax.ppermute(
            weights, ("z", "core"),
            [(z * 2 + c, (z + 1 - 2 * c) % n_z * 2 + c) for z in range(n_z) for c in range(2)],
        )

    def beyond(weights):
        return lax.ppermute(
            weights, ("z", "core"), [(z * 2 + 1, (z + 2) % n_z * 2 + 1) for z in range(n_z)]
        )

    gu_a = beside(w_gate_up)

    qkv_raw = jnp.einsum("td,cdw->ctw", states_in, w_qkv, preferred_element_type=F32)
    squares = jnp.sum(qkv_raw[:2] * qkv_raw[:2], axis=2)
    cached_own = spread(cached, "x").reshape((n_x * n_z,) + cached.shape[1:])
    group_from = jnp.stack(
        [blk] + [(core * n_x + x_at) * n_z + (z_at - g) % n_z for g in range(n_z)]
    ).astype(jnp.int32)
    segments = jnp.take(leaf_segment, group_from, axis=0)
    middle, root, position = tree_info(
        segments, jnp.take(leaf_node, group_from, axis=0), node_parent, node_length
    )
    position, middle, root, segments = position[0], middle[1:], root[1:], segments[1:]
    half = HD // 2
    frequency = THETA ** (-2.0 * jnp.arange(half, dtype=F32) / HD)
    angles = position.astype(F32)[:, None] * frequency[None, :]
    cosine, sine = jnp.cos(angles)[:, None, :], jnp.sin(angles)[:, None, :]

    def turned(c):
        scaled = (qkv_raw[c] * qk_gain[c]).reshape(rows, heads_here, HD)
        low, high = scaled[..., :half], scaled[..., half:]
        both = jnp.concatenate([low * cosine - high * sine, high * cosine + low * sine], axis=-1)
        return both.astype(BF)

    terms = []
    left = squares
    for _ in range(3):
        terms.append(lax.reduce_precision(left, 8, 7))
        left = left - terms[-1]
    terms = jnp.stack(terms).reshape(-1, HD).astype(BF)
    term_rows = terms.shape[0]
    terms = jnp.pad(terms, ((0, -term_rows % 16), (0, 0)))
    qkv = jnp.stack(
        [turned(0), turned(1), qkv_raw[2].astype(BF).reshape(rows, heads_here, HD)]
    ).transpose(2, 0, 1, 3).reshape(heads_here, 3 * rows, HD)
    qkv = jnp.concatenate([qkv, jnp.broadcast_to(terms, (heads_here,) + terms.shape)], axis=1)
    qkv, gu_a = lax.optimization_barrier((qkv, gu_a))
    qkv_parts = [across(select_row(qkv, (z_at + s) % n_z), s) for s in range(n_z)]
    terms = jnp.stack([part[3 * rows : 3 * rows + term_rows] for part in qkv_parts]).astype(F32)
    squares = jnp.sum(terms.reshape(n_z, 3, 2, rows), axis=1).transpose(0, 2, 1)
    factors = lax.rsqrt(lax.psum(squares, ("yhi", "ylo")) / columns + EPS)
    w_gate_up, w_down, qkv_parts = lax.optimization_barrier((w_gate_up, w_down, qkv_parts))
    cached_own, qkv_parts = lax.optimization_barrier((cached_own, qkv_parts))
    cached_parts = [cached_own, shift(cached_own, "core", 1)]

    gu_b, dn_b = beyond(w_gate_up), beyond(w_down)

    slots = slot_from.shape[0]
    slot_nodes = jnp.take(slot_node, slot_from)
    slot_lengths = jnp.take(node_length, slot_nodes)
    halves = (n_z, 2, rows // 2, 1)
    needed = jnp.any(
        (middle.reshape(halves) == slot_nodes) | (root.reshape(halves) == slot_nodes), axis=2
    )
    before = jnp.arange(slots)[:, None] < jnp.arange(slots)[None, :]
    rank = jnp.sum(jnp.where(needed[..., :, None] & before, 1, 0), axis=2)
    longest = leaf_node.shape[1] + 4
    places = jnp.arange(longest, dtype=jnp.int32)
    lists = jnp.sum(
        jnp.where(
            needed[..., :, None] & (rank[..., :, None] == places),
            jnp.arange(slots, dtype=jnp.int32)[:, None], 0,
        ),
        axis=2,
    )
    counts = jnp.sum(needed.astype(jnp.int32), axis=2)
    row_info = jnp.stack([middle, root, segments], axis=-1)
    attended = attention(
        slot_nodes, slot_lengths, lists, counts, qkv_parts, row_info, segments[:, None, :],
        factors, factors[:, None, :, 1], cached_parts,
    )

    def back(values, s):
        pairs = [
            ((y * n_z + z) * 2 + c, (c * n_z + (z - s) % n_z) * 2 + y)
            for y in range(n_y) for z in range(n_z) for c in range(2)
        ]
        return lax.ppermute(values, corner, pairs)

    attended = jnp.concatenate([back(attended[s], s) for s in range(n_z)], axis=1)
    attended, gu_b, dn_b = lax.optimization_barrier((attended, gu_b, dn_b))
    attn_part = jnp.dot(attended, w_out, preferred_element_type=F32)
    attn_part = attn_part.reshape(2, 2, rows // 4, -1)

    def of_core(c):
        return lax.dynamic_index_in_dim(attn_part, c, 1, keepdims=False)

    attn_part = of_core(core) + shift(of_core(1 - core).astype(BF), "core", 1).astype(F32)
    attn_proj = select_row(attn_part, ylo) + shift(
        select_row(attn_part, 1 - ylo).astype(BF), "ylo", 1
    ).astype(F32)
    own_rows = rows // 4
    state_rows = lax.dynamic_slice_in_dim(states_in, head_index * own_rows, own_rows, 0)
    mid_state = (state_rows.astype(F32) + rms_norm(attn_proj, post_gain[0])).astype(BF)

    plane = ("yhi", "x")
    mid_state, w_down = lax.optimization_barrier((mid_state, w_down))
    dn_a = beside(w_down)
    tokens = spread(mid_state, plane)
    tokens, dn_a = lax.optimization_barrier((tokens, dn_a))
    weights = (
        gu_a, dn_a, jnp.where(core == 0, w_gate_up, gu_b), jnp.where(core == 0, w_down, dn_b)
    )
    flat = tokens.reshape(-1, tokens.shape[2])
    other = feed_forward(shift(flat, "core", 1), weights)
    total = feed_forward(flat, weights).astype(F32) + shift(other, "core", 1).astype(F32)
    total = lax.all_to_all(total.astype(BF).reshape(tokens.shape), plane, 0, 0, tiled=True)
    mlp_proj = jnp.sum(total.astype(F32), axis=0)
    return (mid_state.astype(F32) + rms_norm(mlp_proj, post_gain[1])).astype(BF)


def solution(mesh):
    fine = Mesh(mesh.devices.reshape(2, 4, 4, 2, 2), BLK + HEAD)
    placed = (
        P(BLK, None),
        P(None, None, HEAD),
        P(None, HEAD),
        P(HEAD, None),
        P(),
        P(None, None, BLK),
        P(BLK, None),
        P(BLK, None, HEAD),
        P(BLK, None, HEAD),
        P(),
        P(),
        P(),
        P(),
        P(),
    )
    return jax.shard_map(
        on_device, mesh=fine, in_specs=placed, out_specs=P(BLK + HEAD, None), check_vma=False
    )
```

```python
import functools

import jax
import jax.numpy as jnp
from jax import lax
from jax.experimental import pallas as pl
from jax.experimental.pallas import tpu as pltpu
from jax.sharding import Mesh, PartitionSpec as P

HD = 128
EPS = 1e-06
THETA = 500000.0
NEG = -1e30
LOG2E = 1.4426950408889634
BF = jnp.bfloat16
F32 = jnp.float32
BLK = ("yhi", "x", "z")
HEAD = ("ylo", "core")


def shift(values, axis, by):
    n = lax.axis_size(axis)
    return lax.ppermute(values, axis, [(i, (i + by) % n) for i in range(n)])


def spread(values, axes):
    n = 1
    for axis in (axes,) if isinstance(axes, str) else axes:
        n *= lax.axis_size(axis)
    copies = lax.optimization_barrier(jnp.broadcast_to(values, (n,) + values.shape))
    return lax.all_to_all(copies, axes, 0, 0, tiled=True)


def select_row(table, row):
    return lax.dynamic_index_in_dim(table, row, 0, keepdims=False)


def tree_info(leaf_segment, leaf_node, node_parent, node_length):
    groups, tok_rows = leaf_segment.shape
    leaf_count = leaf_node.shape[1]
    middles = node_parent.shape[0]
    all_nodes = node_length.shape[0]
    tenant_count = all_nodes - middles
    leaf_ids = jnp.arange(leaf_count, dtype=jnp.int32)
    onehot = (leaf_segment[:, :, None] == leaf_ids[None, None, :]).astype(jnp.int32)
    middle = jnp.sum(onehot * leaf_node[:, None, :], axis=-1)
    counts = jnp.sum(onehot, axis=1)
    starts = jnp.sum(jnp.where(leaf_ids[None, :] < leaf_ids[:, None], counts[:, None, :], 0), axis=-1)
    first_at = jnp.sum(onehot * starts[:, None, :], axis=-1)
    middle_ids = jnp.arange(middles, dtype=jnp.int32) + tenant_count
    root_node = jnp.sum(jnp.where(middle[..., None] == middle_ids, node_parent, 0), axis=-1)
    node_ids = jnp.arange(all_nodes, dtype=jnp.int32)
    len_middle = jnp.sum(jnp.where(middle[..., None] == node_ids, node_length, 0), axis=-1)
    len_root = jnp.sum(jnp.where(root_node[..., None] == node_ids, node_length, 0), axis=-1)
    offsets = jnp.arange(tok_rows, dtype=jnp.int32)[None, :] - first_at
    return middle, root_node, len_root + len_middle + offsets


def rms_norm(values_in, gain):
    return (
        values_in * lax.rsqrt(jnp.mean(values_in * values_in, axis=-1, keepdims=True) + EPS) * gain
    )


def attention_body(
    nodes_ref, lengths_ref, lists_ref, counts_ref,
    *rest,
):
    out_ref, qkv_ref, k_all, v_all, held, sems, qkv_sems = rest[-7:]
    qkv_parts = rest[:4]
    info_ref, seg_ref, factor_ref, key_factor_ref = rest[4:8]
    parts = rest[8:-7]
    step = pl.program_id(0)
    group = step // 2
    tile = step % 2
    half_rows = out_ref.shape[1]
    rows = 2 * half_rows
    node_rows = k_all.shape[1]
    per_part = parts[0].shape[0]
    batch = held.shape[2] // node_rows

    def new_copies():
        for i, part in enumerate(qkv_parts):
            yield pltpu.make_async_copy(part, qkv_ref.at[i], qkv_sems.at[i])

    def cached_copies():
        for i, part in enumerate(parts):
            for j in range(per_part):
                yield pltpu.make_async_copy(
                    part.at[j, 0], k_all.at[i * per_part + j], sems.at[0, i, j]
                )
                yield pltpu.make_async_copy(
                    part.at[j, 1], v_all.at[i * per_part + j], sems.at[1, i, j]
                )

    @pl.when(step == 0)
    def _():
        for copy in new_copies():
            copy.start()
        for copy in cached_copies():
            copy.start()
        for copy in new_copies():
            copy.wait()

    nt = (((1,), (1,)), ((), ()))
    count = counts_ref[group, tile]

    def work(first):
        q = qkv_ref[group, first : first + half_rows, :]
        seen = first + half_rows
        middle = info_ref[0, first:seen, 0:1]
        root = info_ref[0, first:seen, 1:2]
        seg_col = info_ref[0, first:seen, 2:3]
        seg_row = seg_ref[0][:, :seen]
        row_at = lax.broadcasted_iota(jnp.int32, (half_rows, seen), 0) + first
        col_at = lax.broadcasted_iota(jnp.int32, (half_rows, seen), 1)
        key_at = lax.broadcasted_iota(jnp.int32, (1, node_rows), 1)
        scale = factor_ref[0, first:seen, 0:1] * (HD**-0.5 * LOG2E)
        near = lax.dot_general(q, qkv_ref[group, rows : rows + seen, :], nt, preferred_element_type=F32)
        near = near * scale * key_factor_ref[0][:, :seen]
        near = jnp.where((seg_col == seg_row) & (col_at <= row_at), near, NEG)
        top = jnp.max(near, axis=1, keepdims=True)

        if first == 0:
            @pl.when(step == 0)
            def _():
                for copy in cached_copies():
                    copy.wait()

        def score(i, top):
            best = None
            for j in range(batch):
                slot = lists_ref[group, tile, i * batch + j]
                node = nodes_ref[slot]
                length = jnp.where(i * batch + j < count, lengths_ref[slot], 0)
                s = lax.dot_general(q, k_all[slot], nt, preferred_element_type=F32) * scale
                shown = ((middle == node) | (root == node)) & (key_at < length)
                s = jnp.where(shown, s, NEG)
                held[i, :, j * node_rows : (j + 1) * node_rows] = s
                best = s if best is None else jnp.maximum(best, s)
            return jnp.maximum(top, jnp.max(best, axis=1, keepdims=True))

        batches = (count + batch - 1) // batch
        top = lax.fori_loop(0, batches, score, top)
        weights = jnp.exp2(near - top)
        total = jnp.sum(weights, axis=1, keepdims=True)
        summed = jnp.dot(weights.astype(BF), qkv_ref[group, 2 * rows : 2 * rows + seen, :], preferred_element_type=F32)

        def gather(i, carry):
            total, summed = carry
            added = None
            for j in range(batch):
                slot = lists_ref[group, tile, i * batch + j]
                w = jnp.exp2(held[i, :, j * node_rows : (j + 1) * node_rows] - top)
                added = w if added is None else added + w
                summed = summed + jnp.dot(
                    w.astype(BF), v_all[slot], preferred_element_type=F32
                )
            return total + jnp.sum(added, axis=1, keepdims=True), summed

        total, summed = lax.fori_loop(0, batches, gather, (total, summed))
        out_ref[0] = (summed / total).astype(BF)

    for t in range(2):
        @pl.when(tile == t)
        def _(t=t):
            work(t * half_rows)


def in_hbm(arrays):
    return [pltpu.with_memory_space_constraint(a, pltpu.MemorySpace.HBM) for a in arrays]


def attention(
    nodes, lengths, lists, counts, qkv_parts, row_info, seg_row, factors, key_factors, parts
):
    rows = row_info.shape[1]
    groups = len(qkv_parts)
    per_part, _, node_rows, _ = parts[0].shape
    slots = nodes.shape[0]
    batch = 4
    one = lambda shape: pl.BlockSpec((1,) + shape, lambda i, *_: (i // 2,) + (0,) * len(shape))
    return pl.pallas_call(
        attention_body,
        out_shape=jax.ShapeDtypeStruct((groups, rows, HD), BF),
        grid_spec=pltpu.PrefetchScalarGridSpec(
            num_scalar_prefetch=4,
            grid=(groups * 2,),
            in_specs=[pl.BlockSpec(memory_space=pltpu.MemorySpace.HBM)] * groups
            + [one((rows, 3)), one((1, rows)), one((rows, 2)), one((1, rows))]
            + [pl.BlockSpec(memory_space=pltpu.MemorySpace.HBM)] * len(parts),
            out_specs=pl.BlockSpec((1, rows // 2, HD), lambda i, *_: (i // 2, i % 2, 0)),
            scratch_shapes=[
                pltpu.VMEM((groups,) + qkv_parts[0].shape, BF),
                pltpu.VMEM((slots, node_rows, HD), BF),
                pltpu.VMEM((slots, node_rows, HD), BF),
                pltpu.VMEM((lists.shape[2] // batch, rows // 2, batch * node_rows), F32),
                pltpu.SemaphoreType.DMA((2, len(parts), per_part)),
                pltpu.SemaphoreType.DMA((groups,)),
            ],
        ),
        compiler_params=pltpu.CompilerParams(vmem_limit_bytes=32 << 20),
        cost_estimate=pl.CostEstimate(
            flops=2 * 10**9, transcendentals=4 * 10**6, bytes_accessed=6 * 10**6
        ),
    )(nodes, lengths, lists, counts, *in_hbm(qkv_parts), row_info, seg_row, factors, key_factors, *in_hbm(parts))


def feed_forward_body(
    tokens_ref, gate_a, up_a, dn_a, gu_b, dn_b, out_ref, tokens, gu, dn, made, sems
):
    rows = 256
    blocks = tokens.shape[0] // rows

    def block(ref, i):
        return ref.at[pl.ds(i * rows, rows)]

    def fetch(i):
        return pltpu.make_async_copy(block(tokens_ref, i), block(tokens, i), sems.at[0, i])

    def store(i):
        return pltpu.make_async_copy(block(made, i), block(out_ref, i), sems.at[1, i])

    loads = [
        pltpu.make_async_copy(source, target, sems.at[2 + j, k])
        for k, parts in enumerate(((gate_a, up_a, dn_a), (gu_b.at[0], gu_b.at[1], dn_b)))
        for j, (source, target) in enumerate(zip(parts, (gu.at[k, 0], gu.at[k, 1], dn.at[k])))
    ]
    fetch(0).start()
    for load in loads:
        load.start()
    for i in range(1, blocks):
        fetch(i).start()
    for i in range(blocks):
        fetch(i).wait()
        part = 0.0
        for k in range(2):
            if i == 0:
                loads[3 * k].wait()
                loads[3 * k + 1].wait()
            values = tokens[i * rows : (i + 1) * rows, :]
            gate = jnp.dot(values, gu[k, 0], preferred_element_type=F32)
            up = jnp.dot(values, gu[k, 1], preferred_element_type=F32)
            hidden = (gate / (1.0 + jnp.exp(-gate)) * up).astype(BF)
            if i == 0:
                loads[3 * k + 2].wait()
            part = part + jnp.dot(hidden, dn[k], preferred_element_type=F32)
        made[i * rows : (i + 1) * rows, :] = part.astype(BF)
        store(i).start()
    for i in range(blocks):
        store(i).wait()


def feed_forward(tokens, weights):
    rows, width = tokens.shape
    units = weights[2].shape[0]
    return pl.pallas_call(
        feed_forward_body,
        out_shape=jax.ShapeDtypeStruct((rows, width), BF),
        in_specs=[pl.BlockSpec(memory_space=pltpu.MemorySpace.HBM)] * 6,
        out_specs=pl.BlockSpec(memory_space=pltpu.MemorySpace.HBM),
        scratch_shapes=[
            pltpu.VMEM((rows, width), BF),
            pltpu.VMEM((2, 2, width, units), BF),
            pltpu.VMEM((2, units, width), BF),
            pltpu.VMEM((rows, width), BF),
            pltpu.SemaphoreType.DMA((5, 2)),
        ],
        compiler_params=pltpu.CompilerParams(vmem_limit_bytes=48 << 20),
        cost_estimate=pl.CostEstimate(
            flops=2 * rows * width * units * 6,
            transcendentals=2 * rows * units,
            bytes_accessed=(2 * rows * width + 6 * width * units) * 2,
        ),
    )(tokens, *weights)


def on_device(
    states_in,
    w_qkv,
    qk_gain,
    w_out,
    post_gain,
    w_gate_up,
    w_down,
    cache_keys,
    cache_values,
    slot_node,
    node_length,
    node_parent,
    leaf_segment,
    leaf_node,
):
    yhi, x_at, z_at, ylo, core = (lax.axis_index(a) for a in ("yhi", "x", "z", "ylo", "core"))
    n_y, n_x, n_z = (lax.axis_size(a) for a in BLK)
    blk = (yhi * n_x + x_at) * n_z + z_at
    head_index = ylo * 2 + core
    rows = states_in.shape[0]
    heads_here = w_qkv.shape[2] // HD
    columns = w_qkv.shape[2] * 4

    corner = ("yhi", "z", "core")

    def across(values, s):
        pairs = [
            ((y * n_z + z) * 2 + c, (c * n_z + (z + s) % n_z) * 2 + y)
            for y in range(n_y) for z in range(n_z) for c in range(2)
        ]
        return lax.ppermute(values, corner, pairs)

    def head_piece(s):
        cut = ((z_at + s) % n_z) * HD
        return jnp.stack(
            [lax.dynamic_slice_in_dim(c[0], cut, HD, 1) for c in (cache_keys, cache_values)]
        )

    cached = jnp.stack([across(head_piece(s), s) for s in range(n_z)])
    slot_from = jnp.stack(
        [
            (jnp.where(c == 0, core, 1 - core) * n_x + x) * n_z + (z_at - sz) % n_z
            for c in range(2) for x in range(n_x) for sz in range(n_z)
        ]
    ).astype(jnp.int32)

    w_out = lax.dynamic_slice_in_dim(jnp.concatenate([w_out, w_out]), z_at * HD, w_out.shape[0], 0)

    def beside(weights):
        return lax.ppermute(
            weights, ("z", "core"),
            [(z * 2 + c, (z + 1 - 2 * c) % n_z * 2 + c) for z in range(n_z) for c in range(2)],
        )

    def beyond(weights):
        return lax.ppermute(
            weights, ("z", "core"), [(z * 2 + 1, (z + 2) % n_z * 2 + 1) for z in range(n_z)]
        )

    gate_a = beside(w_gate_up[0])

    qkv_raw = jnp.einsum("td,cdw->ctw", states_in, w_qkv, preferred_element_type=F32)
    squares = jnp.sum(qkv_raw[:2] * qkv_raw[:2], axis=2)
    cached_own = spread(cached, "x").reshape((n_x * n_z,) + cached.shape[1:])
    group_from = jnp.stack(
        [blk] + [(core * n_x + x_at) * n_z + (z_at - g) % n_z for g in range(n_z)]
    ).astype(jnp.int32)
    segments = jnp.take(leaf_segment, group_from, axis=0)
    middle, root, position = tree_info(
        segments, jnp.take(leaf_node, group_from, axis=0), node_parent, node_length
    )
    position, middle, root, segments = position[0], middle[1:], root[1:], segments[1:]
    half = HD // 2
    frequency = THETA ** (-2.0 * jnp.arange(half, dtype=F32) / HD)
    angles = position.astype(F32)[:, None] * frequency[None, :]
    cosine, sine = jnp.cos(angles)[:, None, :], jnp.sin(angles)[:, None, :]

    def turned(c):
        scaled = (qkv_raw[c] * qk_gain[c]).reshape(rows, heads_here, HD)
        low, high = scaled[..., :half], scaled[..., half:]
        both = jnp.concatenate([low * cosine - high * sine, high * cosine + low * sine], axis=-1)
        return both.astype(BF)

    terms = []
    left = squares
    for _ in range(3):
        terms.append(lax.reduce_precision(left, 8, 7))
        left = left - terms[-1]
    terms = jnp.stack(terms).reshape(-1, HD).astype(BF)
    term_rows = terms.shape[0]
    terms = jnp.pad(terms, ((0, -term_rows % 16), (0, 0)))
    qkv = jnp.stack(
        [turned(0), turned(1), qkv_raw[2].astype(BF).reshape(rows, heads_here, HD)]
    ).transpose(2, 0, 1, 3).reshape(heads_here, 3 * rows, HD)
    qkv = jnp.concatenate([qkv, jnp.broadcast_to(terms, (heads_here,) + terms.shape)], axis=1)
    qkv, gate_a = lax.optimization_barrier((qkv, gate_a))
    qkv_parts = [across(select_row(qkv, (z_at + s) % n_z), s) for s in range(n_z)]
    terms = jnp.stack([part[3 * rows : 3 * rows + term_rows] for part in qkv_parts]).astype(F32)
    squares = jnp.sum(terms.reshape(n_z, 3, 2, rows), axis=1).transpose(0, 2, 1)
    factors = lax.rsqrt(lax.psum(squares, ("yhi", "ylo")) / columns + EPS)
    w_gate_up, w_down, qkv_parts = lax.optimization_barrier((w_gate_up, w_down, qkv_parts))
    cached_own, qkv_parts = lax.optimization_barrier((cached_own, qkv_parts))
    cached_parts = [cached_own, shift(cached_own, "core", 1)]

    gu_b, dn_b = beyond(w_gate_up), beyond(w_down)

    slots = slot_from.shape[0]
    slot_nodes = jnp.take(slot_node, slot_from)
    slot_lengths = jnp.take(node_length, slot_nodes)
    halves = (n_z, 2, rows // 2, 1)
    needed = jnp.any(
        (middle.reshape(halves) == slot_nodes) | (root.reshape(halves) == slot_nodes), axis=2
    )
    before = jnp.arange(slots)[:, None] < jnp.arange(slots)[None, :]
    rank = jnp.sum(jnp.where(needed[..., :, None] & before, 1, 0), axis=2)
    longest = leaf_node.shape[1] + 4
    places = jnp.arange(longest, dtype=jnp.int32)
    lists = jnp.sum(
        jnp.where(
            needed[..., :, None] & (rank[..., :, None] == places),
            jnp.arange(slots, dtype=jnp.int32)[:, None], 0,
        ),
        axis=2,
    )
    counts = jnp.sum(needed.astype(jnp.int32), axis=2)
    row_info = jnp.stack([middle, root, segments], axis=-1)
    attended = attention(
        slot_nodes, slot_lengths, lists, counts, qkv_parts, row_info, segments[:, None, :],
        factors, factors[:, None, :, 1], cached_parts,
    )

    def back(values, s):
        pairs = [
            ((y * n_z + z) * 2 + c, (c * n_z + (z - s) % n_z) * 2 + y)
            for y in range(n_y) for z in range(n_z) for c in range(2)
        ]
        return lax.ppermute(values, corner, pairs)

    attended = jnp.concatenate([back(attended[s], s) for s in range(n_z)], axis=1)
    attended, gu_b, dn_b = lax.optimization_barrier((attended, gu_b, dn_b))
    attn_part = jnp.dot(attended, w_out, preferred_element_type=F32)
    attn_part = attn_part.reshape(2, 2, rows // 4, -1)

    def of_core(c):
        return lax.dynamic_index_in_dim(attn_part, c, 1, keepdims=False)

    attn_part = of_core(core) + shift(of_core(1 - core).astype(BF), "core", 1).astype(F32)
    attn_proj = select_row(attn_part, ylo) + shift(
        select_row(attn_part, 1 - ylo).astype(BF), "ylo", 1
    ).astype(F32)
    own_rows = rows // 4
    state_rows = lax.dynamic_slice_in_dim(states_in, head_index * own_rows, own_rows, 0)
    mid_state = (state_rows.astype(F32) + rms_norm(attn_proj, post_gain[0])).astype(BF)

    plane = ("yhi", "x")
    mid_state, w_down, w_gate_up = lax.optimization_barrier((mid_state, w_down, w_gate_up))
    up_a, dn_a = beside(w_gate_up[1]), beside(w_down)
    tokens = spread(mid_state, plane)
    tokens, up_a, dn_a = lax.optimization_barrier((tokens, up_a, dn_a))
    weights = (
        gate_a, up_a, dn_a, jnp.where(core == 0, w_gate_up, gu_b), jnp.where(core == 0, w_down, dn_b)
    )
    flat = tokens.reshape(-1, tokens.shape[2])
    other = feed_forward(shift(flat, "core", 1), weights)
    total = feed_forward(flat, weights).astype(F32) + shift(other, "core", 1).astype(F32)
    total = lax.all_to_all(total.astype(BF).reshape(tokens.shape), plane, 0, 0, tiled=True)
    mlp_proj = jnp.sum(total.astype(F32), axis=0)
    return (mid_state.astype(F32) + rms_norm(mlp_proj, post_gain[1])).astype(BF)


def solution(mesh):
    fine = Mesh(mesh.devices.reshape(2, 4, 4, 2, 2), BLK + HEAD)
    placed = (
        P(BLK, None),
        P(None, None, HEAD),
        P(None, HEAD),
        P(HEAD, None),
        P(),
        P(None, None, BLK),
        P(BLK, None),
        P(BLK, None, HEAD),
        P(BLK, None, HEAD),
        P(),
        P(),
        P(),
        P(),
        P(),
    )
    return jax.shard_map(
        on_device, mesh=fine, in_specs=placed, out_specs=P(BLK + HEAD, None), check_vma=False
    )
```

```python
import functools

import jax
import jax.numpy as jnp
from jax import lax
from jax.experimental import pallas as pl
from jax.experimental.pallas import tpu as pltpu
from jax.sharding import Mesh, PartitionSpec as P

HD = 128
EPS = 1e-06
THETA = 500000.0
NEG = -1e30
LOG2E = 1.4426950408889634
BF = jnp.bfloat16
F32 = jnp.float32
BLK = ("yhi", "x", "z")
HEAD = ("ylo", "core")


def shift(values, axis, by):
    n = lax.axis_size(axis)
    return lax.ppermute(values, axis, [(i, (i + by) % n) for i in range(n)])


def spread(values, axes):
    n = 1
    for axis in (axes,) if isinstance(axes, str) else axes:
        n *= lax.axis_size(axis)
    copies = lax.optimization_barrier(jnp.broadcast_to(values, (n,) + values.shape))
    return lax.all_to_all(copies, axes, 0, 0, tiled=True)


def select_row(table, row):
    return lax.dynamic_index_in_dim(table, row, 0, keepdims=False)


def tree_info(leaf_segment, leaf_node, node_parent, node_length):
    groups, tok_rows = leaf_segment.shape
    leaf_count = leaf_node.shape[1]
    middles = node_parent.shape[0]
    all_nodes = node_length.shape[0]
    tenant_count = all_nodes - middles
    leaf_ids = jnp.arange(leaf_count, dtype=jnp.int32)
    onehot = (leaf_segment[:, :, None] == leaf_ids[None, None, :]).astype(jnp.int32)
    middle = jnp.sum(onehot * leaf_node[:, None, :], axis=-1)
    counts = jnp.sum(onehot, axis=1)
    starts = jnp.sum(jnp.where(leaf_ids[None, :] < leaf_ids[:, None], counts[:, None, :], 0), axis=-1)
    first_at = jnp.sum(onehot * starts[:, None, :], axis=-1)
    middle_ids = jnp.arange(middles, dtype=jnp.int32) + tenant_count
    root_node = jnp.sum(jnp.where(middle[..., None] == middle_ids, node_parent, 0), axis=-1)
    node_ids = jnp.arange(all_nodes, dtype=jnp.int32)
    len_middle = jnp.sum(jnp.where(middle[..., None] == node_ids, node_length, 0), axis=-1)
    len_root = jnp.sum(jnp.where(root_node[..., None] == node_ids, node_length, 0), axis=-1)
    offsets = jnp.arange(tok_rows, dtype=jnp.int32)[None, :] - first_at
    return middle, root_node, len_root + len_middle + offsets


def rms_norm(values_in, gain):
    return (
        values_in * lax.rsqrt(jnp.mean(values_in * values_in, axis=-1, keepdims=True) + EPS) * gain
    )


def attention_body(
    nodes_ref, lengths_ref, lists_ref, counts_ref,
    *rest,
):
    out_ref, qkv_ref, k_all, v_all, held, sems, qkv_sems = rest[-7:]
    qkv_parts = rest[:4]
    info_ref, seg_ref, factor_ref, key_factor_ref = rest[4:8]
    parts = rest[8:-7]
    step = pl.program_id(0)
    group = step // 2
    tile = step % 2
    half_rows = out_ref.shape[1]
    rows = 2 * half_rows
    node_rows = k_all.shape[1]
    per_part = parts[0].shape[0]
    batch = held.shape[2] // node_rows

    def new_copies():
        for i, part in enumerate(qkv_parts):
            yield pltpu.make_async_copy(part, qkv_ref.at[i], qkv_sems.at[i])

    def cached_copies():
        for i, part in enumerate(parts):
            for j in range(per_part):
                yield pltpu.make_async_copy(
                    part.at[j, 0], k_all.at[i * per_part + j], sems.at[0, i, j]
                )
                yield pltpu.make_async_copy(
                    part.at[j, 1], v_all.at[i * per_part + j], sems.at[1, i, j]
                )

    @pl.when(step == 0)
    def _():
        for copy in new_copies():
            copy.start()
        for copy in cached_copies():
            copy.start()
        for copy in new_copies():
            copy.wait()

    nt = (((1,), (1,)), ((), ()))
    count = counts_ref[group, tile]

    def work(first):
        q = qkv_ref[group, first : first + half_rows, :]
        seen = first + half_rows
        middle = info_ref[0, first:seen, 0:1]
        root = info_ref[0, first:seen, 1:2]
        seg_col = info_ref[0, first:seen, 2:3]
        seg_row = seg_ref[0][:, :seen]
        row_at = lax.broadcasted_iota(jnp.int32, (half_rows, seen), 0) + first
        col_at = lax.broadcasted_iota(jnp.int32, (half_rows, seen), 1)
        key_at = lax.broadcasted_iota(jnp.int32, (1, node_rows), 1)
        scale = factor_ref[0, first:seen, 0:1] * (HD**-0.5 * LOG2E)
        near = lax.dot_general(q, qkv_ref[group, rows : rows + seen, :], nt, preferred_element_type=F32)
        near = near * scale * key_factor_ref[0][:, :seen]
        near = jnp.where((seg_col == seg_row) & (col_at <= row_at), near, NEG)
        top = jnp.max(near, axis=1, keepdims=True)

        if first == 0:
            @pl.when(step == 0)
            def _():
                for copy in cached_copies():
                    copy.wait()

        def score(i, top):
            best = None
            for j in range(batch):
                slot = lists_ref[group, tile, i * batch + j]
                node = nodes_ref[slot]
                length = jnp.where(i * batch + j < count, lengths_ref[slot], 0)
                s = lax.dot_general(q, k_all[slot], nt, preferred_element_type=F32) * scale
                shown = ((middle == node) | (root == node)) & (key_at < length)
                s = jnp.where(shown, s, NEG)
                held[i, :, j * node_rows : (j + 1) * node_rows] = s
                best = s if best is None else jnp.maximum(best, s)
            return jnp.maximum(top, jnp.max(best, axis=1, keepdims=True))

        batches = (count + batch - 1) // batch
        top = lax.fori_loop(0, batches, score, top)
        weights = jnp.exp2(near - top)
        total = jnp.sum(weights, axis=1, keepdims=True)
        summed = jnp.dot(weights.astype(BF), qkv_ref[group, 2 * rows : 2 * rows + seen, :], preferred_element_type=F32)

        def gather(i, carry):
            total, summed = carry
            added = None
            for j in range(batch):
                slot = lists_ref[group, tile, i * batch + j]
                w = jnp.exp2(held[i, :, j * node_rows : (j + 1) * node_rows] - top)
                added = w if added is None else added + w
                summed = summed + jnp.dot(
                    w.astype(BF), v_all[slot], preferred_element_type=F32
                )
            return total + jnp.sum(added, axis=1, keepdims=True), summed

        total, summed = lax.fori_loop(0, batches, gather, (total, summed))
        out_ref[0] = (summed / total).astype(BF)

    for t in range(2):
        @pl.when(tile == t)
        def _(t=t):
            work(t * half_rows)


def in_hbm(arrays):
    return [pltpu.with_memory_space_constraint(a, pltpu.MemorySpace.HBM) for a in arrays]


def attention(
    nodes, lengths, lists, counts, qkv_parts, row_info, seg_row, factors, key_factors, parts
):
    rows = row_info.shape[1]
    groups = len(qkv_parts)
    per_part, _, node_rows, _ = parts[0].shape
    slots = nodes.shape[0]
    batch = 4
    one = lambda shape: pl.BlockSpec((1,) + shape, lambda i, *_: (i // 2,) + (0,) * len(shape))
    return pl.pallas_call(
        attention_body,
        out_shape=jax.ShapeDtypeStruct((groups, rows, HD), BF),
        grid_spec=pltpu.PrefetchScalarGridSpec(
            num_scalar_prefetch=4,
            grid=(groups * 2,),
            in_specs=[pl.BlockSpec(memory_space=pltpu.MemorySpace.HBM)] * groups
            + [one((rows, 3)), one((1, rows)), one((rows, 2)), one((1, rows))]
            + [pl.BlockSpec(memory_space=pltpu.MemorySpace.HBM)] * len(parts),
            out_specs=pl.BlockSpec((1, rows // 2, HD), lambda i, *_: (i // 2, i % 2, 0)),
            scratch_shapes=[
                pltpu.VMEM((groups,) + qkv_parts[0].shape, BF),
                pltpu.VMEM((slots, node_rows, HD), BF),
                pltpu.VMEM((slots, node_rows, HD), BF),
                pltpu.VMEM((lists.shape[2] // batch, rows // 2, batch * node_rows), F32),
                pltpu.SemaphoreType.DMA((2, len(parts), per_part)),
                pltpu.SemaphoreType.DMA((groups,)),
            ],
        ),
        compiler_params=pltpu.CompilerParams(vmem_limit_bytes=32 << 20),
        cost_estimate=pl.CostEstimate(
            flops=2 * 10**9, transcendentals=4 * 10**6, bytes_accessed=6 * 10**6
        ),
    )(nodes, lengths, lists, counts, *in_hbm(qkv_parts), row_info, seg_row, factors, key_factors, *in_hbm(parts))


def feed_forward_body(tokens_ref, gu_a, dn_a, gu_b, dn_b, out_ref, tokens, gu, dn, made, sems):
    rows = 256
    blocks = tokens.shape[0] // rows

    def block(ref, i):
        return ref.at[pl.ds(i * rows, rows)]

    def fetch(i):
        return pltpu.make_async_copy(block(tokens_ref, i), block(tokens, i), sems.at[0, i])

    def store(i):
        return pltpu.make_async_copy(block(made, i), block(out_ref, i), sems.at[1, i])

    loads = [
        pltpu.make_async_copy(source, target, sems.at[2 + j, k])
        for k, pair in enumerate(((gu_a, dn_a), (gu_b, dn_b)))
        for j, (source, target) in enumerate(((pair[0], gu.at[k]), (pair[1], dn.at[k])))
    ]
    fetch(0).start()
    for load in loads:
        load.start()
    for i in range(1, blocks):
        fetch(i).start()
    for i in range(blocks):
        fetch(i).wait()
        part = 0.0
        for k in range(2):
            if i == 0:
                loads[2 * k].wait()
            values = tokens[i * rows : (i + 1) * rows, :]
            gate = jnp.dot(values, gu[k, 0], preferred_element_type=F32)
            up = jnp.dot(values, gu[k, 1], preferred_element_type=F32)
            hidden = (gate / (1.0 + jnp.exp(-gate)) * up).astype(BF)
            if i == 0:
                loads[2 * k + 1].wait()
            part = part + jnp.dot(hidden, dn[k], preferred_element_type=F32)
        made[i * rows : (i + 1) * rows, :] = part.astype(BF)
        store(i).start()
    for i in range(blocks):
        store(i).wait()


def feed_forward(tokens, weights):
    rows, width = tokens.shape
    units = weights[1].shape[0]
    return pl.pallas_call(
        feed_forward_body,
        out_shape=jax.ShapeDtypeStruct((rows, width), BF),
        in_specs=[pl.BlockSpec(memory_space=pltpu.MemorySpace.HBM)] * 5,
        out_specs=pl.BlockSpec(memory_space=pltpu.MemorySpace.HBM),
        scratch_shapes=[
            pltpu.VMEM((rows, width), BF),
            pltpu.VMEM((2, 2, width, units), BF),
            pltpu.VMEM((2, units, width), BF),
            pltpu.VMEM((rows, width), BF),
            pltpu.SemaphoreType.DMA((4, 2)),
        ],
        compiler_params=pltpu.CompilerParams(vmem_limit_bytes=48 << 20),
        cost_estimate=pl.CostEstimate(
            flops=2 * rows * width * units * 6,
            transcendentals=2 * rows * units,
            bytes_accessed=(2 * rows * width + 6 * width * units) * 2,
        ),
    )(tokens, *weights)


def on_device(
    states_in,
    w_qkv,
    qk_gain,
    w_out,
    post_gain,
    w_gate_up,
    w_down,
    cache_keys,
    cache_values,
    slot_node,
    node_length,
    node_parent,
    leaf_segment,
    leaf_node,
):
    yhi, x_at, z_at, ylo, core = (lax.axis_index(a) for a in ("yhi", "x", "z", "ylo", "core"))
    n_y, n_x, n_z = (lax.axis_size(a) for a in BLK)
    blk = (yhi * n_x + x_at) * n_z + z_at
    head_index = ylo * 2 + core
    rows = states_in.shape[0]
    heads_here = w_qkv.shape[2] // HD
    columns = w_qkv.shape[2] * 4

    corner = ("yhi", "z", "core")

    def across(values, s):
        pairs = [
            ((y * n_z + z) * 2 + c, (c * n_z + (z + s) % n_z) * 2 + y)
            for y in range(n_y) for z in range(n_z) for c in range(2)
        ]
        return lax.ppermute(values, corner, pairs)

    def head_piece(s):
        cut = ((z_at + s) % n_z) * HD
        return jnp.stack(
            [lax.dynamic_slice_in_dim(c[0], cut, HD, 1) for c in (cache_keys, cache_values)]
        )

    cached = jnp.stack([across(head_piece(s), s) for s in range(n_z)])
    slot_from = jnp.stack(
        [
            (jnp.where(c == 0, core, 1 - core) * n_x + x) * n_z + (z_at - sz) % n_z
            for c in range(2) for x in range(n_x) for sz in range(n_z)
        ]
    ).astype(jnp.int32)

    w_out = lax.dynamic_slice_in_dim(jnp.concatenate([w_out, w_out]), z_at * HD, w_out.shape[0], 0)

    def beside(weights):
        return lax.ppermute(
            weights, ("z", "core"),
            [(z * 2 + c, (z + 1 - 2 * c) % n_z * 2 + c) for z in range(n_z) for c in range(2)],
        )

    def beyond(weights):
        return lax.ppermute(
            weights, ("z", "core"), [(z * 2 + 1, (z + 2) % n_z * 2 + 1) for z in range(n_z)]
        )

    dn_a = beside(w_down)

    qkv_raw = jnp.einsum("td,cdw->ctw", states_in, w_qkv, preferred_element_type=F32)
    squares = jnp.sum(qkv_raw[:2] * qkv_raw[:2], axis=2)
    cached_own = spread(cached, "x").reshape((n_x * n_z,) + cached.shape[1:])
    group_from = jnp.stack(
        [blk] + [(core * n_x + x_at) * n_z + (z_at - g) % n_z for g in range(n_z)]
    ).astype(jnp.int32)
    segments = jnp.take(leaf_segment, group_from, axis=0)
    middle, root, position = tree_info(
        segments, jnp.take(leaf_node, group_from, axis=0), node_parent, node_length
    )
    position, middle, root, segments = position[0], middle[1:], root[1:], segments[1:]
    half = HD // 2
    frequency = THETA ** (-2.0 * jnp.arange(half, dtype=F32) / HD)
    angles = position.astype(F32)[:, None] * frequency[None, :]
    cosine, sine = jnp.cos(angles)[:, None, :], jnp.sin(angles)[:, None, :]

    def turned(c):
        scaled = (qkv_raw[c] * qk_gain[c]).reshape(rows, heads_here, HD)
        low, high = scaled[..., :half], scaled[..., half:]
        both = jnp.concatenate([low * cosine - high * sine, high * cosine + low * sine], axis=-1)
        return both.astype(BF)

    terms = []
    left = squares
    for _ in range(3):
        terms.append(lax.reduce_precision(left, 8, 7))
        left = left - terms[-1]
    terms = jnp.stack(terms).reshape(-1, HD).astype(BF)
    term_rows = terms.shape[0]
    terms = jnp.pad(terms, ((0, -term_rows % 16), (0, 0)))
    qkv = jnp.stack(
        [turned(0), turned(1), qkv_raw[2].astype(BF).reshape(rows, heads_here, HD)]
    ).transpose(2, 0, 1, 3).reshape(heads_here, 3 * rows, HD)
    qkv = jnp.concatenate([qkv, jnp.broadcast_to(terms, (heads_here,) + terms.shape)], axis=1)
    qkv, dn_a = lax.optimization_barrier((qkv, dn_a))
    qkv_parts = [across(select_row(qkv, (z_at + s) % n_z), s) for s in range(n_z)]
    terms = jnp.stack([part[3 * rows : 3 * rows + term_rows] for part in qkv_parts]).astype(F32)
    squares = jnp.sum(terms.reshape(n_z, 3, 2, rows), axis=1).transpose(0, 2, 1)
    factors = lax.rsqrt(lax.psum(squares, ("yhi", "ylo")) / columns + EPS)
    w_gate_up, w_down, qkv_parts = lax.optimization_barrier((w_gate_up, w_down, qkv_parts))
    cached_own, factors = lax.optimization_barrier((cached_own, factors))
    cached_parts = [cached_own, shift(cached_own, "core", 1)]

    gu_b, dn_b = beyond(w_gate_up), beyond(w_down)

    slots = slot_from.shape[0]
    slot_nodes = jnp.take(slot_node, slot_from)
    slot_lengths = jnp.take(node_length, slot_nodes)
    halves = (n_z, 2, rows // 2, 1)
    needed = jnp.any(
        (middle.reshape(halves) == slot_nodes) | (root.reshape(halves) == slot_nodes), axis=2
    )
    before = jnp.arange(slots)[:, None] < jnp.arange(slots)[None, :]
    rank = jnp.sum(jnp.where(needed[..., :, None] & before, 1, 0), axis=2)
    longest = leaf_node.shape[1] + 4
    places = jnp.arange(longest, dtype=jnp.int32)
    lists = jnp.sum(
        jnp.where(
            needed[..., :, None] & (rank[..., :, None] == places),
            jnp.arange(slots, dtype=jnp.int32)[:, None], 0,
        ),
        axis=2,
    )
    counts = jnp.sum(needed.astype(jnp.int32), axis=2)
    row_info = jnp.stack([middle, root, segments], axis=-1)
    attended = attention(
        slot_nodes, slot_lengths, lists, counts, qkv_parts, row_info, segments[:, None, :],
        factors, factors[:, None, :, 1], cached_parts,
    )

    def back(values, s):
        pairs = [
            ((y * n_z + z) * 2 + c, (c * n_z + (z - s) % n_z) * 2 + y)
            for y in range(n_y) for z in range(n_z) for c in range(2)
        ]
        return lax.ppermute(values, corner, pairs)

    attended = jnp.concatenate([back(attended[s], s) for s in range(n_z)], axis=1)
    attended, gu_b, dn_b = lax.optimization_barrier((attended, gu_b, dn_b))
    attn_part = jnp.dot(attended, w_out, preferred_element_type=F32)
    attn_part = attn_part.reshape(2, 2, rows // 4, -1)

    def of_core(c):
        return lax.dynamic_index_in_dim(attn_part, c, 1, keepdims=False)

    attn_part = of_core(core) + shift(of_core(1 - core).astype(BF), "core", 1).astype(F32)
    attn_proj = select_row(attn_part, ylo) + shift(
        select_row(attn_part, 1 - ylo).astype(BF), "ylo", 1
    ).astype(F32)
    own_rows = rows // 4
    state_rows = lax.dynamic_slice_in_dim(states_in, head_index * own_rows, own_rows, 0)
    mid_state = (state_rows.astype(F32) + rms_norm(attn_proj, post_gain[0])).astype(BF)

    plane = ("yhi", "x")
    mid_state, w_gate_up = lax.optimization_barrier((mid_state, w_gate_up))
    gu_a = beside(w_gate_up)
    tokens = spread(mid_state, plane)
    tokens, gu_a = lax.optimization_barrier((tokens, gu_a))
    weights = (
        gu_a, dn_a, jnp.where(core == 0, w_gate_up, gu_b), jnp.where(core == 0, w_down, dn_b)
    )
    flat = tokens.reshape(-1, tokens.shape[2])
    other = feed_forward(shift(flat, "core", 1), weights)
    total = feed_forward(flat, weights).astype(F32) + shift(other, "core", 1).astype(F32)
    total = lax.all_to_all(total.astype(BF).reshape(tokens.shape), plane, 0, 0, tiled=True)
    mlp_proj = jnp.sum(total.astype(F32), axis=0)
    return (mid_state.astype(F32) + rms_norm(mlp_proj, post_gain[1])).astype(BF)


def solution(mesh):
    fine = Mesh(mesh.devices.reshape(2, 4, 4, 2, 2), BLK + HEAD)
    placed = (
        P(BLK, None),
        P(None, None, HEAD),
        P(None, HEAD),
        P(HEAD, None),
        P(),
        P(None, None, BLK),
        P(BLK, None),
        P(BLK, None, HEAD),
        P(BLK, None, HEAD),
        P(),
        P(),
        P(),
        P(),
        P(),
    )
    return jax.shard_map(
        on_device, mesh=fine, in_specs=placed, out_specs=P(BLK + HEAD, None), check_vma=False
    )
```

```python
import functools

import jax
import jax.numpy as jnp
from jax import lax
from jax.experimental import pallas as pl
from jax.experimental.pallas import tpu as pltpu
from jax.sharding import Mesh, PartitionSpec as P

HD = 128
EPS = 1e-06
THETA = 500000.0
NEG = -1e30
LOG2E = 1.4426950408889634
BF = jnp.bfloat16
F32 = jnp.float32
BLK = ("yhi", "x", "z")
HEAD = ("ylo", "core")


def shift(values, axis, by):
    n = lax.axis_size(axis)
    return lax.ppermute(values, axis, [(i, (i + by) % n) for i in range(n)])


def spread(values, axes):
    n = 1
    for axis in (axes,) if isinstance(axes, str) else axes:
        n *= lax.axis_size(axis)
    copies = lax.optimization_barrier(jnp.broadcast_to(values, (n,) + values.shape))
    return lax.all_to_all(copies, axes, 0, 0, tiled=True)


def select_row(table, row):
    return lax.dynamic_index_in_dim(table, row, 0, keepdims=False)


def tree_info(leaf_segment, leaf_node, node_parent, node_length):
    groups, tok_rows = leaf_segment.shape
    leaf_count = leaf_node.shape[1]
    middles = node_parent.shape[0]
    all_nodes = node_length.shape[0]
    tenant_count = all_nodes - middles
    leaf_ids = jnp.arange(leaf_count, dtype=jnp.int32)
    onehot = (leaf_segment[:, :, None] == leaf_ids[None, None, :]).astype(jnp.int32)
    middle = jnp.sum(onehot * leaf_node[:, None, :], axis=-1)
    counts = jnp.sum(onehot, axis=1)
    starts = jnp.sum(jnp.where(leaf_ids[None, :] < leaf_ids[:, None], counts[:, None, :], 0), axis=-1)
    first_at = jnp.sum(onehot * starts[:, None, :], axis=-1)
    middle_ids = jnp.arange(middles, dtype=jnp.int32) + tenant_count
    root_node = jnp.sum(jnp.where(middle[..., None] == middle_ids, node_parent, 0), axis=-1)
    node_ids = jnp.arange(all_nodes, dtype=jnp.int32)
    len_middle = jnp.sum(jnp.where(middle[..., None] == node_ids, node_length, 0), axis=-1)
    len_root = jnp.sum(jnp.where(root_node[..., None] == node_ids, node_length, 0), axis=-1)
    offsets = jnp.arange(tok_rows, dtype=jnp.int32)[None, :] - first_at
    return middle, root_node, len_root + len_middle + offsets


def rms_norm(values_in, gain):
    return (
        values_in * lax.rsqrt(jnp.mean(values_in * values_in, axis=-1, keepdims=True) + EPS) * gain
    )


def attention_body(
    nodes_ref, lengths_ref, lists_ref, counts_ref,
    *rest,
):
    out_ref, qkv_ref, k_all, v_all, held, sems, qkv_sems = rest[-7:]
    qkv_parts = rest[:4]
    info_ref, seg_ref, factor_ref, key_factor_ref = rest[4:8]
    parts = rest[8:-7]
    step = pl.program_id(0)
    group = step // 2
    tile = step % 2
    half_rows = out_ref.shape[1]
    rows = 2 * half_rows
    node_rows = k_all.shape[1]
    per_part = parts[0].shape[0]
    batch = held.shape[2] // node_rows

    def new_copies():
        for i, part in enumerate(qkv_parts):
            yield pltpu.make_async_copy(part, qkv_ref.at[i], qkv_sems.at[i])

    def cached_copies():
        for i, part in enumerate(parts):
            for j in range(per_part):
                yield pltpu.make_async_copy(
                    part.at[j, 0], k_all.at[i * per_part + j], sems.at[0, i, j]
                )
                yield pltpu.make_async_copy(
                    part.at[j, 1], v_all.at[i * per_part + j], sems.at[1, i, j]
                )

    @pl.when(step == 0)
    def _():
        for copy in new_copies():
            copy.start()
        for copy in cached_copies():
            copy.start()
        for copy in new_copies():
            copy.wait()

    nt = (((1,), (1,)), ((), ()))
    count = counts_ref[group, tile]

    def work(first):
        q = qkv_ref[group, first : first + half_rows, :]
        seen = first + half_rows
        middle = info_ref[0, first:seen, 0:1]
        root = info_ref[0, first:seen, 1:2]
        seg_col = info_ref[0, first:seen, 2:3]
        seg_row = seg_ref[0][:, :seen]
        row_at = lax.broadcasted_iota(jnp.int32, (half_rows, seen), 0) + first
        col_at = lax.broadcasted_iota(jnp.int32, (half_rows, seen), 1)
        key_at = lax.broadcasted_iota(jnp.int32, (1, node_rows), 1)
        scale = factor_ref[0, first:seen, 0:1] * (HD**-0.5 * LOG2E)
        near = lax.dot_general(q, qkv_ref[group, rows : rows + seen, :], nt, preferred_element_type=F32)
        near = near * scale * key_factor_ref[0][:, :seen]
        near = jnp.where((seg_col == seg_row) & (col_at <= row_at), near, NEG)
        top = jnp.max(near, axis=1, keepdims=True)

        if first == 0:
            @pl.when(step == 0)
            def _():
                for copy in cached_copies():
                    copy.wait()

        def score(i, top):
            best = None
            for j in range(batch):
                slot = lists_ref[group, tile, i * batch + j]
                node = nodes_ref[slot]
                length = jnp.where(i * batch + j < count, lengths_ref[slot], 0)
                s = lax.dot_general(q, k_all[slot], nt, preferred_element_type=F32) * scale
                shown = ((middle == node) | (root == node)) & (key_at < length)
                s = jnp.where(shown, s, NEG)
                held[i, :, j * node_rows : (j + 1) * node_rows] = s
                best = s if best is None else jnp.maximum(best, s)
            return jnp.maximum(top, jnp.max(best, axis=1, keepdims=True))

        batches = (count + batch - 1) // batch
        top = lax.fori_loop(0, batches, score, top)
        weights = jnp.exp2(near - top)
        total = jnp.sum(weights, axis=1, keepdims=True)
        summed = jnp.dot(weights.astype(BF), qkv_ref[group, 2 * rows : 2 * rows + seen, :], preferred_element_type=F32)

        def gather(i, carry):
            total, summed = carry
            added = None
            for j in range(batch):
                slot = lists_ref[group, tile, i * batch + j]
                w = jnp.exp2(held[i, :, j * node_rows : (j + 1) * node_rows] - top)
                added = w if added is None else added + w
                summed = summed + jnp.dot(
                    w.astype(BF), v_all[slot], preferred_element_type=F32
                )
            return total + jnp.sum(added, axis=1, keepdims=True), summed

        total, summed = lax.fori_loop(0, batches, gather, (total, summed))
        out_ref[0] = (summed / total).astype(BF)

    for t in range(2):
        @pl.when(tile == t)
        def _(t=t):
            work(t * half_rows)


def in_hbm(arrays):
    return [pltpu.with_memory_space_constraint(a, pltpu.MemorySpace.HBM) for a in arrays]


def attention(
    nodes, lengths, lists, counts, qkv_parts, row_info, seg_row, factors, key_factors, parts
):
    rows = row_info.shape[1]
    groups = len(qkv_parts)
    per_part, _, node_rows, _ = parts[0].shape
    slots = nodes.shape[0]
    batch = 4
    one = lambda shape: pl.BlockSpec((1,) + shape, lambda i, *_: (i // 2,) + (0,) * len(shape))
    return pl.pallas_call(
        attention_body,
        out_shape=jax.ShapeDtypeStruct((groups, rows, HD), BF),
        grid_spec=pltpu.PrefetchScalarGridSpec(
            num_scalar_prefetch=4,
            grid=(groups * 2,),
            in_specs=[pl.BlockSpec(memory_space=pltpu.MemorySpace.HBM)] * groups
            + [one((rows, 3)), one((1, rows)), one((rows, 2)), one((1, rows))]
            + [pl.BlockSpec(memory_space=pltpu.MemorySpace.HBM)] * len(parts),
            out_specs=pl.BlockSpec((1, rows // 2, HD), lambda i, *_: (i // 2, i % 2, 0)),
            scratch_shapes=[
                pltpu.VMEM((groups,) + qkv_parts[0].shape, BF),
                pltpu.VMEM((slots, node_rows, HD), BF),
                pltpu.VMEM((slots, node_rows, HD), BF),
                pltpu.VMEM((lists.shape[2] // batch, rows // 2, batch * node_rows), F32),
                pltpu.SemaphoreType.DMA((2, len(parts), per_part)),
                pltpu.SemaphoreType.DMA((groups,)),
            ],
        ),
        compiler_params=pltpu.CompilerParams(vmem_limit_bytes=32 << 20),
        cost_estimate=pl.CostEstimate(
            flops=2 * 10**9, transcendentals=4 * 10**6, bytes_accessed=6 * 10**6
        ),
    )(nodes, lengths, lists, counts, *in_hbm(qkv_parts), row_info, seg_row, factors, key_factors, *in_hbm(parts))


def feed_forward_body(
    core_ref, tokens_ref, gu_a, dn_a, gu_own, dn_own, gu_far, dn_far, out_ref,
    tokens, gu, dn, made, sems,
):
    rows = 256
    blocks = tokens.shape[0] // rows

    def block(ref, i):
        return ref.at[pl.ds(i * rows, rows)]

    def fetch(i):
        return pltpu.make_async_copy(block(tokens_ref, i), block(tokens, i), sems.at[0, i])

    def store(i):
        return pltpu.make_async_copy(block(made, i), block(out_ref, i), sems.at[1, i])

    def share(k, gu_ref, dn_ref):
        return [
            pltpu.make_async_copy(gu_ref, gu.at[k], sems.at[2, k]),
            pltpu.make_async_copy(dn_ref, dn.at[k], sems.at[3, k]),
        ]

    loads = share(0, gu_a, dn_a) + share(1, gu_far, dn_far)
    fetch(0).start()
    for load in share(0, gu_a, dn_a):
        load.start()

    @pl.when(core_ref[0] == 0)
    def _():
        for load in share(1, gu_own, dn_own):
            load.start()

    @pl.when(core_ref[0] != 0)
    def _():
        for load in share(1, gu_far, dn_far):
            load.start()

    for i in range(1, blocks):
        fetch(i).start()
    for i in range(blocks):
        fetch(i).wait()
        part = 0.0
        for k in range(2):
            if i == 0:
                loads[2 * k].wait()
            values = tokens[i * rows : (i + 1) * rows, :]
            gate = jnp.dot(values, gu[k, 0], preferred_element_type=F32)
            up = jnp.dot(values, gu[k, 1], preferred_element_type=F32)
            hidden = (gate / (1.0 + jnp.exp(-gate)) * up).astype(BF)
            if i == 0:
                loads[2 * k + 1].wait()
            part = part + jnp.dot(hidden, dn[k], preferred_element_type=F32)
        made[i * rows : (i + 1) * rows, :] = part.astype(BF)
        store(i).start()
    for i in range(blocks):
        store(i).wait()


def feed_forward(core, tokens, weights):
    rows, width = tokens.shape
    units = weights[1].shape[0]
    return pl.pallas_call(
        feed_forward_body,
        out_shape=jax.ShapeDtypeStruct((rows, width), BF),
        in_specs=[pl.BlockSpec(memory_space=pltpu.MemorySpace.SMEM)]
        + [pl.BlockSpec(memory_space=pltpu.MemorySpace.HBM)] * 7,
        out_specs=pl.BlockSpec(memory_space=pltpu.MemorySpace.HBM),
        scratch_shapes=[
            pltpu.VMEM((rows, width), BF),
            pltpu.VMEM((2, 2, width, units), BF),
            pltpu.VMEM((2, units, width), BF),
            pltpu.VMEM((rows, width), BF),
            pltpu.SemaphoreType.DMA((4, 2)),
        ],
        compiler_params=pltpu.CompilerParams(vmem_limit_bytes=48 << 20),
        cost_estimate=pl.CostEstimate(
            flops=2 * rows * width * units * 6,
            transcendentals=2 * rows * units,
            bytes_accessed=(2 * rows * width + 6 * width * units) * 2,
        ),
    )(core, tokens, *weights)


def on_device(
    states_in,
    w_qkv,
    qk_gain,
    w_out,
    post_gain,
    w_gate_up,
    w_down,
    cache_keys,
    cache_values,
    slot_node,
    node_length,
    node_parent,
    leaf_segment,
    leaf_node,
):
    yhi, x_at, z_at, ylo, core = (lax.axis_index(a) for a in ("yhi", "x", "z", "ylo", "core"))
    n_y, n_x, n_z = (lax.axis_size(a) for a in BLK)
    blk = (yhi * n_x + x_at) * n_z + z_at
    head_index = ylo * 2 + core
    rows = states_in.shape[0]
    heads_here = w_qkv.shape[2] // HD
    columns = w_qkv.shape[2] * 4

    corner = ("yhi", "z", "core")

    def across(values, s):
        pairs = [
            ((y * n_z + z) * 2 + c, (c * n_z + (z + s) % n_z) * 2 + y)
            for y in range(n_y) for z in range(n_z) for c in range(2)
        ]
        return lax.ppermute(values, corner, pairs)

    def head_piece(s):
        cut = ((z_at + s) % n_z) * HD
        return jnp.stack(
            [lax.dynamic_slice_in_dim(c[0], cut, HD, 1) for c in (cache_keys, cache_values)]
        )

    cached = jnp.stack([across(head_piece(s), s) for s in range(n_z)])
    slot_from = jnp.stack(
        [
            (jnp.where(c == 0, core, 1 - core) * n_x + x) * n_z + (z_at - sz) % n_z
            for c in range(2) for x in range(n_x) for sz in range(n_z)
        ]
    ).astype(jnp.int32)

    w_out = lax.dynamic_slice_in_dim(jnp.concatenate([w_out, w_out]), z_at * HD, w_out.shape[0], 0)

    def beside(weights):
        return lax.ppermute(
            weights, ("z", "core"),
            [(z * 2 + c, (z + 1 - 2 * c) % n_z * 2 + c) for z in range(n_z) for c in range(2)],
        )

    def beyond(weights):
        return lax.ppermute(
            weights, ("z", "core"), [(z * 2 + 1, (z + 2) % n_z * 2 + 1) for z in range(n_z)]
        )

    dn_a = beside(w_down)

    qkv_raw = jnp.einsum("td,cdw->ctw", states_in, w_qkv, preferred_element_type=F32)
    squares = jnp.sum(qkv_raw[:2] * qkv_raw[:2], axis=2)
    cached_own = spread(cached, "x").reshape((n_x * n_z,) + cached.shape[1:])
    group_from = jnp.stack(
        [blk] + [(core * n_x + x_at) * n_z + (z_at - g) % n_z for g in range(n_z)]
    ).astype(jnp.int32)
    segments = jnp.take(leaf_segment, group_from, axis=0)
    middle, root, position = tree_info(
        segments, jnp.take(leaf_node, group_from, axis=0), node_parent, node_length
    )
    position, middle, root, segments = position[0], middle[1:], root[1:], segments[1:]
    half = HD // 2
    frequency = THETA ** (-2.0 * jnp.arange(half, dtype=F32) / HD)
    angles = position.astype(F32)[:, None] * frequency[None, :]
    cosine, sine = jnp.cos(angles)[:, None, :], jnp.sin(angles)[:, None, :]

    def turned(c):
        scaled = (qkv_raw[c] * qk_gain[c]).reshape(rows, heads_here, HD)
        low, high = scaled[..., :half], scaled[..., half:]
        both = jnp.concatenate([low * cosine - high * sine, high * cosine + low * sine], axis=-1)
        return both.astype(BF)

    terms = []
    left = squares
    for _ in range(3):
        terms.append(lax.reduce_precision(left, 8, 7))
        left = left - terms[-1]
    terms = jnp.stack(terms).reshape(-1, HD).astype(BF)
    term_rows = terms.shape[0]
    terms = jnp.pad(terms, ((0, -term_rows % 16), (0, 0)))
    qkv = jnp.stack(
        [turned(0), turned(1), qkv_raw[2].astype(BF).reshape(rows, heads_here, HD)]
    ).transpose(2, 0, 1, 3).reshape(heads_here, 3 * rows, HD)
    qkv = jnp.concatenate([qkv, jnp.broadcast_to(terms, (heads_here,) + terms.shape)], axis=1)
    qkv, dn_a = lax.optimization_barrier((qkv, dn_a))
    qkv_parts = [across(select_row(qkv, (z_at + s) % n_z), s) for s in range(n_z)]
    terms = jnp.stack([part[3 * rows : 3 * rows + term_rows] for part in qkv_parts]).astype(F32)
    squares = jnp.sum(terms.reshape(n_z, 3, 2, rows), axis=1).transpose(0, 2, 1)
    factors = lax.rsqrt(lax.psum(squares, ("yhi", "ylo")) / columns + EPS)
    w_gate_up, w_down, qkv_parts = lax.optimization_barrier((w_gate_up, w_down, qkv_parts))
    cached_own, factors = lax.optimization_barrier((cached_own, factors))
    cached_parts = [cached_own, shift(cached_own, "core", 1)]

    gu_b, dn_b = beyond(w_gate_up), beyond(w_down)

    slots = slot_from.shape[0]
    slot_nodes = jnp.take(slot_node, slot_from)
    slot_lengths = jnp.take(node_length, slot_nodes)
    halves = (n_z, 2, rows // 2, 1)
    needed = jnp.any(
        (middle.reshape(halves) == slot_nodes) | (root.reshape(halves) == slot_nodes), axis=2
    )
    before = jnp.arange(slots)[:, None] < jnp.arange(slots)[None, :]
    rank = jnp.sum(jnp.where(needed[..., :, None] & before, 1, 0), axis=2)
    longest = leaf_node.shape[1] + 4
    places = jnp.arange(longest, dtype=jnp.int32)
    lists = jnp.sum(
        jnp.where(
            needed[..., :, None] & (rank[..., :, None] == places),
            jnp.arange(slots, dtype=jnp.int32)[:, None], 0,
        ),
        axis=2,
    )
    counts = jnp.sum(needed.astype(jnp.int32), axis=2)
    row_info = jnp.stack([middle, root, segments], axis=-1)
    attended = attention(
        slot_nodes, slot_lengths, lists, counts, qkv_parts, row_info, segments[:, None, :],
        factors, factors[:, None, :, 1], cached_parts,
    )

    def back(values, s):
        pairs = [
            ((y * n_z + z) * 2 + c, (c * n_z + (z - s) % n_z) * 2 + y)
            for y in range(n_y) for z in range(n_z) for c in range(2)
        ]
        return lax.ppermute(values, corner, pairs)

    attended = jnp.concatenate([back(attended[s], s) for s in range(n_z)], axis=1)
    attended, gu_b, dn_b = lax.optimization_barrier((attended, gu_b, dn_b))
    attn_part = jnp.dot(attended, w_out, preferred_element_type=F32)
    attn_part = attn_part.reshape(2, 2, rows // 4, -1)

    def of_core(c):
        return lax.dynamic_index_in_dim(attn_part, c, 1, keepdims=False)

    attn_part = of_core(core) + shift(of_core(1 - core).astype(BF), "core", 1).astype(F32)
    attn_proj = select_row(attn_part, ylo) + shift(
        select_row(attn_part, 1 - ylo).astype(BF), "ylo", 1
    ).astype(F32)
    own_rows = rows // 4
    state_rows = lax.dynamic_slice_in_dim(states_in, head_index * own_rows, own_rows, 0)
    mid_state = (state_rows.astype(F32) + rms_norm(attn_proj, post_gain[0])).astype(BF)

    plane = ("yhi", "x")
    mid_state, w_gate_up = lax.optimization_barrier((mid_state, w_gate_up))
    gu_a = beside(w_gate_up)
    tokens = spread(mid_state, plane)
    tokens, gu_a = lax.optimization_barrier((tokens, gu_a))
    weights = (gu_a, dn_a, w_gate_up, w_down, gu_b, dn_b)
    core_at = core.astype(jnp.int32).reshape(1)
    flat = tokens.reshape(-1, tokens.shape[2])
    other = feed_forward(core_at, shift(flat, "core", 1), weights)
    total = feed_forward(core_at, flat, weights).astype(F32) + shift(other, "core", 1).astype(F32)
    total = lax.all_to_all(total.astype(BF).reshape(tokens.shape), plane, 0, 0, tiled=True)
    mlp_proj = jnp.sum(total.astype(F32), axis=0)
    return (mid_state.astype(F32) + rms_norm(mlp_proj, post_gain[1])).astype(BF)


def solution(mesh):
    fine = Mesh(mesh.devices.reshape(2, 4, 4, 2, 2), BLK + HEAD)
    placed = (
        P(BLK, None),
        P(None, None, HEAD),
        P(None, HEAD),
        P(HEAD, None),
        P(),
        P(None, None, BLK),
        P(BLK, None),
        P(BLK, None, HEAD),
        P(BLK, None, HEAD),
        P(),
        P(),
        P(),
        P(),
        P(),
    )
    return jax.shard_map(
        on_device, mesh=fine, in_specs=placed, out_specs=P(BLK + HEAD, None), check_vma=False
    )
```
